32 devices in a mesh: dp: 8 (over z, y), head: 4 (over x, core).
Axes of the slice: x: 2, y: 2, z: 4, core: 2. Of those that a mesh axis runs over, the one named last changes fastest.
Arguments:
- inputs: bfloat16 [8192, 2048], P('dp', 'head'), may hold values from -6 to 6
- cotangent: bfloat16 [8192, 2048], P('dp', 'head'), may hold values from -6 to 6
- token_valid: int32 [8192], P('dp'), may hold values from 0 to 1, as said below
- block_opens: int32 [32], P('dp'), may hold values from 0 to 1, as said below
- block_widths: int32 [32], P('dp'), may hold values from 16 to 64, as said below
- weight_inner: float32 [2048, 2, 4096], P('dp', None, 'head'), may hold values from -0.125 to 0.125
- weight_step: float32 [2048, 64], P('dp', 'head'), may hold values from -0.125 to 0.125
- weight_output: float32 [4096, 2048], P('head', 'dp'), may hold values from -0.09375 to 0.09375
- weight_state: float32 [2048, 256], P(('dp', 'head')), may hold values from -0.125 to 0.125
- norm_gain: float32 [2048], P(('dp', 'head')), may hold values from 0.5 to 1.5
- channel_table: float32 [6, 4096], P(None, 'head'), may hold values from -1.5 to 1.5, as said below
- head_table: float32 [3, 64], P(None, 'head'), may hold values from -9 to 1.5
- state_filter: float32 [256, 5], P(('dp', 'head')), may hold values from -2.5 to 2.5
- momentum_inner: float32 [2048, 2, 4096], P('dp', None, 'head'), may hold values from -112 to 112
- momentum_step: float32 [2048, 64], P('dp', 'head'), may hold values from -160 to 160
- momentum_output: float32 [4096, 2048], P('head', 'dp'), may hold values from -256 to 256
- momentum_state: float32 [2048, 256], P(('dp', 'head')), may hold values from -56 to 56
- momentum_gain: float32 [2048], P(('dp', 'head')), may hold values from -512 to 512
- momentum_channel: float32 [6, 4096], P(None, 'head'), may hold values from -256 to 256
- momentum_head: float32 [3, 64], P(None, 'head'), may hold values from -1024 to 1024
- momentum_filter: float32 [256, 5], P(('dp', 'head')), may hold values from -256 to 256
- average_inner: float32 [2048, 2, 4096], P('dp', None, 'head'), may hold values from -0.125 to 0.125
- average_step: float32 [2048, 64], P('dp', 'head'), may hold values from -0.125 to 0.125
- average_output: float32 [4096, 2048], P('head', 'dp'), may hold values from -0.09375 to 0.09375
- average_state: float32 [2048, 256], P(('dp', 'head')), may hold values from -0.125 to 0.125
- average_gain: float32 [2048], P(('dp', 'head')), may hold values from 0.5 to 1.5
- average_channel: float32 [6, 4096], P(None, 'head'), may hold values from -3 to 3
- average_head: float32 [3, 64], P(None, 'head'), may hold values from -6 to 6
- average_filter: float32 [256, 5], P(('dp', 'head')), may hold values from -3 to 3
Outputs:
- layer_output: bfloat16 [8192, 2048], P('dp', 'head')
- grad_input: float32 [8192, 2048], P('dp', 'head')
- updated_inner: float32 [2048, 2, 4096], P('dp', None, 'head')
- carried_inner: float32 [2048, 2, 4096], P('dp', None, 'head')
- smoothed_inner: float32 [2048, 2, 4096], P('dp', None, 'head')
- updated_step: float32 [2048, 64], P('dp', 'head')
- carried_step: float32 [2048, 64], P('dp', 'head')
- smoothed_step: float32 [2048, 64], P('dp', 'head')
- updated_output: float32 [4096, 2048], P('head', 'dp')
- carried_output: float32 [4096, 2048], P('head', 'dp')
- smoothed_output: float32 [4096, 2048], P('head', 'dp')
- updated_state: float32 [2048, 256], P(('dp', 'head'))
- carried_state: float32 [2048, 256], P(('dp', 'head'))
- smoothed_state: float32 [2048, 256], P(('dp', 'head'))
- updated_gain: float32 [2048], P(('dp', 'head'))
- carried_gain: float32 [2048], P(('dp', 'head'))
- smoothed_gain: float32 [2048], P(('dp', 'head'))
- updated_channel: float32 [6, 4096], P(None, 'head')
- carried_channel: float32 [6, 4096], P(None, 'head')
- smoothed_channel: float32 [6, 4096], P(None, 'head')
- updated_head: float32 [3, 64], P(None, 'head')
- carried_head: float32 [3, 64], P(None, 'head')
- smoothed_head: float32 [3, 64], P(None, 'head')
- updated_filter: float32 [256, 5], P(('dp', 'head'))
- carried_filter: float32 [256, 5], P(('dp', 'head'))
- smoothed_filter: float32 [256, 5], P(('dp', 'head'))
The draws below stay inside these ranges and needn't reach their ends.
Inputs may be any that keep to these rules, and one draw needn't show every extreme that they name: `block_opens`: the first block of each index of dp's 1024 tokens begins a sequence; some index of dp holds one sequence of all its 1024 tokens. `block_widths`: the same for all blocks of a sequence, a multiple of 16. `token_valid`: 1 on a prefix of each sequence that covers all its blocks but the last, and 128 or more tokens of the last; 0 on the rest of that block. `channel_table`: rows 0 to 3 taps, row 4 biases, row 5 gains.
All inputs are finite; a program needn't handle non-finite values.
Results may differ from the reference program's by a relative error of at most 0.0095.
The reference program's roundings to bfloat16 on the way count: a program that leaves them out, or rounds other values in their place, can miss the bound.
Values may be sent and summed in bfloat16 or wider, within the bound.
No kernel may reach another device: no remote copies, remote signals or barrier semaphores. Data moves between devices by JAX's collectives and lax.ppermute only.
A program may use at most 192 MiB of HBM per device.

```python
import math
from functools import partial
import jax
import jax.numpy as jnp
from jax import lax

D = 2048
DI = 4096
H = 64
P_SIZE = 64
NS = 128
KC = 4
BLK = 256
TOK_DEV = 1024
TOKENS = 8192
NBLK = 32
N_DP = 8
N_HEAD = 4


def sequence_layout(key):
    base = jax.random.fold_in(key, 17)
    key_start, key_level, key_count = jax.random.split(base, 3)
    blocks_device = TOK_DEV // BLK
    positions = jnp.arange(NBLK)
    within = positions % blocks_device
    openings = jax.random.randint(key_start, (NBLK,), 0, 2)
    openings = jnp.where(within == 0, 1, openings)
    openings = jnp.where(positions < blocks_device, jnp.where(within == 0, 1, 0), openings)
    sequence_index = jnp.cumsum(openings) - 1
    levels = jax.random.randint(key_level, (NBLK,), 1, 5)
    levels = jnp.where(positions == 0, 4, levels)
    levels = jnp.where(positions == 1, 1, levels)
    widths = levels[sequence_index] * (H // 4)
    following = jnp.concatenate([openings[1:], jnp.ones((1,), jnp.int32)])
    counts = jax.random.randint(key_count, (NBLK,), BLK // 2, BLK + 1)
    counts = jnp.where(following == 1, counts, BLK)
    counts = jnp.where(positions < blocks_device, BLK, counts)
    live = (jnp.arange(BLK)[None, :] < counts[:, None]).astype(jnp.int32).reshape(NBLK * BLK)
    return (openings.astype(jnp.int32), widths.astype(jnp.int32), live)


def draw_block_opens(key, part):
    return sequence_layout(key)[0]


def draw_block_widths(key, part):
    return sequence_layout(key)[1]


def draw_token_valid(key, part):
    return sequence_layout(key)[2]


def draw_channel_table(key, part):
    key_taps, key_bias, key_gain = jax.random.split(jax.random.fold_in(key, 31), 3)
    taps = jnp.clip(0.5 * jax.random.normal(key_taps, (KC, DI), jnp.float32), -1.5, 1.5)
    biases = jnp.clip(0.3 * jax.random.normal(key_bias, (1, DI), jnp.float32), -1.2, 1.2)
    gains = 1.0 + 0.3 * jax.random.uniform(key_gain, (1, DI), jnp.float32, -1.0, 1.0)
    return jnp.concatenate([taps, biases, gains], axis=0)


def draw_head_table(key, part):
    key_bias, key_rate, key_skip = jax.random.split(jax.random.fold_in(key, 29), 3)
    biases = jax.random.uniform(key_bias, (H,), jnp.float32, -5.0, 1.5)
    log_rates = jax.random.uniform(key_rate, (H,), jnp.float32, -6.0, 1.5)
    skips = jax.random.uniform(key_skip, (H,), jnp.float32, 0.5, 1.5)
    return jnp.stack([biases, log_rates, skips], axis=0)


def steps_of(own_key, extent, cuts, least, high):
    def one(dim, parts):
        draws = jax.random.uniform(jax.random.fold_in(jax.random.fold_in(own_key, 6), dim), (parts,), jnp.float32, least / len(cuts), high / len(cuts))
        return jnp.repeat(jnp.exp(draws), extent[dim] // parts).reshape((-1,) + (1,) * (len(extent) - dim - 1))

    factor_of = one(*cuts[0])
    for cut in cuts[1:]:
        factor_of = factor_of * one(*cut)
    return factor_of


def gaussian(stream_key, dims, width, most, shards=(), kind=jnp.bfloat16):
    values = width * jax.random.normal(stream_key, dims, jnp.float32)
    if shards:
        values = values * steps_of(stream_key, dims, shards, -0.22, 0.18)
    return jnp.clip(values, -most, most).astype(kind)


def setup_inputs(seed: int = 0) -> dict:
    splits = jax.random.split(jax.random.key(seed), 30)
    inputs = gaussian(splits[0], (TOKENS, D), 1.0, 6.0, ((0, 8), (1, 4)))
    cotangent = gaussian(splits[1], (TOKENS, D), 1.0, 6.0, ((0, 8), (1, 4)))
    token_valid = draw_token_valid(jax.random.fold_in(splits[29], 71), 0)
    block_opens = draw_block_opens(jax.random.fold_in(splits[29], 71), 0)
    block_widths = draw_block_widths(jax.random.fold_in(splits[29], 71), 0)
    weight_inner = gaussian(splits[5], (D, 2, DI), D ** -0.5, 0.125, ((0, 8), (2, 4)), jnp.float32)
    weight_step = gaussian(splits[6], (D, H), D ** -0.5, 0.125, ((0, 8), (1, 4)), jnp.float32)
    weight_output = gaussian(splits[7], (DI, D), DI ** -0.5, 0.09375, ((0, 4), (1, 8)), jnp.float32)
    weight_state = gaussian(splits[8], (D, 2 * NS), D ** -0.5, 0.125, ((0, 32),), jnp.float32)
    norm_gain = jnp.clip(1.0 + 0.1 * jax.random.normal(splits[9], (D,), jnp.float32), 0.5, 1.5)
    channel_table = draw_channel_table(jax.random.fold_in(splits[29], 71), 0)
    head_table = draw_head_table(jax.random.fold_in(splits[29], 71), 0)
    state_filter = gaussian(splits[12], (2 * NS, KC + 1), 0.5, 2.5, ((0, 32),), jnp.float32)
    momentum_inner = gaussian(splits[13], (D, 2, DI), (0.2 * TOKENS ** 0.5), 112.0, ((0, 8), (2, 4)), jnp.float32)
    momentum_step = gaussian(splits[14], (D, H), (0.3 * TOKENS ** 0.5), 160.0, ((0, 8), (1, 4)), jnp.float32)
    momentum_output = gaussian(splits[15], (DI, D), (0.5 * TOKENS ** 0.5), 256.0, ((0, 4), (1, 8)), jnp.float32)
    momentum_state = gaussian(splits[16], (D, 2 * NS), (0.1 * TOKENS ** 0.5), 56.0, ((0, 32),), jnp.float32)
    momentum_gain = gaussian(splits[17], (D,), (1.0 * TOKENS ** 0.5), 512.0, ((0, 32),), jnp.float32)
    momentum_channel = gaussian(splits[18], (KC + 2, DI), (0.5 * TOKENS ** 0.5), 256.0, ((1, 4),), jnp.float32)
    momentum_head = gaussian(splits[19], (3, H), (2.0 * TOKENS ** 0.5), 1024.0, ((1, 4),), jnp.float32)
    momentum_filter = gaussian(splits[20], (2 * NS, KC + 1), (0.5 * TOKENS ** 0.5), 256.0, ((0, 32),), jnp.float32)
    average_inner = gaussian(splits[21], (D, 2, DI), D ** -0.5, 0.125, ((0, 8), (2, 4)), jnp.float32)
    average_step = gaussian(splits[22], (D, H), D ** -0.5, 0.125, ((0, 8), (1, 4)), jnp.float32)
    average_output = gaussian(splits[23], (DI, D), DI ** -0.5, 0.09375, ((0, 4), (1, 8)), jnp.float32)
    average_state = gaussian(splits[24], (D, 2 * NS), D ** -0.5, 0.125, ((0, 32),), jnp.float32)
    average_gain = jnp.clip(1.0 + 0.1 * jax.random.normal(splits[25], (D,), jnp.float32), 0.5, 1.5)
    average_channel = gaussian(splits[26], (KC + 2, DI), 0.5, 3.0, ((1, 4),), jnp.float32)
    average_head = gaussian(splits[27], (3, H), 1.0, 6.0, ((1, 4),), jnp.float32)
    average_filter = gaussian(splits[28], (2 * NS, KC + 1), 0.5, 3.0, ((0, 32),), jnp.float32)
    return {"inputs": inputs, "cotangent": cotangent, "token_valid": token_valid, "block_opens": block_opens, "block_widths": block_widths, "weight_inner": weight_inner, "weight_step": weight_step, "weight_output": weight_output, "weight_state": weight_state, "norm_gain": norm_gain, "channel_table": channel_table, "head_table": head_table, "state_filter": state_filter, "momentum_inner": momentum_inner, "momentum_step": momentum_step, "momentum_output": momentum_output, "momentum_state": momentum_state, "momentum_gain": momentum_gain, "momentum_channel": momentum_channel, "momentum_head": momentum_head, "momentum_filter": momentum_filter, "average_inner": average_inner, "average_step": average_step, "average_output": average_output, "average_state": average_state, "average_gain": average_gain, "average_channel": average_channel, "average_head": average_head, "average_filter": average_filter}


EPS = 1e-05
MOMENTUM = 0.9
DECAY = 0.0001
AVERAGE = 0.75
RATE_MATRIX = 0.02
RATE_VECTOR = 0.1
HIGHEST = lax.Precision.HIGHEST

@jax.custom_vjp
def low(v):
    return lax.optimization_barrier(v.astype(jnp.bfloat16)).astype(jnp.float32)

@jax.custom_vjp
def low_back(v):
    return v

def low_keep(v):
    return (low(v), None)

def low_pass(kept, grad):
    return (grad,)

def back_keep(v):
    return (v, None)

def back_low(kept, grad):
    return (low(grad),)
low.defvjp(low_keep, low_pass)
low_back.defvjp(back_keep, back_low)

def block_pass(weights, carried, items):
    inner_w, step_w, output_w, state_w, gain_w, channel_w, head_w, filter_w = weights
    state_prev, tail_prev = carried
    block_rows, opening, block_width, valid_rows = items
    kept_share = 1.0 - opening
    inverse = lax.rsqrt(lax.optimization_barrier(jnp.mean(block_rows * block_rows, axis=1)) + EPS)
    normed = low(block_rows * inverse[:, None] * gain_w[None, :])
    gate_values = low_back(jnp.dot(normed, inner_w[:, 0, :], precision=HIGHEST))
    inner_x = low_back(jnp.dot(normed, inner_w[:, 1, :], precision=HIGHEST))
    state_bc = low_back(jnp.dot(normed, state_w, precision=HIGHEST))
    step_raw = low_back(jnp.dot(normed, step_w, precision=HIGHEST))
    joined = jnp.concatenate([inner_x, state_bc], axis=1)
    filters = jnp.concatenate([channel_w[:KC + 1], filter_w.T], axis=1)
    extended = jnp.concatenate([tail_prev * kept_share, joined], axis=0)
    conv_total = filters[KC][None, :]
    for position in range(KC):
        conv_total = conv_total + filters[position][None, :] * extended[position:position + BLK]
    active = jax.nn.silu(conv_total)
    signal_x = low(active[:, :DI]).reshape(BLK, H, P_SIZE)
    signal_b = low(active[:, DI:DI + NS])
    signal_c = low(active[:, DI + NS:])
    step_rates = jax.nn.softplus(step_raw + head_w[0][None, :])
    log_rates = step_rates * (-jnp.exp(head_w[1]))[None, :]
    cumulated = jnp.cumsum(log_rates, axis=0)
    lower_mask = (jnp.arange(BLK)[:, None] >= jnp.arange(BLK)[None, :])[:, :, None]
    spread = cumulated[:, None, :] - cumulated[None, :, :]
    decays = jnp.where(lower_mask, jnp.exp(jnp.where(lower_mask, spread, 0.0)), 0.0)
    intersection = jnp.dot(signal_c, signal_b.T, precision=HIGHEST)
    mixing = intersection[:, :, None] * decays * step_rates[None, :, :]
    inner_part = jnp.einsum('tuh,uhp->thp', mixing, signal_x, precision=HIGHEST)
    entering = state_prev * kept_share
    outer_part = jnp.exp(cumulated)[:, :, None] * jnp.einsum('hps,ts->thp', entering, signal_c, precision=HIGHEST)
    local_rank = jnp.arange(H) % (H // N_HEAD)
    head_used = (local_rank * H < block_width * (H // N_HEAD)).astype(jnp.float32)
    mixed = (inner_part + outer_part + head_w[2][None, :, None] * signal_x) * head_used[None, :, None]
    ending = jnp.exp(cumulated[-1][None, :] - cumulated) * step_rates
    state_next = jnp.exp(cumulated[-1])[:, None, None] * entering + jnp.einsum('uh,uhp,us->hps', ending, signal_x, signal_b, precision=HIGHEST)
    gated = mixed.reshape(BLK, DI) * jax.nn.silu(gate_values)
    total_sq = lax.optimization_barrier(jnp.sum(gated * gated, axis=1))
    norm_scale = lax.rsqrt(total_sq / (block_width.astype(jnp.float32) * P_SIZE) + EPS)
    normalized = low(gated * norm_scale[:, None] * channel_w[KC + 1][None, :])
    branch = jnp.dot(normalized, output_w, precision=HIGHEST)
    return ((state_next, joined[BLK - KC + 1:]), block_rows + valid_rows[:, None] * branch)

def advance(weight, gradient, moment, average, rate):
    adjusted = gradient + DECAY * weight
    moment_next = MOMENTUM * moment + adjusted
    weight_next = weight - rate * (adjusted + MOMENTUM * moment_next)
    average_next = AVERAGE * average + (1.0 - AVERAGE) * weight_next
    return (weight_next, moment_next, average_next)

def reference(inputs, cotangent, token_valid, block_opens, block_widths, weight_inner, weight_step, weight_output, weight_state, norm_gain, channel_table, head_table, state_filter, momentum_inner, momentum_step, momentum_output, momentum_state, momentum_gain, momentum_channel, momentum_head, momentum_filter, average_inner, average_step, average_output, average_state, average_gain, average_channel, average_head, average_filter):
    blocks_group = TOK_DEV // BLK

    def forward(input_rows, inner_w, step_w, output_w, state_w, gain_w, channel_w, head_w, filter_w):
        weights = (low(inner_w), low(step_w), low(output_w), low(state_w), low(gain_w), low(channel_w), low(head_w), low(filter_w))
        grouped = (input_rows.reshape(N_DP, blocks_group, BLK, D), block_opens.astype(jnp.float32).reshape(N_DP, blocks_group), block_widths.reshape(N_DP, blocks_group), token_valid.astype(jnp.float32).reshape(N_DP, blocks_group, BLK))
        stepper = jax.checkpoint(partial(block_pass, weights))

        def group_pass(items):
            initial = (jnp.zeros((H, P_SIZE, NS), jnp.float32), jnp.zeros((KC - 1, DI + 2 * NS), jnp.float32))
            finals, outputs = lax.scan(stepper, initial, items)
            return outputs
        outputs = lax.map(group_pass, grouped)
        return outputs.reshape(TOKENS, D)
    primals = (inputs.astype(jnp.float32), weight_inner, weight_step, weight_output, weight_state, norm_gain, channel_table, head_table, state_filter)
    result, backward = jax.vjp(forward, *primals)
    grads = backward(cotangent.astype(jnp.float32))
    matrix_rate = RATE_MATRIX / math.sqrt(TOKENS)
    vector_rate = RATE_VECTOR / math.sqrt(TOKENS)
    new_inner = advance(weight_inner, grads[1], momentum_inner, average_inner, matrix_rate)
    new_step = advance(weight_step, grads[2], momentum_step, average_step, matrix_rate)
    new_output = advance(weight_output, grads[3], momentum_output, average_output, matrix_rate)
    new_state = advance(weight_state, grads[4], momentum_state, average_state, matrix_rate)
    new_gain = advance(norm_gain, grads[5], momentum_gain, average_gain, vector_rate)
    new_channel = advance(channel_table, grads[6], momentum_channel, average_channel, vector_rate)
    new_head = advance(head_table, grads[7], momentum_head, average_head, vector_rate)
    new_filter = advance(state_filter, grads[8], momentum_filter, average_filter, vector_rate)
    return (result.astype(jnp.bfloat16), grads[0], new_inner[0], new_inner[1], new_inner[2], new_step[0], new_step[1], new_step[2], new_output[0], new_output[1], new_output[2], new_state[0], new_state[1], new_state[2], new_gain[0], new_gain[1], new_gain[2], new_channel[0], new_channel[1], new_channel[2], new_head[0], new_head[1], new_head[2], new_filter[0], new_filter[1], new_filter[2])
```

```python
import math

import jax
import jax.numpy as jnp
from jax import lax
from jax.sharding import PartitionSpec as P

D = 2048
H = 64
P_SIZE = 64
NS = 128
KC = 4
BLK = 256


EPS = 1e-05
MOMENTUM = 0.9
DECAY = 0.0001
AVERAGE = 0.75
RATE_MATRIX = 0.02
RATE_VECTOR = 0.1
HIGHEST = lax.Precision.HIGHEST


def rounded(value):
    return lax.optimization_barrier(value.astype(jnp.bfloat16)).astype(jnp.float32)


def convolve(inner_x, state_bc, taps_x, taps_bc, openings):
    joined = jnp.concatenate([inner_x, state_bc], axis=1)
    filters = jnp.concatenate([taps_x, taps_bc], axis=1)
    within = jnp.arange(joined.shape[0]) % BLK
    conv_total = filters[KC][None, :] + filters[KC - 1][None, :] * joined
    for offset in range(1, KC):
        shifted = jnp.concatenate(
            [jnp.zeros((offset, joined.shape[1]), jnp.float32), joined[:-offset]], axis=0
        )
        allowed = 1.0 - openings * (within < offset).astype(jnp.float32)
        conv_total = conv_total + filters[KC - 1 - offset][None, :] * shifted * allowed[:, None]
    active = jax.nn.silu(conv_total)
    split_at = inner_x.shape[1]
    return (active[:, :split_at], active[:, split_at:])


def state_mixer(signal_x, signal_bc, step_raw, gate_values, table, head_used, block_open):
    token_count, channels = signal_x.shape
    heads_here = table.shape[1]
    blocks_here = token_count // BLK
    step_rates = jax.nn.softplus(step_raw + table[0][None, :])
    log_rates = step_rates * (-jnp.exp(table[1]))[None, :]
    cumulated = jnp.cumsum(log_rates.reshape(blocks_here, BLK, heads_here), axis=1)
    rates_block = step_rates.reshape(blocks_here, BLK, heads_here)
    values = signal_x.reshape(blocks_here, BLK, heads_here, P_SIZE)
    inputs_map = signal_bc[:, :NS].reshape(blocks_here, BLK, NS)
    outputs_map = signal_bc[:, NS:].reshape(blocks_here, BLK, NS)
    lower_mask = (jnp.arange(BLK)[:, None] >= jnp.arange(BLK)[None, :])[None, :, :, None]
    spread = cumulated[:, :, None, :] - cumulated[:, None, :, :]
    decays = jnp.where(lower_mask, jnp.exp(jnp.where(lower_mask, spread, 0.0)), 0.0)
    intersection = jnp.einsum("nts,nus->ntu", outputs_map, inputs_map, precision=HIGHEST)
    mixing = intersection[..., None] * decays * rates_block[:, None, :, :]
    inner_part = jnp.einsum("ntuh,nuhp->nthp", mixing, values, precision=HIGHEST)
    ending = jnp.exp(cumulated[:, -1:, :] - cumulated) * rates_block
    pieces = jnp.einsum("nuh,nuhp,nus->nhps", ending, values, inputs_map, precision=HIGHEST)
    totals = jnp.exp(cumulated[:, -1, :])

    def carry_state(state_now, entries):
        piece_state, total_decay, opening = entries
        entering = state_now * (1.0 - opening)
        return (total_decay[:, None, None] * entering + piece_state, entering)

    initial = jnp.zeros((heads_here, P_SIZE, NS), jnp.float32)
    finals, entered = lax.scan(carry_state, initial, (pieces, totals, block_open))
    outer_part = jnp.exp(cumulated)[..., None] * jnp.einsum(
        "nhps,nts->nthp", entered, outputs_map, precision=HIGHEST
    )
    mixed = (inner_part + outer_part + table[2][None, None, :, None] * values) * head_used.reshape(
        blocks_here, BLK, heads_here
    )[..., None]
    gated = mixed.reshape(token_count, channels) * jax.nn.silu(gate_values)
    return (gated, jnp.sum(gated * gated, axis=1))


def gated_norm(gated, total_sq, gate_gain, norm_counts):
    norm_scale = lax.rsqrt(total_sq / norm_counts + EPS)
    return gated * norm_scale[:, None] * gate_gain[None, :]


def advance(weight, gradient, moment, average, rate):
    adjusted = gradient + DECAY * weight
    moment_next = MOMENTUM * moment + adjusted
    weight_next = weight - rate * (adjusted + MOMENTUM * moment_next)
    average_next = AVERAGE * average + (1.0 - AVERAGE) * weight_next
    return (weight_next, moment_next, average_next)


Y_SIZE = 2


def swap_pairs(size):
    return [(i, i ^ 1) for i in range(size)]


def gather_dp(shard, axis):
    count = lax.axis_size("dp")
    if count != 8:
        return lax.all_gather(shard, "dp", axis=axis, tiled=True)
    rows = count // Y_SIZE
    index = lax.axis_index("dp")
    row, column = index // Y_SIZE, index % Y_SIZE
    width = shard.shape[axis]
    held = {0: shard}
    for shift in range(1, rows):
        perm = [(i, (i + shift * Y_SIZE) % count) for i in range(count)]
        held[shift] = lax.ppermute(shard, "dp", perm)
    shape = list(shard.shape)
    shape[axis] = width * count
    full = jnp.zeros(shape, shard.dtype)
    for shift in range(rows):
        other = lax.ppermute(held[shift], "dp", swap_pairs(count))
        base = ((row - shift) % rows) * Y_SIZE
        full = lax.dynamic_update_slice_in_dim(full, held[shift], (base + column) * width, axis)
        full = lax.dynamic_update_slice_in_dim(full, other, (base + 1 - column) * width, axis)
    return full


def reduce_dp(value, axis):
    count = lax.axis_size("dp")
    low = jnp.bfloat16
    if count != 8:
        return lax.psum_scatter(
            value.astype(low), "dp", scatter_dimension=axis, tiled=True
        ).astype(jnp.float32)
    rows = count // Y_SIZE
    index = lax.axis_index("dp")
    row, column = index // Y_SIZE, index % Y_SIZE
    width = value.shape[axis] // count
    total = None
    for shift in (1, 2, 3, 0):
        base = ((row + shift) % rows) * Y_SIZE
        away = lax.dynamic_slice_in_dim(value, (base + 1 - column) * width, width, axis)
        kept = lax.dynamic_slice_in_dim(value, (base + column) * width, width, axis)
        came = lax.ppermute(away.astype(low), "dp", swap_pairs(count))
        pair = kept + came.astype(jnp.float32)
        if shift:
            perm = [(i, (i + shift * Y_SIZE) % count) for i in range(count)]
            pair = lax.ppermute(pair.astype(low), "dp", perm).astype(jnp.float32)
        total = pair if total is None else total + pair
    return total


def reduce_head(value):
    count = lax.axis_size("head")
    low = jnp.bfloat16
    if count != 4:
        return lax.psum_scatter(value, "head", scatter_dimension=0, tiled=False)
    index = lax.axis_index("head")
    side, core = index // 2, index % 2
    both = value.reshape(2, 2, *value.shape[1:])
    away = lax.dynamic_index_in_dim(both, 1 - core, 1, keepdims=False)
    kept = lax.dynamic_index_in_dim(both, core, 1, keepdims=False)
    came = lax.ppermute(away.astype(low), "head", swap_pairs(count))
    pair = kept + came.astype(jnp.float32)
    away = lax.dynamic_index_in_dim(pair, 1 - side, 0, keepdims=False)
    kept = lax.dynamic_index_in_dim(pair, side, 0, keepdims=False)
    came = lax.ppermute(away.astype(low), "head", [(i, (i + 2) % 4) for i in range(count)])
    return kept + came.astype(jnp.float32)


def gather_head(piece, axis):
    count = lax.axis_size("head")
    if count != 4:
        return lax.all_gather(piece, "head", axis=axis, tiled=True)
    index = lax.axis_index("head")
    width = piece.shape[axis]
    near = lax.ppermute(piece, "head", swap_pairs(count))
    first = index % 2 == 0
    pair = jnp.concatenate(
        [jnp.where(first, piece, near), jnp.where(first, near, piece)], axis=axis
    )
    far = lax.ppermute(pair, "head", [(i, (i + 2) % 4) for i in range(count)])
    lower = index < 2
    return jnp.concatenate(
        [jnp.where(lower, pair, far), jnp.where(lower, far, pair)], axis=axis
    )


def body(
    inputs,
    cotangent,
    token_valid,
    block_opens,
    block_widths,
    weight_inner,
    weight_step,
    weight_output,
    weight_state,
    norm_gain,
    channel_table,
    head_table,
    state_filter,
    momentum_inner,
    momentum_step,
    momentum_output,
    momentum_state,
    momentum_gain,
    momentum_channel,
    momentum_head,
    momentum_filter,
    average_inner,
    average_step,
    average_output,
    average_state,
    average_gain,
    average_channel,
    average_head,
    average_filter,
):
    low = jnp.bfloat16
    count_dp = lax.axis_size("dp")
    heads_own = weight_step.shape[1]
    rows_all, state_rows = weight_state.shape[0], state_filter.shape[0]
    filter_block = jnp.pad(state_filter.astype(low), ((0, rows_all - state_rows), (0, 0)))
    shared_piece = jnp.concatenate(
        [weight_state.astype(low), norm_gain.astype(low)[:, None], filter_block], axis=1
    )
    shared_rows = gather_head(shared_piece, 0)
    small_rows = jnp.concatenate([shared_rows, weight_step.astype(low)], axis=1)
    small_rows = jnp.pad(small_rows, ((0, 0), (0, -small_rows.shape[1] % 128)))
    inner_value = gather_dp(weight_inner[:, 1].astype(low), 0)
    small_full = gather_dp(small_rows, 0)
    inner_gate = gather_dp(weight_inner[:, 0].astype(low), 0)
    output_full = gather_dp(weight_output.astype(low), 1)
    width_state = weight_state.shape[1]
    state_full = small_full[:, :width_state]
    gain_full = small_full[:, width_state]
    filter_full = small_full[:, width_state + 1 : width_state + 1 + KC + 1]
    filter_full = filter_full.reshape(-1, rows_all, KC + 1)[:, :state_rows].reshape(-1, KC + 1)
    step_full = small_full[:, width_state + KC + 2 : width_state + KC + 2 + heads_own]
    channel_used = rounded(channel_table)
    head_values = rounded(head_table)
    gathered = lax.all_gather(inputs, "head", axis=1, tiled=True)
    tokens_full = gathered.astype(jnp.float32)
    inverse = lax.rsqrt(jnp.mean(tokens_full * tokens_full, axis=1) + EPS)
    gain_float = gain_full.astype(jnp.float32)
    normed = (tokens_full * inverse[:, None] * gain_float[None, :]).astype(jnp.bfloat16)
    gate_values = jnp.dot(normed, inner_gate, preferred_element_type=jnp.float32)
    inner_x = jnp.dot(normed, inner_value, preferred_element_type=jnp.float32)
    state_bc = jnp.dot(normed, state_full, preferred_element_type=jnp.float32)
    step_raw = jnp.dot(normed, step_full, preferred_element_type=jnp.float32)
    block_open = block_opens.astype(jnp.float32)
    openings = jnp.repeat(block_open, BLK)
    widths = jnp.repeat(block_widths, BLK)
    heads_local = step_full.shape[1]
    head_used = (jnp.arange(heads_local)[None, :] * H < widths[:, None] * heads_local).astype(
        jnp.float32
    )
    norm_counts = widths.astype(jnp.float32) * P_SIZE
    valid_rows = token_valid.astype(jnp.float32)
    taps_x = channel_used[: KC + 1]
    gate_gain = channel_used[KC + 1]
    taps_bc = filter_full.astype(jnp.float32).T

    def conv_part(inner_value, state_value, taps_first, taps_second):
        return convolve(inner_value, state_value, taps_first, taps_second, openings)

    (conv_x, conv_bc), conv_back = jax.vjp(conv_part, inner_x, state_bc, taps_x, taps_bc)
    signal_x = rounded(conv_x)
    signal_bc = rounded(conv_bc)

    def mix_part(signal_first, signal_second, raw_steps, gate_part, table):
        return state_mixer(
            signal_first, signal_second, raw_steps, gate_part, table, head_used, block_open
        )

    (gated, local_sq), mix_back = jax.vjp(
        mix_part, signal_x, signal_bc, step_raw, gate_values, head_values
    )
    total_sq = lax.psum(local_sq, "head")

    def norm_part(gated_value, sum_value, gain_value):
        return gated_norm(gated_value, sum_value, gain_value, norm_counts)

    normalized, norm_back_fn = jax.vjp(norm_part, gated, total_sq, gate_gain)
    projected = normalized.astype(jnp.bfloat16)
    partial_out = jnp.dot(projected, output_full, preferred_element_type=jnp.float32)
    branch = lax.psum_scatter(
        partial_out.astype(jnp.bfloat16), "head", scatter_dimension=1, tiled=True
    ).astype(jnp.float32)
    own_inputs = inputs.astype(jnp.float32)
    layer_output = (own_inputs + valid_rows[:, None] * branch).astype(jnp.bfloat16)
    masked = cotangent * token_valid.astype(jnp.bfloat16)[:, None]
    shard_piece = lax.all_gather(masked, "head", axis=1, tiled=True)
    grad_normal = jnp.einsum(
        "tw,cw->tc", shard_piece, output_full, preferred_element_type=jnp.float32
    )
    block_grad = jnp.einsum("tc,tw->cw", projected, shard_piece, preferred_element_type=jnp.float32)
    grad_gated, grad_sq_part, grad_gate_gain = norm_back_fn(grad_normal)
    grad_sq = lax.psum(grad_sq_part, "head")
    grad_sx, grad_sbc, grad_raw, grad_gate, grad_head = mix_back((grad_gated, grad_sq))
    grad_inner_x, grad_state_bc, grad_taps_x, grad_taps_bc = conv_back((grad_sx, grad_sbc))
    gate_low = grad_gate.astype(jnp.bfloat16)
    inner_low = grad_inner_x.astype(jnp.bfloat16)
    state_low = grad_state_bc.astype(jnp.bfloat16)
    step_low = grad_raw.astype(jnp.bfloat16)
    grad_gate_w = jnp.einsum("td,tc->dc", normed, gate_low, preferred_element_type=jnp.float32)
    grad_inner_w = jnp.einsum("td,tc->dc", normed, inner_low, preferred_element_type=jnp.float32)
    grad_state = jnp.einsum("td,ts->ds", normed, state_low, preferred_element_type=jnp.float32)
    grad_step = jnp.einsum("td,th->dh", normed, step_low, preferred_element_type=jnp.float32)
    grad_normed = jnp.einsum("tc,dc->td", gate_low, inner_gate, preferred_element_type=jnp.float32)
    grad_normed = grad_normed + jnp.einsum(
        "tc,dc->td", inner_low, inner_value, preferred_element_type=jnp.float32
    )
    grad_normed = grad_normed + jnp.einsum(
        "ts,ds->td", state_low, state_full, preferred_element_type=jnp.float32
    )
    grad_normed = grad_normed + jnp.einsum(
        "th,dh->td", step_low, step_full, preferred_element_type=jnp.float32
    )
    own_grad = lax.psum_scatter(
        grad_normed.astype(jnp.bfloat16), "head", scatter_dimension=1, tiled=True
    ).astype(jnp.float32)
    own_width = inputs.shape[1]
    start_column = lax.axis_index("head") * own_width
    own_gain = lax.dynamic_slice_in_dim(gain_float, start_column, own_width)
    scaled = own_grad * own_gain[None, :]
    row_part = jnp.sum(scaled * own_inputs, axis=1)
    grad_gain_own = jnp.sum(own_grad * own_inputs * inverse[:, None], axis=0)
    row_total = lax.psum(row_part, "head")
    inverse_cube = inverse * inverse * inverse
    grad_input = (
        cotangent.astype(jnp.float32)
        + inverse[:, None] * scaled
        - own_inputs * (inverse_cube * row_total / D)[:, None]
    )
    grad_gain_full = lax.dynamic_update_slice_in_dim(
        jnp.zeros((D,), jnp.float32), grad_gain_own, start_column, 0
    )
    grad_channel = jnp.concatenate([grad_taps_x, grad_gate_gain[None, :]], axis=0)
    grad_filter = grad_taps_bc.T
    output_reduced = reduce_dp(block_grad, 1)
    gate_reduced = reduce_dp(grad_gate_w, 0)
    inner_reduced = reduce_dp(grad_inner_w, 0)
    inner_reduced = jnp.stack([gate_reduced, inner_reduced], axis=1)
    count_head = lax.axis_size("head")
    filter_part = jnp.pad(
        grad_filter.reshape(count_dp, count_head, state_rows * (KC + 1)),
        ((0, 0), (0, 0), (0, rows_all - state_rows * (KC + 1))),
    ).reshape(D, 1)
    shared_part = jnp.concatenate(
        [grad_state, grad_gain_full[:, None], filter_part], axis=1
    ).reshape(count_dp, count_head, rows_all, width_state + 2)
    shared_own = reduce_head(jnp.swapaxes(shared_part, 0, 1))
    table_part = jnp.concatenate([grad_channel.reshape(-1), grad_head.reshape(-1)])
    table_width = -(-table_part.shape[0] // rows_all)
    table_part = jnp.pad(table_part, (0, table_width * rows_all - table_part.shape[0]))
    table_part = jnp.broadcast_to(
        table_part.reshape(1, rows_all, table_width), (count_dp, rows_all, table_width)
    )
    step_part = grad_step.reshape(count_dp, rows_all, -1)
    small_part = jnp.concatenate([shared_own, step_part, table_part], axis=2)
    small_own = reduce_dp(small_part.reshape(count_dp * rows_all, -1), 0)
    state_reduced = small_own[:, :width_state]
    gain_reduced = small_own[:, width_state]
    filter_reduced = small_own[: state_rows * (KC + 1), width_state + 1].reshape(state_rows, KC + 1)
    at = width_state + 2
    step_reduced = small_own[:, at : at + step_part.shape[2]].reshape(-1, heads_own)
    table_own = small_own[:, at + step_part.shape[2] :].reshape(-1)
    channel_size = grad_channel.shape[0] * grad_channel.shape[1]
    channel_reduced = table_own[:channel_size].reshape(grad_channel.shape)
    head_reduced = table_own[channel_size : channel_size + grad_head.size].reshape(grad_head.shape)
    total_tokens = inputs.shape[0] * lax.axis_size("dp")
    matrix_rate = RATE_MATRIX / math.sqrt(total_tokens)
    vector_rate = RATE_VECTOR / math.sqrt(total_tokens)
    new_inner = advance(weight_inner, inner_reduced, momentum_inner, average_inner, matrix_rate)
    new_step = advance(weight_step, step_reduced, momentum_step, average_step, matrix_rate)
    new_output = advance(
        weight_output, output_reduced, momentum_output, average_output, matrix_rate
    )
    new_state = advance(weight_state, state_reduced, momentum_state, average_state, matrix_rate)
    new_gain = advance(norm_gain, gain_reduced, momentum_gain, average_gain, vector_rate)
    new_channel = advance(
        channel_table, channel_reduced, momentum_channel, average_channel, vector_rate
    )
    new_head = advance(head_table, head_reduced, momentum_head, average_head, vector_rate)
    new_filter = advance(state_filter, filter_reduced, momentum_filter, average_filter, vector_rate)
    return (
        layer_output,
        grad_input,
        new_inner[0],
        new_inner[1],
        new_inner[2],
        new_step[0],
        new_step[1],
        new_step[2],
        new_output[0],
        new_output[1],
        new_output[2],
        new_state[0],
        new_state[1],
        new_state[2],
        new_gain[0],
        new_gain[1],
        new_gain[2],
        new_channel[0],
        new_channel[1],
        new_channel[2],
        new_head[0],
        new_head[1],
        new_head[2],
        new_filter[0],
        new_filter[1],
        new_filter[2],
    )


def solution(mesh):
    in_specs = (
        P("dp", "head"),
        P("dp", "head"),
        P("dp"),
        P("dp"),
        P("dp"),
        P("dp", None, "head"),
        P("dp", "head"),
        P("head", "dp"),
        P(("dp", "head"), None),
        P(("dp", "head")),
        P(None, "head"),
        P(None, "head"),
        P(("dp", "head"), None),
        P("dp", None, "head"),
        P("dp", "head"),
        P("head", "dp"),
        P(("dp", "head"), None),
        P(("dp", "head")),
        P(None, "head"),
        P(None, "head"),
        P(("dp", "head"), None),
        P("dp", None, "head"),
        P("dp", "head"),
        P("head", "dp"),
        P(("dp", "head"), None),
        P(("dp", "head")),
        P(None, "head"),
        P(None, "head"),
        P(("dp", "head"), None),
    )
    out_specs = (
        P("dp", "head"),
        P("dp", "head"),
        P("dp", None, "head"),
        P("dp", None, "head"),
        P("dp", None, "head"),
        P("dp", "head"),
        P("dp", "head"),
        P("dp", "head"),
        P("head", "dp"),
        P("head", "dp"),
        P("head", "dp"),
        P(("dp", "head"), None),
        P(("dp", "head"), None),
        P(("dp", "head"), None),
        P(("dp", "head")),
        P(("dp", "head")),
        P(("dp", "head")),
        P(None, "head"),
        P(None, "head"),
        P(None, "head"),
        P(None, "head"),
        P(None, "head"),
        P(None, "head"),
        P(("dp", "head"), None),
        P(("dp", "head"), None),
        P(("dp", "head"), None),
    )
    return jax.shard_map(body, mesh=mesh, in_specs=in_specs, out_specs=out_specs, check_vma=False)
```

```python
import functools
import math

import jax
import jax.numpy as jnp
from jax import lax
from jax.experimental import pallas as pl
from jax.experimental.pallas import tpu as pltpu
from jax.sharding import PartitionSpec as P

D = 2048
H = 64
P_SIZE = 64
NS = 128
KC = 4
BLK = 256


EPS = 1e-05
MOMENTUM = 0.9
DECAY = 0.0001
AVERAGE = 0.75
RATE_MATRIX = 0.02
RATE_VECTOR = 0.1
HIGHEST = lax.Precision.HIGHEST


def rounded(value):
    return lax.optimization_barrier(value.astype(jnp.bfloat16)).astype(jnp.float32)


def advance(weight, gradient, moment, average, rate):
    adjusted = gradient + DECAY * weight
    moment_next = MOMENTUM * moment + adjusted
    weight_next = weight - rate * (adjusted + MOMENTUM * moment_next)
    average_next = AVERAGE * average + (1.0 - AVERAGE) * weight_next
    return (weight_next, moment_next, average_next)


LANES = 128
FAR = -1e30
NT = (((1,), (1,)), ((), ()))
TN = (((0,), (0,)), ((), ()))


def dot32(first, second, dims=(((1,), (0,)), ((), ()))):
    return lax.dot_general(first, second, dims, preferred_element_type=jnp.float32)


def softplus(value):
    return jnp.maximum(value, 0.0) + jnp.log1p(jnp.exp(-jnp.abs(value)))


def triangle(upper):
    first = lax.broadcasted_iota(jnp.int32, (BLK, BLK), 0)
    second = lax.broadcasted_iota(jnp.int32, (BLK, BLK), 1)
    return first <= second if upper else first >= second


def filtered(window, taps, lanes):
    total = taps[KC : KC + 1, lanes] + taps[0:1, lanes] * window[5 : 5 + BLK, lanes]
    for offset in range(1, KC):
        total = total + taps[offset : offset + 1, lanes] * window[5 + offset : 5 + offset + BLK, lanes]
    return total


def step_parts(raw, table, heads):
    lane = lax.broadcasted_iota(jnp.int32, (BLK, LANES), 1)
    shifted = raw + table[0:1, :]
    rates = jnp.where(lane < heads, softplus(shifted), 0.0)
    decay = -jnp.exp(table[1:2, :])
    cumulated = jnp.dot(
        triangle(False).astype(jnp.float32),
        rates * decay,
        precision=HIGHEST,
        preferred_element_type=jnp.float32,
    )
    return shifted, rates, decay, cumulated


def spread_columns(value, out, heads):
    for head in range(heads):
        out[head] = jnp.broadcast_to(value[:, head : head + 1], (BLK, LANES))


def mixer_kernel(
    heads, opens, widths, v_ref, s_ref, tx, ts, table, mixed, entered,
    window, window_s, state, xs, cum_wide, rate_wide, cum_rows, rate_rows,
):
    block = pl.program_id(0)
    low = jnp.bfloat16

    @pl.when(opens[block] == 1)
    def _():
        window[0:8, :] = jnp.zeros_like(window[0:8, :])
        window_s[0:8, :] = jnp.zeros_like(window_s[0:8, :])
        state[...] = jnp.zeros_like(state)

    @pl.when(opens[block] != 1)
    def _():
        window[0:8, :] = window[BLK : BLK + 8, :]
        window_s[0:8, :] = window_s[BLK : BLK + 8, :]

    window[8 : 8 + BLK, :] = v_ref[...]
    window_s[8 : 8 + BLK, :] = s_ref[:, : 2 * NS]
    shared = filtered(window_s, ts, slice(None))
    shared = (shared * jax.nn.sigmoid(shared)).astype(low)
    maps_in, maps_out = shared[:, :NS], shared[:, NS:]
    maps_in_t = jnp.transpose(maps_in.astype(jnp.float32)).astype(low)
    _, rates, _, cumulated = step_parts(s_ref[:, 2 * NS :], table, heads)
    cum_rows[...] = jnp.transpose(cumulated)[: cum_rows.shape[0]]
    rate_rows[...] = jnp.transpose(rates)[: rate_rows.shape[0]]
    spread_columns(cumulated, cum_wide, heads)
    spread_columns(rates, rate_wide, heads)
    crossing = dot32(maps_out, maps_in, NT)
    width = widths[block]

    def pair(index, _):
        lanes = pl.ds(pl.multiple_of(index * LANES, LANES), LANES)
        pre = filtered(window, tx, lanes)
        values = (pre * jax.nn.sigmoid(pre)).astype(low)
        side = lax.broadcasted_iota(jnp.int32, (BLK, LANES), 1) < P_SIZE
        lower = triangle(False)
        cum_pair = jnp.where(side, cum_wide[2 * index], cum_wide[2 * index + 1])
        rate_pair = jnp.where(side, rate_wide[2 * index], rate_wide[2 * index + 1])
        now = state[:, lanes]
        entered[0, :, lanes] = now
        total = jnp.exp(cum_pair) * dot32(maps_out, now.astype(low))
        for half in range(2):
            head = 2 * index + half
            column = cum_wide[head]
            spread = jnp.concatenate([column, column], axis=1) - cum_rows[pl.ds(head, 1), :]
            decays = jnp.exp(jnp.where(lower, spread, FAR))
            mixing = (crossing * decays * rate_rows[pl.ds(head, 1), :]).astype(low)
            own = side if half == 0 else jnp.logical_not(side)
            total = total + dot32(mixing, jnp.where(own, values, jnp.zeros_like(values)))
        wide = values.astype(jnp.float32)
        total = total + tx[6:7, lanes] * wide
        row = lax.broadcasted_iota(jnp.int32, (1, LANES), 1)
        head_row = 2 * index + (row >= P_SIZE).astype(jnp.int32)
        used = (head_row * H < width * heads).astype(jnp.float32)
        mixed[:, lanes] = total * used
        last = cum_pair[BLK - 1 : BLK, :]
        ending = jnp.exp(last - cum_pair) * rate_pair
        state[:, lanes] = jnp.exp(last) * now + dot32(maps_in_t, (wide * ending).astype(low))
        return 0

    lax.fori_loop(0, heads // 2, pair, 0)


def mixer_back_kernel(
    heads, count, opens, v_ref, v_tail, s_ref, s_tail, tx, ts, table, ybar, entered,
    inner_low, small_low, tx_grad, ts_grad, table_grad,
    window, window_s, ahead, ahead_s, state_grad, cum_wide, rate_wide,
    cum_rows, z_rows, cross_grad, maps_grad, column_sum, outer_sum, rate_sum, last_sum,
):
    low = jnp.bfloat16
    step = pl.program_id(0)
    block = count - 1 - step
    opened = opens[block] == 1

    @pl.when(step == 0)
    def _():
        ahead[BLK : BLK + 8, :] = jnp.zeros_like(ahead[BLK : BLK + 8, :])
        ahead_s[BLK : BLK + 8, :] = jnp.zeros_like(ahead_s[BLK : BLK + 8, :])
        state_grad[...] = jnp.zeros_like(state_grad)
        tx_grad[...] = jnp.zeros_like(tx_grad)
        ts_grad[...] = jnp.zeros_like(ts_grad)
        table_grad[...] = jnp.zeros_like(table_grad)
        z_rows[...] = jnp.zeros_like(z_rows)

    @pl.when(opened)
    def _():
        window[0:8, :] = jnp.zeros_like(window[0:8, :])
        window_s[0:8, :] = jnp.zeros_like(window_s[0:8, :])

    @pl.when(jnp.logical_not(opened))
    def _():
        window[0:8, :] = v_tail[...]
        window_s[0:8, :] = s_tail[:, : 2 * NS]

    window[8 : 8 + BLK, :] = v_ref[...]
    window_s[8 : 8 + BLK, :] = s_ref[:, : 2 * NS]
    pre_s = filtered(window_s, ts, slice(None))
    share_s = jax.nn.sigmoid(pre_s)
    shared = (pre_s * share_s).astype(low)
    slope_s = share_s * (1.0 + pre_s * (1.0 - share_s))
    maps_in, maps_out = shared[:, :NS], shared[:, NS:]
    maps_out_t = jnp.transpose(maps_out.astype(jnp.float32)).astype(low)
    shifted, rates, decay, cumulated = step_parts(s_ref[:, 2 * NS :], table, heads)
    cum_rows[...] = jnp.transpose(cumulated)[: cum_rows.shape[0]]
    spread_columns(cumulated, cum_wide, heads)
    spread_columns(rates, rate_wide, heads)
    crossing = dot32(maps_in, maps_out, NT)
    for held in (cross_grad, maps_grad, column_sum, outer_sum, rate_sum, last_sum):
        held[...] = jnp.zeros_like(held)

    def pair(index, _):
        lanes = pl.ds(pl.multiple_of(index * LANES, LANES), LANES)
        pre = filtered(window, tx, lanes)
        share = jax.nn.sigmoid(pre)
        values = (pre * share).astype(low)
        slope = share * (1.0 + pre * (1.0 - share))
        lane = lax.broadcasted_iota(jnp.int32, (BLK, LANES), 1)
        side = lane < P_SIZE
        upper = triangle(True)
        cum_pair = jnp.where(side, cum_wide[2 * index], cum_wide[2 * index + 1])
        rate_pair = jnp.where(side, rate_wide[2 * index], rate_wide[2 * index + 1])
        back = ybar[:, lanes]
        back_low = back.astype(low)
        wide = values.astype(jnp.float32)
        now = entered[0, :, lanes]
        now_low = now.astype(low)
        after = state_grad[:, lanes]
        after_low = after.astype(low)
        grown = jnp.exp(cum_pair)
        last = cum_pair[BLK - 1 : BLK, :]
        total_decay = jnp.exp(last)
        ending = jnp.exp(last - cum_pair) * rate_pair
        outer = dot32(maps_out, now_low)
        inward = dot32(maps_in, after_low)
        back_grown = back * grown
        back_grown_low = back_grown.astype(low)
        maps_grad[:, NS:] += dot32(back_grown_low, now_low, NT)
        maps_grad[:, :NS] += dot32((wide * ending).astype(low), after_low, NT)
        state_grad[:, lanes] = total_decay * after + dot32(maps_out_t, back_grown_low)
        grad = ending * inward + tx[6:7, lanes] * back
        pick = (
            lax.broadcasted_iota(jnp.int32, (LANES, LANES), 1)
            == 2 * index + (lax.broadcasted_iota(jnp.int32, (LANES, LANES), 0) >= P_SIZE).astype(jnp.int32)
        ).astype(low)

        def to_heads(value):
            high = value.astype(low)
            rest = (value - high.astype(jnp.float32)).astype(low)
            return dot32(high, pick) + dot32(rest, pick)

        outer_sum[...] += to_heads(back_grown * outer)
        rate_sum[...] += to_heads(wide * inward)
        kept = jnp.sum(total_decay * after * now, axis=0, keepdims=True)
        last_sum[...] += to_heads(jnp.broadcast_to(kept, (8, LANES)))
        tx_grad[6:7, lanes] += jnp.sum(back * wide, axis=0, keepdims=True)
        zero = jnp.zeros_like(values)
        for half in range(2):
            head = 2 * index + half
            own = side if half == 0 else jnp.logical_not(side)
            column = cum_wide[head]
            rate = rate_wide[head]
            spread = cum_rows[pl.ds(head, 1), :] - jnp.concatenate([column, column], axis=1)
            decays = jnp.exp(jnp.where(upper, spread, FAR))
            weighted = decays * jnp.concatenate([rate, rate], axis=1)
            products = dot32(jnp.where(own, values, zero), back_low, NT)
            summed = jnp.sum(products * (crossing * decays), axis=1, keepdims=True)
            column_sum[...] += jnp.where(lane == head, summed, 0.0)
            mixing = crossing * weighted
            z_rows[pl.ds(head, 1), :] = jnp.sum(products * mixing, axis=0, keepdims=True)
            cross_grad[...] += products * weighted
            grad = grad + dot32(mixing.astype(low), jnp.where(own, back_low, zero))
        back_pre = grad * slope
        ahead[0:BLK, lanes] = back_pre
        spent = tx[KC - 1 : KC, lanes] * back_pre
        for offset in range(1, KC):
            spent = spent + tx[KC - 1 - offset : KC - offset, lanes] * ahead[offset : offset + BLK, lanes]
        inner_low[:, lanes] = spent.astype(low)
        for position in range(KC):
            tx_grad[position : position + 1, lanes] += jnp.sum(
                back_pre * window[5 + position : 5 + position + BLK, lanes], axis=0, keepdims=True
            )
        tx_grad[KC : KC + 1, lanes] += jnp.sum(back_pre, axis=0, keepdims=True)
        return 0

    lax.fori_loop(0, heads // 2, pair, 0)
    cross = cross_grad[...]
    cross_low = cross.astype(low)
    maps_grad[:, :NS] += dot32(cross_low, maps_out)
    maps_grad[:, NS:] += dot32(jnp.transpose(cross).astype(low), maps_in)
    back_pre_s = maps_grad[...] * slope_s
    ahead_s[0:BLK, :] = back_pre_s
    spent_s = ts[KC - 1 : KC, :] * back_pre_s
    for offset in range(1, KC):
        spent_s = spent_s + ts[KC - 1 - offset : KC - offset, :] * ahead_s[offset : offset + BLK, :]
    small_low[:, : 2 * NS] = spent_s.astype(low)
    for position in range(KC):
        ts_grad[position : position + 1, :] += jnp.sum(
            back_pre_s * window_s[5 + position : 5 + position + BLK, :], axis=0, keepdims=True
        )
    ts_grad[KC : KC + 1, :] += jnp.sum(back_pre_s, axis=0, keepdims=True)
    lane = lax.broadcasted_iota(jnp.int32, (BLK, LANES), 1)
    falling = jnp.exp(cumulated[BLK - 1 : BLK, :] - cumulated)
    ended = rate_sum[...] * falling
    ended_rate = ended * rates
    own_sum = column_sum[...]
    cum_grad = jnp.transpose(z_rows[...]) + outer_sum[...] - rates * own_sum - ended_rate
    final = last_sum[0:1, :] + jnp.sum(ended_rate, axis=0, keepdims=True)
    place = lax.broadcasted_iota(jnp.int32, (BLK, LANES), 0)
    cum_grad = cum_grad + jnp.where(place == BLK - 1, final, 0.0)
    log_grad = jnp.dot(
        triangle(True).astype(jnp.float32),
        cum_grad,
        precision=HIGHEST,
        preferred_element_type=jnp.float32,
    )
    rate_grad = own_sum + ended + decay * log_grad
    raw_grad = jnp.where(lane < heads, rate_grad * jax.nn.sigmoid(shifted), 0.0)
    small_low[:, 2 * NS :] = raw_grad.astype(low)
    table_grad[0:1, :] += jnp.sum(raw_grad, axis=0, keepdims=True)
    table_grad[1:2, :] += decay * jnp.sum(rates * log_grad, axis=0, keepdims=True)

    @pl.when(opened)
    def _():
        ahead[BLK : BLK + 8, :] = jnp.zeros_like(ahead[BLK : BLK + 8, :])
        ahead_s[BLK : BLK + 8, :] = jnp.zeros_like(ahead_s[BLK : BLK + 8, :])
        state_grad[...] = jnp.zeros_like(state_grad)

    @pl.when(jnp.logical_not(opened))
    def _():
        ahead[BLK : BLK + 8, :] = ahead[0:8, :]
        ahead_s[BLK : BLK + 8, :] = ahead_s[0:8, :]


VMEM_LIMIT = 56 * 1024 * 1024


def mixer(opens, widths, inner, small, tx, ts, table, interpret=False):
    tokens, channels = inner.shape
    heads, count = channels // P_SIZE, tokens // BLK
    whole = lambda rows, columns: pl.BlockSpec((rows, columns), lambda i, *_: (0, 0))
    rows = lambda columns: pl.BlockSpec((BLK, columns), lambda i, *_: (i, 0))
    wide = pltpu.VMEM((heads, BLK, LANES), jnp.float32)
    row_pad = -(-heads // 8) * 8
    return pl.pallas_call(
        functools.partial(mixer_kernel, heads),
        out_shape=(
            jax.ShapeDtypeStruct((tokens, channels), jnp.float32),
            jax.ShapeDtypeStruct((count, NS, channels), jnp.float32),
        ),
        grid_spec=pltpu.PrefetchScalarGridSpec(
            num_scalar_prefetch=2,
            grid=(count,),
            in_specs=[rows(channels), rows(3 * LANES), whole(8, channels), whole(8, 2 * NS), whole(8, LANES)],
            out_specs=[rows(channels), pl.BlockSpec((1, NS, channels), lambda i, *_: (i, 0, 0))],
            scratch_shapes=[
                pltpu.VMEM((BLK + 8, channels), jnp.float32),
                pltpu.VMEM((BLK + 8, 2 * NS), jnp.float32),
                pltpu.VMEM((NS, channels), jnp.float32),
                pltpu.VMEM((8, LANES), jnp.bfloat16),
                wide,
                wide,
                pltpu.VMEM((row_pad, BLK), jnp.float32),
                pltpu.VMEM((row_pad, BLK), jnp.float32),
            ],
        ),
        compiler_params=pltpu.CompilerParams(vmem_limit_bytes=VMEM_LIMIT),
        name="mixer",
        interpret=interpret,
    )(opens, widths, inner, small, tx, ts, table)


def mixer_back(opens, inner, small, tx, ts, table, ybar, entered, interpret=False):
    tokens, channels = inner.shape
    heads, count = channels // P_SIZE, tokens // BLK
    per = BLK // 8
    turn = lambda i: count - 1 - i
    whole = lambda rows, columns: pl.BlockSpec((rows, columns), lambda i, *_: (0, 0))
    rows = lambda columns: pl.BlockSpec((BLK, columns), lambda i, *_: (turn(i), 0))
    tail = lambda columns: pl.BlockSpec(
        (8, columns), lambda i, *_: (jnp.maximum(turn(i) * per - 1, 0), 0)
    )
    wide = pltpu.VMEM((heads, BLK, LANES), jnp.float32)
    row_pad = -(-heads // 8) * 8
    column = pltpu.VMEM((BLK, LANES), jnp.float32)
    return pl.pallas_call(
        functools.partial(mixer_back_kernel, heads, count),
        out_shape=(
            jax.ShapeDtypeStruct((tokens, channels), jnp.bfloat16),
            jax.ShapeDtypeStruct((tokens, 3 * LANES), jnp.bfloat16),
            jax.ShapeDtypeStruct((8, channels), jnp.float32),
            jax.ShapeDtypeStruct((8, 2 * NS), jnp.float32),
            jax.ShapeDtypeStruct((8, LANES), jnp.float32),
        ),
        grid_spec=pltpu.PrefetchScalarGridSpec(
            num_scalar_prefetch=1,
            grid=(count,),
            in_specs=[
                rows(channels),
                tail(channels),
                rows(3 * LANES),
                tail(3 * LANES),
                whole(8, channels),
                whole(8, 2 * NS),
                whole(8, LANES),
                rows(channels),
                pl.BlockSpec((1, NS, channels), lambda i, *_: (turn(i), 0, 0)),
            ],
            out_specs=[rows(channels), rows(3 * LANES), whole(8, channels), whole(8, 2 * NS), whole(8, LANES)],
            scratch_shapes=[
                pltpu.VMEM((BLK + 8, channels), jnp.float32),
                pltpu.VMEM((BLK + 8, 2 * NS), jnp.float32),
                pltpu.VMEM((BLK + 8, channels), jnp.float32),
                pltpu.VMEM((BLK + 8, 2 * NS), jnp.float32),
                pltpu.VMEM((NS, channels), jnp.float32),
                wide,
                wide,
                pltpu.VMEM((row_pad, BLK), jnp.float32),
                pltpu.VMEM((LANES, BLK), jnp.float32),
                pltpu.VMEM((BLK, BLK), jnp.float32),
                pltpu.VMEM((BLK, 2 * NS), jnp.float32),
                column,
                column,
                column,
                pltpu.VMEM((8, LANES), jnp.float32),
            ],
        ),
        compiler_params=pltpu.CompilerParams(vmem_limit_bytes=VMEM_LIMIT),
        name="mixer_back",
        interpret=interpret,
    )(opens, inner, inner, small, small, tx, ts, table, ybar, entered)


Y_SIZE = 2


def swap_pairs(size):
    return [(i, i ^ 1) for i in range(size)]


def gather_dp(shard, axis):
    count = lax.axis_size("dp")
    if count != 8:
        return lax.all_gather(shard, "dp", axis=axis, tiled=True)
    rows = count // Y_SIZE
    index = lax.axis_index("dp")
    row, column = index // Y_SIZE, index % Y_SIZE
    width = shard.shape[axis]
    held = {0: shard}
    for shift in range(1, rows):
        perm = [(i, (i + shift * Y_SIZE) % count) for i in range(count)]
        held[shift] = lax.ppermute(shard, "dp", perm)
    shape = list(shard.shape)
    shape[axis] = width * count
    full = jnp.zeros(shape, shard.dtype)
    for shift in range(rows):
        other = lax.ppermute(held[shift], "dp", swap_pairs(count))
        base = ((row - shift) % rows) * Y_SIZE
        full = lax.dynamic_update_slice_in_dim(full, held[shift], (base + column) * width, axis)
        full = lax.dynamic_update_slice_in_dim(full, other, (base + 1 - column) * width, axis)
    return full


def reduce_dp(value, axis):
    count = lax.axis_size("dp")
    low = jnp.bfloat16
    if count != 8:
        return lax.psum_scatter(
            value.astype(low), "dp", scatter_dimension=axis, tiled=True
        ).astype(jnp.float32)
    rows = count // Y_SIZE
    index = lax.axis_index("dp")
    row, column = index // Y_SIZE, index % Y_SIZE
    width = value.shape[axis] // count
    total = None
    for shift in (1, 2, 3, 0):
        base = ((row + shift) % rows) * Y_SIZE
        away = lax.dynamic_slice_in_dim(value, (base + 1 - column) * width, width, axis)
        kept = lax.dynamic_slice_in_dim(value, (base + column) * width, width, axis)
        came = lax.ppermute(away.astype(low), "dp", swap_pairs(count))
        pair = kept + came.astype(jnp.float32)
        if shift:
            perm = [(i, (i + shift * Y_SIZE) % count) for i in range(count)]
            pair = lax.ppermute(pair.astype(low), "dp", perm).astype(jnp.float32)
        total = pair if total is None else total + pair
    return total


def reduce_head(value):
    count = lax.axis_size("head")
    low = jnp.bfloat16
    if count != 4:
        return lax.psum_scatter(value, "head", scatter_dimension=0, tiled=False)
    index = lax.axis_index("head")
    side, core = index // 2, index % 2
    both = value.reshape(2, 2, *value.shape[1:])
    away = lax.dynamic_index_in_dim(both, 1 - core, 1, keepdims=False)
    kept = lax.dynamic_index_in_dim(both, core, 1, keepdims=False)
    came = lax.ppermute(away.astype(low), "head", swap_pairs(count))
    pair = kept + came.astype(jnp.float32)
    away = lax.dynamic_index_in_dim(pair, 1 - side, 0, keepdims=False)
    kept = lax.dynamic_index_in_dim(pair, side, 0, keepdims=False)
    came = lax.ppermute(away.astype(low), "head", [(i, (i + 2) % 4) for i in range(count)])
    return kept + came.astype(jnp.float32)


def gather_head(piece, axis):
    count = lax.axis_size("head")
    if count != 4:
        return lax.all_gather(piece, "head", axis=axis, tiled=True)
    index = lax.axis_index("head")
    width = piece.shape[axis]
    near = lax.ppermute(piece, "head", swap_pairs(count))
    first = index % 2 == 0
    pair = jnp.concatenate(
        [jnp.where(first, piece, near), jnp.where(first, near, piece)], axis=axis
    )
    far = lax.ppermute(pair, "head", [(i, (i + 2) % 4) for i in range(count)])
    lower = index < 2
    return jnp.concatenate(
        [jnp.where(lower, pair, far), jnp.where(lower, far, pair)], axis=axis
    )


def body(
    inputs,
    cotangent,
    token_valid,
    block_opens,
    block_widths,
    weight_inner,
    weight_step,
    weight_output,
    weight_state,
    norm_gain,
    channel_table,
    head_table,
    state_filter,
    momentum_inner,
    momentum_step,
    momentum_output,
    momentum_state,
    momentum_gain,
    momentum_channel,
    momentum_head,
    momentum_filter,
    average_inner,
    average_step,
    average_output,
    average_state,
    average_gain,
    average_channel,
    average_head,
    average_filter,
):
    low = jnp.bfloat16
    full_type = jnp.float32
    count_dp = lax.axis_size("dp")
    count_head = lax.axis_size("head")
    tokens, channels = inputs.shape[0], weight_inner.shape[2]
    heads_own = weight_step.shape[1]
    rows_all, state_rows = weight_state.shape[0], state_filter.shape[0]
    width_state = weight_state.shape[1]
    filter_block = jnp.pad(state_filter.astype(low), ((0, rows_all - state_rows), (0, 0)))
    shared_piece = jnp.concatenate(
        [weight_state.astype(low), norm_gain.astype(low)[:, None], filter_block], axis=1
    )
    shared_rows = gather_head(shared_piece, 0)
    small_rows = jnp.concatenate(
        [shared_rows[:, :width_state], weight_step.astype(low), shared_rows[:, width_state:]],
        axis=1,
    )
    small_rows = jnp.pad(small_rows, ((0, 0), (0, width_state + LANES - small_rows.shape[1])))
    inner_value = gather_dp(weight_inner[:, 1].astype(low), 0)
    small_full = gather_dp(small_rows, 0)
    inner_gate = gather_dp(weight_inner[:, 0].astype(low), 0)
    output_full = gather_dp(weight_output.astype(low), 1)
    at_gain = width_state + heads_own
    gain_full = small_full[:, at_gain]
    filter_full = small_full[:, at_gain + 1 : at_gain + 1 + KC + 1]
    filter_full = filter_full.reshape(-1, rows_all, KC + 1)[:, :state_rows].reshape(-1, KC + 1)
    channel_used = rounded(channel_table)
    head_values = rounded(head_table)
    gathered = lax.all_gather(inputs, "head", axis=1, tiled=True)
    masked = cotangent * token_valid.astype(low)[:, None]
    shard_piece = lax.all_gather(masked, "head", axis=1, tiled=True)
    tokens_full = gathered.astype(full_type)
    inverse = lax.rsqrt(jnp.mean(tokens_full * tokens_full, axis=1) + EPS)
    gain_float = gain_full.astype(full_type)
    normed = (tokens_full * inverse[:, None] * gain_float[None, :]).astype(low)
    inner_x = jnp.dot(normed, inner_value, preferred_element_type=full_type)
    small_x = jnp.dot(normed, small_full, preferred_element_type=full_type)
    widths = jnp.repeat(block_widths, BLK)
    channel_head = jnp.arange(channels) // P_SIZE
    used = (channel_head[None, :] * H < widths[:, None] * heads_own).astype(full_type)
    norm_counts = widths.astype(full_type) * P_SIZE
    valid_rows = token_valid.astype(full_type)
    gate_gain = channel_used[KC + 1]
    skip_wide = jnp.repeat(head_values[2], P_SIZE)
    taps_x = jnp.concatenate(
        [channel_used, skip_wide[None, :], jnp.zeros((1, channels), full_type)], axis=0
    )
    taps_s = jnp.pad(filter_full.astype(full_type).T, ((0, 8 - KC - 1), (0, 0)))
    table = jnp.pad(head_values, ((0, 5), (0, LANES - heads_own)))
    mixed, entered = mixer(block_opens, block_widths, inner_x, small_x, taps_x, taps_s, table)
    gate_values = jnp.dot(normed, inner_gate, preferred_element_type=full_type)
    gate_share = jax.nn.sigmoid(gate_values)
    gate_silu = gate_values * gate_share
    gated = mixed * gate_silu
    local_sq = jnp.sum(gated * gated, axis=1)
    grad_normal = jnp.einsum(
        "tw,cw->tc", shard_piece, output_full, preferred_element_type=full_type
    )
    grad_gained = grad_normal * gate_gain[None, :]
    local_dot = jnp.sum(grad_gained * gated, axis=1)
    total_sq, total_dot = lax.psum(jnp.stack([local_sq, local_dot]), "head")
    norm_scale = lax.rsqrt(total_sq / norm_counts + EPS)
    projected = (gated * norm_scale[:, None] * gate_gain[None, :]).astype(low)
    partial_out = jnp.dot(projected, output_full, preferred_element_type=full_type)
    branch = lax.psum_scatter(
        partial_out.astype(low), "head", scatter_dimension=1, tiled=True
    ).astype(full_type)
    own_inputs = inputs.astype(full_type)
    layer_output = (own_inputs + valid_rows[:, None] * branch).astype(low)
    block_grad = jnp.einsum("tc,tw->cw", projected, shard_piece, preferred_element_type=full_type)
    grad_gate_gain = jnp.sum(grad_normal * gated * norm_scale[:, None], axis=0)
    scale_back = norm_scale * norm_scale * norm_scale / norm_counts * total_dot
    back_gated = grad_gained * norm_scale[:, None] - gated * scale_back[:, None]
    ybar = back_gated * gate_silu * used
    gate_slope = gate_share * (1.0 + gate_values * (1.0 - gate_share))
    gate_low = (back_gated * mixed * gate_slope).astype(low)
    inner_low, small_low, taps_grad, state_taps, table_grad = mixer_back(
        block_opens, inner_x, small_x, taps_x, taps_s, table, ybar, entered
    )
    grad_gate_w = jnp.einsum("td,tc->dc", normed, gate_low, preferred_element_type=full_type)
    grad_inner_w = jnp.einsum("td,tc->dc", normed, inner_low, preferred_element_type=full_type)
    grad_small = jnp.einsum("td,ts->ds", normed, small_low, preferred_element_type=full_type)
    grad_normed = jnp.einsum("tc,dc->td", gate_low, inner_gate, preferred_element_type=full_type)
    grad_normed = grad_normed + jnp.einsum(
        "tc,dc->td", inner_low, inner_value, preferred_element_type=full_type
    )
    grad_normed = grad_normed + jnp.einsum(
        "ts,ds->td", small_low, small_full, preferred_element_type=full_type
    )
    own_grad = lax.psum_scatter(
        grad_normed.astype(low), "head", scatter_dimension=1, tiled=True
    ).astype(full_type)
    own_width = inputs.shape[1]
    start_column = lax.axis_index("head") * own_width
    own_gain = lax.dynamic_slice_in_dim(gain_float, start_column, own_width)
    scaled = own_grad * own_gain[None, :]
    row_part = jnp.sum(scaled * own_inputs, axis=1)
    grad_gain_own = jnp.sum(own_grad * own_inputs * inverse[:, None], axis=0)
    row_total = lax.psum(row_part, "head")
    inverse_cube = inverse * inverse * inverse
    grad_input = (
        cotangent.astype(full_type)
        + inverse[:, None] * scaled
        - own_inputs * (inverse_cube * row_total / D)[:, None]
    )
    grad_gain_full = lax.dynamic_update_slice_in_dim(
        jnp.zeros((D,), full_type), grad_gain_own, start_column, 0
    )
    grad_channel = jnp.concatenate([taps_grad[: KC + 1], grad_gate_gain[None, :]], axis=0)
    grad_skip = jnp.sum(taps_grad[KC + 2].reshape(heads_own, P_SIZE), axis=1)
    grad_head = jnp.concatenate([table_grad[:2, :heads_own], grad_skip[None, :]], axis=0)
    grad_filter = state_taps[: KC + 1].T
    output_reduced = reduce_dp(block_grad, 1)
    gate_reduced = reduce_dp(grad_gate_w, 0)
    inner_reduced = reduce_dp(grad_inner_w, 0)
    inner_reduced = jnp.stack([gate_reduced, inner_reduced], axis=1)
    filter_part = jnp.pad(
        grad_filter.reshape(count_dp, count_head, state_rows * (KC + 1)),
        ((0, 0), (0, 0), (0, rows_all - state_rows * (KC + 1))),
    ).reshape(D, 1)
    shared_part = jnp.concatenate(
        [grad_small[:, :width_state], grad_gain_full[:, None], filter_part], axis=1
    ).reshape(count_dp, count_head, rows_all, width_state + 2)
    shared_own = reduce_head(jnp.swapaxes(shared_part, 0, 1))
    grad_step = grad_small[:, width_state : width_state + heads_own]
    table_part = jnp.concatenate([grad_channel.reshape(-1), grad_head.reshape(-1)])
    table_width = -(-table_part.shape[0] // rows_all)
    table_part = jnp.pad(table_part, (0, table_width * rows_all - table_part.shape[0]))
    table_part = jnp.broadcast_to(
        table_part.reshape(1, rows_all, table_width), (count_dp, rows_all, table_width)
    )
    step_part = grad_step.reshape(count_dp, rows_all, -1)
    small_part = jnp.concatenate([shared_own, step_part, table_part], axis=2)
    small_own = reduce_dp(small_part.reshape(count_dp * rows_all, -1), 0)
    state_reduced = small_own[:, :width_state]
    gain_reduced = small_own[:, width_state]
    filter_reduced = small_own[: state_rows * (KC + 1), width_state + 1].reshape(state_rows, KC + 1)
    at = width_state + 2
    step_reduced = small_own[:, at : at + step_part.shape[2]].reshape(-1, heads_own)
    table_own = small_own[:, at + step_part.shape[2] :].reshape(-1)
    channel_size = grad_channel.shape[0] * grad_channel.shape[1]
    channel_reduced = table_own[:channel_size].reshape(grad_channel.shape)
    head_reduced = table_own[channel_size : channel_size + grad_head.size].reshape(grad_head.shape)
    total_tokens = inputs.shape[0] * lax.axis_size("dp")
    matrix_rate = RATE_MATRIX / math.sqrt(total_tokens)
    vector_rate = RATE_VECTOR / math.sqrt(total_tokens)
    new_inner = advance(weight_inner, inner_reduced, momentum_inner, average_inner, matrix_rate)
    new_step = advance(weight_step, step_reduced, momentum_step, average_step, matrix_rate)
    new_output = advance(
        weight_output, output_reduced, momentum_output, average_output, matrix_rate
    )
    new_state = advance(weight_state, state_reduced, momentum_state, average_state, matrix_rate)
    new_gain = advance(norm_gain, gain_reduced, momentum_gain, average_gain, vector_rate)
    new_channel = advance(
        channel_table, channel_reduced, momentum_channel, average_channel, vector_rate
    )
    new_head = advance(head_table, head_reduced, momentum_head, average_head, vector_rate)
    new_filter = advance(state_filter, filter_reduced, momentum_filter, average_filter, vector_rate)
    return (
        layer_output,
        grad_input,
        new_inner[0],
        new_inner[1],
        new_inner[2],
        new_step[0],
        new_step[1],
        new_step[2],
        new_output[0],
        new_output[1],
        new_output[2],
        new_state[0],
        new_state[1],
        new_state[2],
        new_gain[0],
        new_gain[1],
        new_gain[2],
        new_channel[0],
        new_channel[1],
        new_channel[2],
        new_head[0],
        new_head[1],
        new_head[2],
        new_filter[0],
        new_filter[1],
        new_filter[2],
    )


def solution(mesh):
    in_specs = (
        P("dp", "head"),
        P("dp", "head"),
        P("dp"),
        P("dp"),
        P("dp"),
        P("dp", None, "head"),
        P("dp", "head"),
        P("head", "dp"),
        P(("dp", "head"), None),
        P(("dp", "head")),
        P(None, "head"),
        P(None, "head"),
        P(("dp", "head"), None),
        P("dp", None, "head"),
        P("dp", "head"),
        P("head", "dp"),
        P(("dp", "head"), None),
        P(("dp", "head")),
        P(None, "head"),
        P(None, "head"),
        P(("dp", "head"), None),
        P("dp", None, "head"),
        P("dp", "head"),
        P("head", "dp"),
        P(("dp", "head"), None),
        P(("dp", "head")),
        P(None, "head"),
        P(None, "head"),
        P(("dp", "head"), None),
    )
    out_specs = (
        P("dp", "head"),
        P("dp", "head"),
        P("dp", None, "head"),
        P("dp", None, "head"),
        P("dp", None, "head"),
        P("dp", "head"),
        P("dp", "head"),
        P("dp", "head"),
        P("head", "dp"),
        P("head", "dp"),
        P("head", "dp"),
        P(("dp", "head"), None),
        P(("dp", "head"), None),
        P(("dp", "head"), None),
        P(("dp", "head")),
        P(("dp", "head")),
        P(("dp", "head")),
        P(None, "head"),
        P(None, "head"),
        P(None, "head"),
        P(None, "head"),
        P(None, "head"),
        P(None, "head"),
        P(("dp", "head"), None),
        P(("dp", "head"), None),
        P(("dp", "head"), None),
    )
    return jax.shard_map(body, mesh=mesh, in_specs=in_specs, out_specs=out_specs, check_vma=False)
```

```python
import functools
import math

import jax
import jax.numpy as jnp
from jax import lax
from jax.experimental import pallas as pl
from jax.experimental.pallas import tpu as pltpu
from jax.sharding import PartitionSpec as P

D = 2048
H = 64
P_SIZE = 64
NS = 128
KC = 4
BLK = 256


EPS = 1e-05
MOMENTUM = 0.9
DECAY = 0.0001
AVERAGE = 0.75
RATE_MATRIX = 0.02
RATE_VECTOR = 0.1
HIGHEST = lax.Precision.HIGHEST


def rounded(value):
    return lax.optimization_barrier(value.astype(jnp.bfloat16)).astype(jnp.float32)


def advance(weight, gradient, moment, average, rate):
    adjusted = gradient + DECAY * weight
    moment_next = MOMENTUM * moment + adjusted
    weight_next = weight - rate * (adjusted + MOMENTUM * moment_next)
    average_next = AVERAGE * average + (1.0 - AVERAGE) * weight_next
    return (weight_next, moment_next, average_next)


LANES = 128
Y_SIZE = 2
FAR = -1e30
NT = (((1,), (1,)), ((), ()))
TN = (((0,), (0,)), ((), ()))


def dot32(first, second, dims=(((1,), (0,)), ((), ()))):
    return lax.dot_general(first, second, dims, preferred_element_type=jnp.float32)


def lasting(micros):
    work = int(micros * 1.0 * 1_000_000)
    return pl.CostEstimate(flops=work * 1000, transcendentals=1, bytes_accessed=work * 3)


def softplus(value):
    return jnp.maximum(value, 0.0) + jnp.log1p(jnp.exp(-jnp.abs(value)))


def triangle(upper):
    first = lax.broadcasted_iota(jnp.int32, (BLK, BLK), 0)
    second = lax.broadcasted_iota(jnp.int32, (BLK, BLK), 1)
    return first <= second if upper else first >= second


def filtered(window, taps, lanes):
    total = taps[KC : KC + 1, lanes] + taps[0:1, lanes] * window[5 : 5 + BLK, lanes]
    for offset in range(1, KC):
        total = total + taps[offset : offset + 1, lanes] * window[5 + offset : 5 + offset + BLK, lanes]
    return total


def step_parts(raw, table, heads):
    lane = lax.broadcasted_iota(jnp.int32, (BLK, LANES), 1)
    shifted = raw + table[0:1, :]
    rates = jnp.where(lane < heads, softplus(shifted), 0.0)
    decay = -jnp.exp(table[1:2, :])
    cumulated = jnp.dot(
        triangle(False).astype(jnp.float32),
        rates * decay,
        precision=HIGHEST,
        preferred_element_type=jnp.float32,
    )
    return shifted, rates, decay, cumulated


def spread_columns(value, out, heads):
    for head in range(heads):
        out[head] = jnp.broadcast_to(value[:, head : head + 1], (BLK, LANES))


def mixer_kernel(
    heads, opens, widths, v_ref, s_ref, tx, ts, table, mixed, entered,
    window, window_s, state, xs, cum_wide, rate_wide, cum_rows, rate_rows,
):
    block = pl.program_id(0)
    low = jnp.bfloat16

    @pl.when(opens[block] == 1)
    def _():
        window[0:8, :] = jnp.zeros_like(window[0:8, :])
        window_s[0:8, :] = jnp.zeros_like(window_s[0:8, :])
        state[...] = jnp.zeros_like(state)

    @pl.when(opens[block] != 1)
    def _():
        window[0:8, :] = window[BLK : BLK + 8, :]
        window_s[0:8, :] = window_s[BLK : BLK + 8, :]

    window[8 : 8 + BLK, :] = v_ref[...]
    window_s[8 : 8 + BLK, :] = s_ref[:, : 2 * NS]
    shared = filtered(window_s, ts, slice(None))
    shared = (shared * jax.nn.sigmoid(shared)).astype(low)
    maps_in, maps_out = shared[:, :NS], shared[:, NS:]
    maps_in_t = jnp.transpose(maps_in.astype(jnp.float32)).astype(low)
    _, rates, _, cumulated = step_parts(s_ref[:, 2 * NS :], table, heads)
    cum_rows[...] = jnp.transpose(cumulated)[: cum_rows.shape[0]]
    rate_rows[...] = jnp.transpose(rates)[: rate_rows.shape[0]]
    spread_columns(cumulated, cum_wide, heads)
    spread_columns(rates, rate_wide, heads)
    crossing = dot32(maps_out, maps_in, NT)
    width = widths[block]

    def pair(index, _):
        lanes = pl.ds(pl.multiple_of(index * LANES, LANES), LANES)
        pre = filtered(window, tx, lanes)
        values = (pre * jax.nn.sigmoid(pre)).astype(low)
        side = lax.broadcasted_iota(jnp.int32, (BLK, LANES), 1) < P_SIZE
        lower = triangle(False)
        cum_pair = jnp.where(side, cum_wide[2 * index], cum_wide[2 * index + 1])
        rate_pair = jnp.where(side, rate_wide[2 * index], rate_wide[2 * index + 1])
        now = state[:, lanes]
        entered[0, :, lanes] = now
        total = jnp.exp(cum_pair) * dot32(maps_out, now.astype(low))
        for half in range(2):
            head = 2 * index + half
            column = cum_wide[head]
            spread = jnp.concatenate([column, column], axis=1) - cum_rows[pl.ds(head, 1), :]
            decays = jnp.exp(jnp.where(lower, spread, FAR))
            mixing = (crossing * decays * rate_rows[pl.ds(head, 1), :]).astype(low)
            own = side if half == 0 else jnp.logical_not(side)
            total = total + dot32(mixing, jnp.where(own, values, jnp.zeros_like(values)))
        wide = values.astype(jnp.float32)
        total = total + tx[6:7, lanes] * wide
        row = lax.broadcasted_iota(jnp.int32, (1, LANES), 1)
        head_row = 2 * index + (row >= P_SIZE).astype(jnp.int32)
        used = (head_row * H < width * heads).astype(jnp.float32)
        mixed[:, lanes] = total * used
        last = cum_pair[BLK - 1 : BLK, :]
        ending = jnp.exp(last - cum_pair) * rate_pair
        state[:, lanes] = jnp.exp(last) * now + dot32(maps_in_t, (wide * ending).astype(low))
        return 0

    lax.fori_loop(0, heads // 2, pair, 0)


def mixer_back_kernel(
    heads, count, opens, v_ref, v_tail, s_ref, s_tail, tx, ts, table, ybar, entered,
    inner_low, small_low, tx_grad, ts_grad, table_grad,
    window, window_s, ahead, ahead_s, state_grad, cum_wide, rate_wide,
    cum_rows, z_rows, cross_grad, maps_grad, column_sum, outer_sum, rate_sum, last_sum,
):
    low = jnp.bfloat16
    step = pl.program_id(0)
    block = count - 1 - step
    opened = opens[block] == 1

    @pl.when(step == 0)
    def _():
        ahead[BLK : BLK + 8, :] = jnp.zeros_like(ahead[BLK : BLK + 8, :])
        ahead_s[BLK : BLK + 8, :] = jnp.zeros_like(ahead_s[BLK : BLK + 8, :])
        state_grad[...] = jnp.zeros_like(state_grad)
        tx_grad[...] = jnp.zeros_like(tx_grad)
        ts_grad[...] = jnp.zeros_like(ts_grad)
        table_grad[...] = jnp.zeros_like(table_grad)
        z_rows[...] = jnp.zeros_like(z_rows)

    @pl.when(opened)
    def _():
        window[0:8, :] = jnp.zeros_like(window[0:8, :])
        window_s[0:8, :] = jnp.zeros_like(window_s[0:8, :])

    @pl.when(jnp.logical_not(opened))
    def _():
        window[0:8, :] = v_tail[...]
        window_s[0:8, :] = s_tail[:, : 2 * NS]

    window[8 : 8 + BLK, :] = v_ref[...]
    window_s[8 : 8 + BLK, :] = s_ref[:, : 2 * NS]
    pre_s = filtered(window_s, ts, slice(None))
    share_s = jax.nn.sigmoid(pre_s)
    shared = (pre_s * share_s).astype(low)
    slope_s = share_s * (1.0 + pre_s * (1.0 - share_s))
    maps_in, maps_out = shared[:, :NS], shared[:, NS:]
    maps_out_t = jnp.transpose(maps_out.astype(jnp.float32)).astype(low)
    shifted, rates, decay, cumulated = step_parts(s_ref[:, 2 * NS :], table, heads)
    cum_rows[...] = jnp.transpose(cumulated)[: cum_rows.shape[0]]
    spread_columns(cumulated, cum_wide, heads)
    spread_columns(rates, rate_wide, heads)
    crossing = dot32(maps_in, maps_out, NT)
    for held in (cross_grad, maps_grad, column_sum, outer_sum, rate_sum, last_sum):
        held[...] = jnp.zeros_like(held)

    def pair(index, _):
        lanes = pl.ds(pl.multiple_of(index * LANES, LANES), LANES)
        pre = filtered(window, tx, lanes)
        share = jax.nn.sigmoid(pre)
        values = (pre * share).astype(low)
        slope = share * (1.0 + pre * (1.0 - share))
        lane = lax.broadcasted_iota(jnp.int32, (BLK, LANES), 1)
        side = lane < P_SIZE
        upper = triangle(True)
        cum_pair = jnp.where(side, cum_wide[2 * index], cum_wide[2 * index + 1])
        rate_pair = jnp.where(side, rate_wide[2 * index], rate_wide[2 * index + 1])
        back = ybar[:, lanes]
        back_low = back.astype(low)
        wide = values.astype(jnp.float32)
        now = entered[0, :, lanes]
        now_low = now.astype(low)
        after = state_grad[:, lanes]
        after_low = after.astype(low)
        grown = jnp.exp(cum_pair)
        last = cum_pair[BLK - 1 : BLK, :]
        total_decay = jnp.exp(last)
        ending = jnp.exp(last - cum_pair) * rate_pair
        outer = dot32(maps_out, now_low)
        inward = dot32(maps_in, after_low)
        back_grown = back * grown
        back_grown_low = back_grown.astype(low)
        maps_grad[:, NS:] += dot32(back_grown_low, now_low, NT)
        maps_grad[:, :NS] += dot32((wide * ending).astype(low), after_low, NT)
        state_grad[:, lanes] = total_decay * after + dot32(maps_out_t, back_grown_low)
        grad = ending * inward + tx[6:7, lanes] * back
        pick = (
            lax.broadcasted_iota(jnp.int32, (LANES, LANES), 1)
            == 2 * index + (lax.broadcasted_iota(jnp.int32, (LANES, LANES), 0) >= P_SIZE).astype(jnp.int32)
        ).astype(low)

        def to_heads(value):
            high = value.astype(low)
            rest = (value - high.astype(jnp.float32)).astype(low)
            return dot32(high, pick) + dot32(rest, pick)

        outer_sum[...] += to_heads(back_grown * outer)
        rate_sum[...] += to_heads(wide * inward)
        kept = jnp.sum(total_decay * after * now, axis=0, keepdims=True)
        last_sum[...] += to_heads(jnp.broadcast_to(kept, (8, LANES)))
        tx_grad[6:7, lanes] += jnp.sum(back * wide, axis=0, keepdims=True)
        zero = jnp.zeros_like(values)
        for half in range(2):
            head = 2 * index + half
            own = side if half == 0 else jnp.logical_not(side)
            column = cum_wide[head]
            rate = rate_wide[head]
            spread = cum_rows[pl.ds(head, 1), :] - jnp.concatenate([column, column], axis=1)
            decays = jnp.exp(jnp.where(upper, spread, FAR))
            weighted = decays * jnp.concatenate([rate, rate], axis=1)
            products = dot32(jnp.where(own, values, zero), back_low, NT)
            summed = jnp.sum(products * (crossing * decays), axis=1, keepdims=True)
            column_sum[...] += jnp.where(lane == head, summed, 0.0)
            mixing = crossing * weighted
            z_rows[pl.ds(head, 1), :] = jnp.sum(products * mixing, axis=0, keepdims=True)
            cross_grad[...] += products * weighted
            grad = grad + dot32(mixing.astype(low), jnp.where(own, back_low, zero))
        back_pre = grad * slope
        ahead[0:BLK, lanes] = back_pre
        spent = tx[KC - 1 : KC, lanes] * back_pre
        for offset in range(1, KC):
            spent = spent + tx[KC - 1 - offset : KC - offset, lanes] * ahead[offset : offset + BLK, lanes]
        inner_low[:, lanes] = spent.astype(low)
        for position in range(KC):
            tx_grad[position : position + 1, lanes] += jnp.sum(
                back_pre * window[5 + position : 5 + position + BLK, lanes], axis=0, keepdims=True
            )
        tx_grad[KC : KC + 1, lanes] += jnp.sum(back_pre, axis=0, keepdims=True)
        return 0

    lax.fori_loop(0, heads // 2, pair, 0)
    cross = cross_grad[...]
    cross_low = cross.astype(low)
    maps_grad[:, :NS] += dot32(cross_low, maps_out)
    maps_grad[:, NS:] += dot32(jnp.transpose(cross).astype(low), maps_in)
    back_pre_s = maps_grad[...] * slope_s
    ahead_s[0:BLK, :] = back_pre_s
    spent_s = ts[KC - 1 : KC, :] * back_pre_s
    for offset in range(1, KC):
        spent_s = spent_s + ts[KC - 1 - offset : KC - offset, :] * ahead_s[offset : offset + BLK, :]
    small_low[:, : 2 * NS] = spent_s.astype(low)
    for position in range(KC):
        ts_grad[position : position + 1, :] += jnp.sum(
            back_pre_s * window_s[5 + position : 5 + position + BLK, :], axis=0, keepdims=True
        )
    ts_grad[KC : KC + 1, :] += jnp.sum(back_pre_s, axis=0, keepdims=True)
    lane = lax.broadcasted_iota(jnp.int32, (BLK, LANES), 1)
    falling = jnp.exp(cumulated[BLK - 1 : BLK, :] - cumulated)
    ended = rate_sum[...] * falling
    ended_rate = ended * rates
    own_sum = column_sum[...]
    cum_grad = jnp.transpose(z_rows[...]) + outer_sum[...] - rates * own_sum - ended_rate
    final = last_sum[0:1, :] + jnp.sum(ended_rate, axis=0, keepdims=True)
    place = lax.broadcasted_iota(jnp.int32, (BLK, LANES), 0)
    cum_grad = cum_grad + jnp.where(place == BLK - 1, final, 0.0)
    log_grad = jnp.dot(
        triangle(True).astype(jnp.float32),
        cum_grad,
        precision=HIGHEST,
        preferred_element_type=jnp.float32,
    )
    rate_grad = own_sum + ended + decay * log_grad
    raw_grad = jnp.where(lane < heads, rate_grad * jax.nn.sigmoid(shifted), 0.0)
    small_low[:, 2 * NS :] = raw_grad.astype(low)
    table_grad[0:1, :] += jnp.sum(raw_grad, axis=0, keepdims=True)
    table_grad[1:2, :] += decay * jnp.sum(rates * log_grad, axis=0, keepdims=True)

    @pl.when(opened)
    def _():
        ahead[BLK : BLK + 8, :] = jnp.zeros_like(ahead[BLK : BLK + 8, :])
        ahead_s[BLK : BLK + 8, :] = jnp.zeros_like(ahead_s[BLK : BLK + 8, :])
        state_grad[...] = jnp.zeros_like(state_grad)

    @pl.when(jnp.logical_not(opened))
    def _():
        ahead[BLK : BLK + 8, :] = ahead[0:8, :]
        ahead_s[BLK : BLK + 8, :] = ahead_s[0:8, :]


VMEM_LIMIT = 56 * 1024 * 1024


def mixer(opens, widths, inner, small, tx, ts, table, interpret=False):
    tokens, channels = inner.shape
    heads, count = channels // P_SIZE, tokens // BLK
    whole = lambda rows, columns: pl.BlockSpec((rows, columns), lambda i, *_: (0, 0))
    rows = lambda columns: pl.BlockSpec((BLK, columns), lambda i, *_: (i, 0))
    wide = pltpu.VMEM((heads, BLK, LANES), jnp.float32)
    row_pad = -(-heads // 8) * 8
    return pl.pallas_call(
        functools.partial(mixer_kernel, heads),
        out_shape=(
            jax.ShapeDtypeStruct((tokens, channels), jnp.float32),
            jax.ShapeDtypeStruct((count, NS, channels), jnp.float32),
        ),
        grid_spec=pltpu.PrefetchScalarGridSpec(
            num_scalar_prefetch=2,
            grid=(count,),
            in_specs=[rows(channels), rows(3 * LANES), whole(8, channels), whole(8, 2 * NS), whole(8, LANES)],
            out_specs=[rows(channels), pl.BlockSpec((1, NS, channels), lambda i, *_: (i, 0, 0))],
            scratch_shapes=[
                pltpu.VMEM((BLK + 8, channels), jnp.float32),
                pltpu.VMEM((BLK + 8, 2 * NS), jnp.float32),
                pltpu.VMEM((NS, channels), jnp.float32),
                pltpu.VMEM((8, LANES), jnp.bfloat16),
                wide,
                wide,
                pltpu.VMEM((row_pad, BLK), jnp.float32),
                pltpu.VMEM((row_pad, BLK), jnp.float32),
            ],
        ),
        compiler_params=pltpu.CompilerParams(vmem_limit_bytes=VMEM_LIMIT),
        cost_estimate=lasting(25),
        name="mixer",
        interpret=interpret,
    )(opens, widths, inner, small, tx, ts, table)


def mixer_back(opens, inner, small, tx, ts, table, ybar, entered, interpret=False):
    tokens, channels = inner.shape
    heads, count = channels // P_SIZE, tokens // BLK
    per = BLK // 8
    turn = lambda i: count - 1 - i
    whole = lambda rows, columns: pl.BlockSpec((rows, columns), lambda i, *_: (0, 0))
    rows = lambda columns: pl.BlockSpec((BLK, columns), lambda i, *_: (turn(i), 0))
    tail = lambda columns: pl.BlockSpec(
        (8, columns), lambda i, *_: (jnp.maximum(turn(i) * per - 1, 0), 0)
    )
    wide = pltpu.VMEM((heads, BLK, LANES), jnp.float32)
    row_pad = -(-heads // 8) * 8
    column = pltpu.VMEM((BLK, LANES), jnp.float32)
    return pl.pallas_call(
        functools.partial(mixer_back_kernel, heads, count),
        out_shape=(
            jax.ShapeDtypeStruct((tokens, channels), jnp.bfloat16),
            jax.ShapeDtypeStruct((tokens, 3 * LANES), jnp.bfloat16),
            jax.ShapeDtypeStruct((8, channels), jnp.float32),
            jax.ShapeDtypeStruct((8, 2 * NS), jnp.float32),
            jax.ShapeDtypeStruct((8, LANES), jnp.float32),
        ),
        grid_spec=pltpu.PrefetchScalarGridSpec(
            num_scalar_prefetch=1,
            grid=(count,),
            in_specs=[
                rows(channels),
                tail(channels),
                rows(3 * LANES),
                tail(3 * LANES),
                whole(8, channels),
                whole(8, 2 * NS),
                whole(8, LANES),
                rows(channels),
                pl.BlockSpec((1, NS, channels), lambda i, *_: (turn(i), 0, 0)),
            ],
            out_specs=[rows(channels), rows(3 * LANES), whole(8, channels), whole(8, 2 * NS), whole(8, LANES)],
            scratch_shapes=[
                pltpu.VMEM((BLK + 8, channels), jnp.float32),
                pltpu.VMEM((BLK + 8, 2 * NS), jnp.float32),
                pltpu.VMEM((BLK + 8, channels), jnp.float32),
                pltpu.VMEM((BLK + 8, 2 * NS), jnp.float32),
                pltpu.VMEM((NS, channels), jnp.float32),
                wide,
                wide,
                pltpu.VMEM((row_pad, BLK), jnp.float32),
                pltpu.VMEM((LANES, BLK), jnp.float32),
                pltpu.VMEM((BLK, BLK), jnp.float32),
                pltpu.VMEM((BLK, 2 * NS), jnp.float32),
                column,
                column,
                column,
                pltpu.VMEM((8, LANES), jnp.float32),
            ],
        ),
        compiler_params=pltpu.CompilerParams(vmem_limit_bytes=VMEM_LIMIT),
        cost_estimate=lasting(43),
        name="mixer_back",
        interpret=interpret,
    )(opens, inner, inner, small, small, tx, ts, table, ybar, entered)


def advance_inner_kernel(rate, count, weight, moment, average, *refs):
    parts, outs = refs[:-3], refs[-3:]

    def total(some):
        return sum(x[...].astype(jnp.float32) for x in some)

    for k, gradient in enumerate((total(parts[:count]), total(parts[count:]))):
        news = advance(weight[:, k, :], gradient, moment[:, k, :], average[:, k, :], rate)
        for out, new in zip(outs, news):
            out[:, k, :] = new


def advance_inner(weight, moment, average, gate, inner, rate):
    rows, two, columns = weight.shape
    count = len(gate)
    tile = min(rows, 64)
    pair = pl.BlockSpec((tile, two, columns), lambda i: (i, 0, 0))
    flat = lambda n: pl.BlockSpec((tile, n), lambda i: (i, 0))
    return pl.pallas_call(
        functools.partial(advance_inner_kernel, rate, count),
        out_shape=(jax.ShapeDtypeStruct(weight.shape, weight.dtype),) * 3,
        grid=(rows // tile,),
        in_specs=[pair] * 3 + [flat(columns)] * (count + len(inner)),
        out_specs=[pair] * 3,
        compiler_params=pltpu.CompilerParams(vmem_limit_bytes=VMEM_LIMIT),
        cost_estimate=lasting(8),
        name="advance_inner",
    )(weight, moment, average, *gate, *inner)


def swap_pairs(size):
    return [(i, i ^ 1) for i in range(size)]


def after(value, *earlier):
    return lax.optimization_barrier((value, *earlier))[0]


def place_kernel(count, slots, *refs):
    pieces, out = refs[:count], refs[count]
    step = pl.program_id(0)
    for i in range(count):

        @pl.when(step == i)
        def _(i=i):
            out[...] = pieces[i][...]


def place(pieces, slots, shape=None):
    count = len(pieces)
    pieces = [x if isinstance(x, tuple) else (x, 0) for x in pieces]
    shape = shape or pieces[0][0].shape
    return pl.pallas_call(
        functools.partial(place_kernel, count),
        out_shape=jax.ShapeDtypeStruct((shape[0] * count, *shape[1:]), pieces[0][0].dtype),
        grid_spec=pltpu.PrefetchScalarGridSpec(
            num_scalar_prefetch=1,
            grid=(count,),
            in_specs=[pl.BlockSpec(shape, lambda i, slots, at=at: (at, 0)) for _, at in pieces],
            out_specs=pl.BlockSpec(shape, lambda i, slots: (slots[i], 0)),
        ),
        compiler_params=pltpu.CompilerParams(vmem_limit_bytes=VMEM_LIMIT),
        cost_estimate=lasting(4),
        name="place",
    )(jnp.stack(slots).astype(jnp.int32), *[x for x, _ in pieces])


def my_column():
    return lax.axis_index("dp") % Y_SIZE


def split_own(value, axis):
    count = lax.axis_size("dp")
    shape = value.shape
    wide = value.reshape(
        *shape[:axis], count // Y_SIZE, Y_SIZE, shape[axis] // count, *shape[axis + 1 :]
    )
    halves = [
        lax.index_in_dim(wide, i, axis + 1, keepdims=False).reshape(
            *shape[:axis], shape[axis] // Y_SIZE, *shape[axis + 1 :]
        )
        for i in range(Y_SIZE)
    ]
    first = my_column() == 0
    return jnp.where(first, halves[0], halves[1]), jnp.where(first, halves[1], halves[0])


def join_own(own, other, axis, width):
    first = my_column() == 0
    shape = own.shape
    halves = [
        x.reshape(*shape[:axis], shape[axis] // width, 1, width, *shape[axis + 1 :])
        for x in (jnp.where(first, own, other), jnp.where(first, other, own))
    ]
    return jnp.concatenate(halves, axis=axis + 1).reshape(
        *shape[:axis], shape[axis] * Y_SIZE, *shape[axis + 1 :]
    )


def halves_kernel(piece, column, x, own, other):
    value = x[...]
    first = column[0] == 0
    for row in range(value.shape[1] // piece // Y_SIZE):
        at = row * Y_SIZE * piece
        low, high = value[:, at : at + piece], value[:, at + piece : at + 2 * piece]
        own[:, row * piece : (row + 1) * piece] = jnp.where(first, low, high)
        other[:, row * piece : (row + 1) * piece] = jnp.where(first, high, low)


def split_columns(value):
    tokens, width = value.shape
    piece = width // lax.axis_size("dp")
    if piece % LANES:
        return split_own(value, 1)
    half = jax.ShapeDtypeStruct((tokens, width // Y_SIZE), value.dtype)
    rows = lambda columns: pl.BlockSpec((BLK, columns), lambda i, *_: (i, 0))
    return pl.pallas_call(
        functools.partial(halves_kernel, piece),
        out_shape=(half, half),
        grid_spec=pltpu.PrefetchScalarGridSpec(
            num_scalar_prefetch=1,
            grid=(tokens // BLK,),
            in_specs=[rows(width)],
            out_specs=[rows(width // Y_SIZE)] * 2,
        ),
        cost_estimate=lasting(5),
        name="halves",
    )(my_column().astype(jnp.int32)[None], value)


def rows_phase(shard):
    count = lax.axis_size("dp")
    held = [shard]
    for shift in range(1, count // Y_SIZE):
        perm = [(i, (i + shift * Y_SIZE) % count) for i in range(count)]
        held.append(lax.ppermute(shard, "dp", perm))
    return held


def begin_gather(shard):
    if lax.axis_size("dp") != 8:
        return [shard]
    return rows_phase(shard)


def end_gather(held, *later):
    if lax.axis_size("dp") != 8:
        return split_own(lax.all_gather(held[0], "dp", axis=0, tiled=True), 0)
    if later:
        held = list(lax.optimization_barrier((*held, *later))[: len(held)])
    row = lax.axis_index("dp") // Y_SIZE
    own = place(held, [(row - i) % len(held) for i in range(len(held))])
    return own, lax.ppermute(own, "dp", swap_pairs(8))


def begin_reduce(kept, away):
    count = lax.axis_size("dp")
    if count != 8:
        return kept, away
    return kept, lax.ppermute(away, "dp", swap_pairs(count))


def fold_pairs(begun, axis=0):
    kept, came = begun
    count = lax.axis_size("dp")
    if count != 8:
        width = kept.shape[axis] // (count // Y_SIZE)
        return None, join_own(kept.astype(came.dtype), came, axis, width)
    shape = kept.shape
    wide = (*shape[:axis], 2, 2, shape[axis] // 4, *shape[axis + 1 :])
    bit = (lax.axis_index("dp") // Y_SIZE) % 2

    def pick(which):
        first, second = (
            lax.dynamic_index_in_dim(x.reshape(wide), which, axis + 1, keepdims=False)
            for x in (kept, came)
        )
        return first + second.astype(jnp.float32)

    return pick(bit), pick(1 - bit).astype(came.dtype)


def swap_low(fold):
    kept, away = fold
    if kept is None:
        return fold
    return kept, lax.ppermute(away, "dp", [(i, i ^ Y_SIZE) for i in range(8)])


def fold_low(swapped, axis=0):
    kept, came = swapped
    if kept is None:
        return None, lax.psum_scatter(came, "dp", scatter_dimension=axis, tiled=True)
    bit = lax.axis_index("dp") // Y_SIZE // 2

    def pick(which):
        first, second = (
            lax.dynamic_index_in_dim(x, which, axis, keepdims=False) for x in (kept, came)
        )
        return first + second.astype(jnp.float32)

    return pick(bit), pick(1 - bit).astype(came.dtype)


def swap_high(fold):
    kept, away = fold
    if kept is None:
        return [away]
    return [kept, lax.ppermute(away, "dp", [(i, i ^ (2 * Y_SIZE)) for i in range(8)])]


def add_parts(parts):
    return sum(x.astype(jnp.float32) for x in parts)


def reduce_head(value):
    count = lax.axis_size("head")
    low = jnp.bfloat16
    if count != 4:
        return lax.psum_scatter(value, "head", scatter_dimension=0, tiled=False)
    index = lax.axis_index("head")
    side, core = index // 2, index % 2
    both = value.reshape(2, 2, *value.shape[1:])
    away = lax.dynamic_index_in_dim(both, 1 - core, 1, keepdims=False)
    kept = lax.dynamic_index_in_dim(both, core, 1, keepdims=False)
    came = lax.ppermute(away.astype(low), "head", swap_pairs(count))
    pair = kept + came.astype(jnp.float32)
    away = lax.dynamic_index_in_dim(pair, 1 - side, 0, keepdims=False)
    kept = lax.dynamic_index_in_dim(pair, side, 0, keepdims=False)
    came = lax.ppermute(away.astype(low), "head", [(i, (i + 2) % 4) for i in range(count)])
    return kept + came.astype(jnp.float32)


def gather_head(piece):
    count = lax.axis_size("head")
    if count != 4:
        return lax.all_gather(piece, "head", axis=0, tiled=True)
    index = lax.axis_index("head")
    far = lax.ppermute(piece, "head", [(i, (i + 2) % 4) for i in range(count)])
    near = lax.ppermute(piece, "head", swap_pairs(count))
    last = lax.ppermute(far, "head", swap_pairs(count))
    across = (index + 2) % 4
    return place([piece, near, far, last], [index, index ^ 1, across, across ^ 1])


LASTING = {
    "norm": 6,
    "project": 8,
    "gate": 10,
    "scale": 6,
    "weight": 8,
    "whole_weight": 11,
    "output_back": 11,
    "norm_back": 10,
    "output": 9,
    "input_back": 20,
}


def call(kernel, name, grid, scalars, args, in_specs, outs, out_specs):
    return pl.pallas_call(
        kernel,
        out_shape=outs,
        grid_spec=pltpu.PrefetchScalarGridSpec(
            num_scalar_prefetch=len(scalars), grid=grid, in_specs=in_specs, out_specs=out_specs
        ),
        compiler_params=pltpu.CompilerParams(vmem_limit_bytes=VMEM_LIMIT),
        cost_estimate=lasting(LASTING[name]),
        name=name,
    )(*scalars, *args)


def rows_of(columns):
    return pl.BlockSpec((BLK, columns), lambda i, *_: (i, 0))


def line_of():
    return pl.BlockSpec((1, BLK), lambda i, *_: (0, i))


def fixed(array):
    return pl.BlockSpec(array.shape, lambda i, *_: (0, 0))


def held_once(array):
    return pl.BlockSpec(array.shape, lambda i, *_: (0, 0), pipeline_mode=pl.Buffered(1))


def typed(kind, *shape):
    return jax.ShapeDtypeStruct(shape, kind)


def to_column(line, columns):
    column = jnp.transpose(jnp.broadcast_to(line, (LANES, BLK)))
    return jnp.concatenate([column] * (columns // LANES), axis=1)


def to_line(value):
    part = value[:, :LANES]
    for at in range(LANES, value.shape[1], LANES):
        part = part + value[:, at : at + LANES]
    return jnp.sum(jnp.transpose(part), axis=0, keepdims=True)


def halves_of(value, piece, first):
    starts = range(0, value.shape[1], Y_SIZE * piece)
    low = jnp.concatenate([value[:, s : s + piece] for s in starts], axis=1)
    high = jnp.concatenate([value[:, s + piece : s + 2 * piece] for s in starts], axis=1)
    return jnp.where(first, low, high), jnp.where(first, high, low)


def norm_kernel(own_in, other_in, gains, own, other, inverse):
    xs = [x[...].astype(jnp.float32) for x in (own_in, other_in)]
    width = xs[0].shape[1]
    sums = to_line(xs[0] * xs[0] + xs[1] * xs[1])
    scale = lax.rsqrt(sums / (2 * width) + EPS)
    inverse[...] = scale
    column = to_column(scale, width)
    for i, (x, out) in enumerate(zip(xs, (own, other))):
        out[...] = (x * column * gains[i : i + 1, :]).astype(jnp.bfloat16)


def norm(xs, gains):
    tokens, width = xs[0].shape
    half = typed(jnp.bfloat16, tokens, width)
    own, other, inverse = call(
        norm_kernel,
        "norm",
        (tokens // BLK,),
        (),
        (*xs, gains),
        [rows_of(width)] * 2 + [fixed(gains)],
        (half, half, typed(jnp.float32, 1, tokens)),
        [rows_of(width)] * 2 + [line_of()],
    )
    return [own, other], inverse


def project_kernel(own, other, w_own, w_other, out):
    out[...] = dot32(own[...], w_own[...]) + dot32(other[...], w_other[...])


def project(halves, weights):
    tokens, width = halves[0].shape
    columns = weights[0].shape[1]
    return call(
        project_kernel,
        "project",
        (tokens // BLK,),
        (),
        (*halves, *weights),
        [rows_of(width)] * 2 + [held_once(w) for w in weights],
        typed(jnp.float32, tokens, columns),
        rows_of(columns),
    )


def gate_kernel(own, other, w_own, w_other, mixed, gate, squares):
    value = dot32(own[...], w_own[...]) + dot32(other[...], w_other[...])
    gate[...] = value
    gated = mixed[...] * (value * jax.nn.sigmoid(value))
    squares[...] = to_line(gated * gated)


def gate_project(halves, weights, mixed):
    tokens, width = halves[0].shape
    columns = mixed.shape[1]
    return call(
        gate_kernel,
        "gate",
        (tokens // BLK,),
        (),
        (*halves, *weights, mixed),
        [rows_of(width)] * 2 + [held_once(w) for w in weights] + [rows_of(columns)],
        (typed(jnp.float32, tokens, columns), typed(jnp.float32, 1, tokens)),
        [rows_of(columns), line_of()],
    )


def scale_kernel(mixed, gate, scale, gain, out):
    value = gate[...]
    gated = mixed[...] * (value * jax.nn.sigmoid(value))
    column = to_column(scale[...], value.shape[1])
    out[...] = (gated * column * gain[...]).astype(jnp.bfloat16)


def scale_gated(mixed, gate, scale, gain):
    tokens, columns = mixed.shape
    return call(
        scale_kernel,
        "scale",
        (tokens // BLK,),
        (),
        (mixed, gate, scale, gain),
        [rows_of(columns)] * 2 + [line_of(), fixed(gain)],
        typed(jnp.bfloat16, tokens, columns),
        rows_of(columns),
    )


def weight_kernel(own, other, back, kept, away):
    kept[...] = dot32(own[...], back[...], TN)
    away[...] = dot32(other[...], back[...], TN).astype(jnp.bfloat16)


def weight_grad(halves, back):
    tokens, width = halves[0].shape
    columns = back.shape[1]
    strip = pl.BlockSpec((tokens, BLK), lambda i, *_: (0, i))
    return call(
        weight_kernel,
        "weight",
        (width // BLK,),
        (),
        (*halves, back),
        [strip] * 2 + [held_once(back)],
        (typed(jnp.float32, width, columns), typed(jnp.bfloat16, width, columns)),
        [rows_of(columns)] * 2,
    )


def whole_weight_kernel(column, own, other, back, out):
    mine = pl.program_id(1) == 0

    @pl.when(mine)
    def _():
        out[...] = dot32(own[...], back[...], TN).astype(jnp.bfloat16)

    @pl.when(jnp.logical_not(mine))
    def _():
        out[...] = dot32(other[...], back[...], TN).astype(jnp.bfloat16)


def whole_weight_grad(halves, back):
    tokens, width = halves[0].shape
    columns = back.shape[1]
    piece = Y_SIZE * width // lax.axis_size("dp")
    if piece % LANES:
        kept, away = weight_grad(halves, back)
        return join_own(kept.astype(away.dtype), away, 0, piece)
    strip = pl.BlockSpec((tokens, piece), lambda i, j, *_: (0, i))
    spot = lambda i, j, column: (Y_SIZE * i + (column[0] + j) % Y_SIZE, 0)
    return call(
        whole_weight_kernel,
        "whole_weight",
        (width // piece, Y_SIZE),
        (my_column().astype(jnp.int32)[None],),
        (*halves, back),
        [strip] * 2
        + [pl.BlockSpec(back.shape, lambda i, j, *_: (0, 0), pipeline_mode=pl.Buffered(1))],
        typed(jnp.bfloat16, Y_SIZE * width, columns),
        pl.BlockSpec((piece, columns), spot),
    )


def store_heads(out, column, own, other):
    first = column[0] == 0
    low = jnp.where(first, own, other).astype(out.dtype)
    high = jnp.where(first, other, own).astype(out.dtype)
    half = out.shape[2] // Y_SIZE
    for head in range(out.shape[0]):
        part = slice(head * half, (head + 1) * half)
        out[head, :, :half] = low[:, part]
        out[head, :, half:] = high[:, part]


def heads_out(tokens, width):
    count = lax.axis_size("head")
    columns = Y_SIZE * width // count
    shape = typed(jnp.bfloat16, count, tokens, columns)
    return shape, pl.BlockSpec((count, BLK, columns), lambda i, *_: (0, i, 0))


def aligned(width):
    count = lax.axis_size("dp")
    return count == Y_SIZE * lax.axis_size("head") and Y_SIZE * width // count % LANES == 0


def sum_heads(value):
    if isinstance(value, tuple):
        step = Y_SIZE * value[0].shape[1] // lax.axis_size("dp")
        whole = join_own(*value, 1, step)
        return lax.psum_scatter(whole, "head", scatter_dimension=1, tiled=True)
    index = lax.axis_index("head")
    side, core = index // 2, index % 2
    both = value.reshape(2, 2, *value.shape[1:])
    away = lax.dynamic_index_in_dim(both, 1 - core, 1, keepdims=False)
    kept = lax.dynamic_index_in_dim(both, core, 1, keepdims=False)
    near = lax.ppermute(away, "head", swap_pairs(4))
    away = lax.dynamic_index_in_dim(kept, 1 - side, 0, keepdims=False).astype(
        jnp.float32
    ) + lax.dynamic_index_in_dim(near, 1 - side, 0, keepdims=False)
    kept = lax.dynamic_index_in_dim(kept, side, 0, keepdims=False).astype(
        jnp.float32
    ) + lax.dynamic_index_in_dim(near, side, 0, keepdims=False)
    far = lax.ppermute(away.astype(value.dtype), "head", [(i, i ^ 2) for i in range(4)])
    return kept + far


def output_back_kernel(own, other, w_own, w_other, mixed, gate, gain, grad, dots):
    value = dot32(own[...], w_own[...]) + dot32(other[...], w_other[...])
    grad[...] = value
    raw = gate[...]
    gated = mixed[...] * (raw * jax.nn.sigmoid(raw))
    dots[...] = to_line(value * gain[...] * gated)


def output_back(halves, weights, mixed, gate, gain):
    tokens, width = halves[0].shape
    columns = mixed.shape[1]
    return call(
        output_back_kernel,
        "output_back",
        (tokens // BLK,),
        (),
        (*halves, *weights, mixed, gate, gain),
        [rows_of(width)] * 2
        + [held_once(w) for w in weights]
        + [rows_of(columns)] * 2
        + [fixed(gain)],
        (typed(jnp.float32, tokens, columns), typed(jnp.float32, 1, tokens)),
        [rows_of(columns), line_of()],
    )


def norm_back_kernel(heads, widths, grad, mixed, gate, gain, scale, scale_back, ybar, gate_low, gain_grad):
    block = pl.program_id(0)
    columns = grad.shape[1]
    raw = gate[...]
    share = jax.nn.sigmoid(raw)
    silu = raw * share
    value, state = grad[...], mixed[...]
    gated = state * silu
    column = to_column(scale[...], columns)
    back = value * gain[...] * column - gated * to_column(scale_back[...], columns)
    lane = lax.broadcasted_iota(jnp.int32, (1, columns), 1)
    used = ((lane // P_SIZE) * H < widths[block] * heads).astype(jnp.float32)
    ybar[...] = back * silu * used
    gate_low[...] = (back * state * (share * (1.0 + raw * (1.0 - share)))).astype(jnp.bfloat16)

    @pl.when(block == 0)
    def _():
        gain_grad[...] = jnp.zeros_like(gain_grad)

    gain_grad[...] += jnp.sum(value * gated * column, axis=0, keepdims=True)


def norm_back(widths, grad, mixed, gate, gain, scale, scale_back):
    tokens, columns = grad.shape
    return call(
        functools.partial(norm_back_kernel, columns // P_SIZE),
        "norm_back",
        (tokens // BLK,),
        (widths,),
        (grad, mixed, gate, gain, scale, scale_back),
        [rows_of(columns)] * 3 + [fixed(gain), line_of(), line_of()],
        (
            typed(jnp.float32, tokens, columns),
            typed(jnp.bfloat16, tokens, columns),
            typed(jnp.float32, 1, columns),
        ),
        [rows_of(columns)] * 2 + [pl.BlockSpec((1, columns), lambda i, *_: (0, 0))],
    )


def output_kernel(column, value, w_own, w_other, *outs):
    own, other = (dot32(value[...], w[...], NT) for w in (w_own, w_other))
    if len(outs) == 1:
        store_heads(outs[0], column, own, other)
    else:
        outs[0][...], outs[1][...] = own.astype(jnp.bfloat16), other.astype(jnp.bfloat16)


def output_project(value, weights):
    tokens, columns = value.shape
    width = weights[0].shape[0]
    half = typed(jnp.bfloat16, tokens, width)
    outs, out_specs = (half, half), [rows_of(width)] * 2
    if aligned(width):
        outs, out_specs = heads_out(tokens, width)
    return call(
        output_kernel,
        "output",
        (tokens // BLK,),
        (my_column().astype(jnp.int32)[None],),
        (value, *weights),
        [rows_of(columns)] + [held_once(w) for w in weights],
        outs,
        out_specs,
    )


def input_back_kernel(column, gate, inner, small, xo, xt, gains, inverse, *refs):
    weights, outs, line, sums = refs[:6], refs[6:-2], refs[-2], refs[-1]
    block = pl.program_id(0)
    scale = to_column(inverse[...], xo.shape[1])

    @pl.when(block == 0)
    def _():
        sums[...] = jnp.zeros_like(sums)

    total, values = None, []
    for i, x in enumerate((xo, xt)):
        value = (
            dot32(gate[...], weights[i][...], NT)
            + dot32(inner[...], weights[2 + i][...], NT)
            + dot32(small[...], weights[4 + i][...], NT)
        )
        values.append(value)
        product = value * x[...].astype(jnp.float32)
        sums[i : i + 1, :] += jnp.sum(product * scale, axis=0, keepdims=True)
        row = product * gains[i : i + 1, :]
        total = row if total is None else total + row
    line[...] = to_line(total)
    if len(outs) == 1:
        store_heads(outs[0], column, *values)
    else:
        outs[0][...], outs[1][...] = (v.astype(jnp.bfloat16) for v in values)


def input_back(backs, xs, gains, inverse, weights):
    tokens, width = xs[0].shape
    half = typed(jnp.bfloat16, tokens, width)
    outs, out_specs = [half, half], [rows_of(width)] * 2
    if aligned(width):
        outs, out_specs = [[x] for x in heads_out(tokens, width)]
    *grads, line, sums = call(
        input_back_kernel,
        "input_back",
        (tokens // BLK,),
        (my_column().astype(jnp.int32)[None],),
        (*backs, *xs, gains, inverse, *weights),
        [rows_of(b.shape[1]) for b in backs]
        + [rows_of(width)] * 2
        + [fixed(gains), line_of()]
        + [held_once(w) for w in weights],
        (*outs, typed(jnp.float32, 1, tokens), typed(jnp.float32, 2, width)),
        [*out_specs, line_of(), pl.BlockSpec((2, width), lambda i, *_: (0, 0))],
    )
    return grads[0] if len(grads) == 1 else tuple(grads), line, sums


def body(
    inputs,
    cotangent,
    token_valid,
    block_opens,
    block_widths,
    weight_inner,
    weight_step,
    weight_output,
    weight_state,
    norm_gain,
    channel_table,
    head_table,
    state_filter,
    momentum_inner,
    momentum_step,
    momentum_output,
    momentum_state,
    momentum_gain,
    momentum_channel,
    momentum_head,
    momentum_filter,
    average_inner,
    average_step,
    average_output,
    average_state,
    average_gain,
    average_channel,
    average_head,
    average_filter,
):
    low = jnp.bfloat16
    full_type = jnp.float32
    count_dp = lax.axis_size("dp")
    count_head = lax.axis_size("head")
    rows_dp, piece = count_dp // Y_SIZE, weight_inner.shape[0]
    tokens, channels = inputs.shape[0], weight_inner.shape[2]
    heads_own = weight_step.shape[1]
    rows_all, state_rows = weight_state.shape[0], state_filter.shape[0]
    width_state = weight_state.shape[1]
    filter_block = jnp.pad(state_filter.astype(low), ((0, rows_all - state_rows), (0, 0)))
    small_piece = jnp.concatenate(
        [
            weight_state.astype(low),
            weight_step.astype(low).reshape(rows_all, -1),
            norm_gain.astype(low)[:, None],
            filter_block,
        ],
        axis=1,
    )
    small_piece = jnp.pad(small_piece, ((0, 0), (0, -small_piece.shape[1] % LANES)))
    gathered = lax.all_gather(inputs, "head", axis=1, tiled=True)
    small_all = lax.all_gather(
        small_piece, ("dp", "head"), axis=0, tiled=False
    ).reshape(count_dp, count_head, rows_all, -1)
    step_size = rows_all * count_head * heads_own // rows_all
    step_full = lax.dynamic_index_in_dim(small_all, lax.axis_index("head"), 1, keepdims=False)
    step_full = step_full[:, :, width_state : width_state + step_size].reshape(D, heads_own)
    extra = small_all[:, :, :, width_state + step_size :].reshape(D, -1)[:, : 2 + KC]
    state_full = small_all[:, :, :, :width_state].reshape(D, width_state)
    filter_full = extra[:, 1:].reshape(-1, rows_all, KC + 1)[:, :state_rows].reshape(-1, KC + 1)
    gains = jnp.stack(split_own(extra[:, 0].astype(full_type), 0))
    step_wide = jnp.pad(step_full, ((0, 0), (0, LANES - heads_own)))
    small_w = split_own(jnp.concatenate([state_full, step_wide], axis=1), 0)
    shards = [
        weight_inner[:, 1].astype(low),
        weight_inner[:, 0].astype(low),
        weight_output.astype(low).T,
    ]
    inner_held = begin_gather(shards[0])
    inner_w = end_gather(inner_held)
    gate_held = begin_gather(after(shards[1], inner_w[0]))
    gate_w = end_gather(gate_held)
    output_held = begin_gather(after(shards[2], *gate_held[1:]))
    gate_w = end_gather(gate_held)
    channel_used = rounded(channel_table)
    head_values = rounded(head_table)
    masked = cotangent * token_valid.astype(low)[:, None]
    masked = after(masked, small_all)
    cots = split_columns(lax.all_gather(masked, "head", axis=1, tiled=True))
    xs = split_columns(gathered)
    normed, inverse_line = norm(xs, gains)
    inner_x = project(normed, inner_w)
    small_x = project(normed, small_w)
    widths = jnp.repeat(block_widths, BLK)
    norm_counts = (widths.astype(full_type) * P_SIZE)[None, :]
    valid_rows = token_valid.astype(full_type)
    gate_gain = channel_used[KC + 1]
    skip_wide = jnp.repeat(head_values[2], P_SIZE)
    taps_x = jnp.concatenate(
        [channel_used, skip_wide[None, :], jnp.zeros((1, channels), full_type)], axis=0
    )
    taps_s = jnp.pad(filter_full.astype(full_type).T, ((0, 8 - KC - 1), (0, 0)))
    table = jnp.pad(head_values, ((0, 5), (0, LANES - heads_own)))
    inner_x = after(inner_x, gate_w[0])
    mixed, entered = mixer(block_opens, block_widths, inner_x, small_x, taps_x, taps_s, table)
    output_w = end_gather(output_held, mixed)
    gate_w = lax.optimization_barrier((*gate_w, mixed, output_w[0]))[:2]
    gate_values, squares = gate_project(normed, gate_w, mixed)
    gain_line = gate_gain[None, :]
    norm_scale = lax.rsqrt(lax.psum(squares, "head") / norm_counts + EPS)
    projected = scale_gated(mixed, gate_values, norm_scale, gain_line)
    output_grad = whole_weight_grad(cots, projected)
    output_reduced = lax.psum_scatter(output_grad, "dp", scatter_dimension=0, tiled=True)
    output_w = lax.optimization_barrier((*output_w, projected))[:2]
    grad_normal, dot_line = output_back(cots, output_w, mixed, gate_values, gain_line)
    total_dot = lax.psum(dot_line, "head")
    scale_back = norm_scale * norm_scale * norm_scale / norm_counts * total_dot
    ybar, gate_low, grad_gate_gain = norm_back(
        block_widths, grad_normal, mixed, gate_values, gain_line, norm_scale, scale_back
    )
    gate_kept, gate_away = weight_grad(normed, gate_low)
    gate_begun = begin_reduce(gate_kept, gate_away)
    ybar = after(ybar, gate_away, gate_kept)
    inner_low, small_low, taps_grad, state_taps, table_grad = mixer_back(
        block_opens, inner_x, small_x, taps_x, taps_s, table, ybar, entered
    )
    inner_grad = whole_weight_grad(normed, inner_low)
    inner_reduced = lax.psum_scatter(inner_grad, "dp", scatter_dimension=0, tiled=True)
    inner_low, small_low, gate_came, projected = lax.optimization_barrier(
        (inner_low, small_low, gate_begun[1], projected, inner_grad)
    )[:4]
    gate_fold = fold_pairs((gate_begun[0], gate_came))
    gate_sent = swap_high(fold_low(swap_low(gate_fold)))
    grad_small = weight_grad(normed, small_low)
    backs = [gate_low, after(inner_low, gate_fold[1]), small_low]
    grad_normed, row_line, gain_sums = input_back(
        backs, xs, gains, inverse_line, (*gate_w, *inner_w, *small_w)
    )
    own_grad = sum_heads(grad_normed).astype(full_type)
    partial_out = output_project(after(projected, row_line), output_w)
    branch = sum_heads(partial_out).astype(full_type)
    own_inputs = inputs.astype(full_type)
    layer_output = (own_inputs + valid_rows[:, None] * branch).astype(low)
    grad_gain = [gain_sums[0], gain_sums[1]]
    inverse = inverse_line[0]
    row_total = lax.psum(row_line, "head")[0]
    own_width = inputs.shape[1]
    own_gain = lax.dynamic_slice_in_dim(
        join_own(gains[0], gains[1], 0, piece), lax.axis_index("head") * own_width, own_width
    )
    scaled = own_grad * own_gain[None, :]
    inverse_cube = inverse * inverse * inverse
    grad_input = (
        cotangent.astype(full_type)
        + inverse[:, None] * scaled
        - own_inputs * (inverse_cube * row_total / D)[:, None]
    )
    grad_channel = jnp.concatenate([taps_grad[: KC + 1], grad_gate_gain], axis=0)
    grad_skip = jnp.sum(taps_grad[KC + 2].reshape(heads_own, P_SIZE), axis=1)
    grad_head = jnp.concatenate([table_grad[:2, :heads_own], grad_skip[None, :]], axis=0)
    grad_filter = state_taps[: KC + 1].T
    filter_size = state_rows * (KC + 1)
    filter_part = jnp.pad(
        grad_filter.reshape(count_dp, count_head, filter_size),
        ((0, 0), (0, 0), (0, rows_all - filter_size)),
    ).reshape(D)
    shared_part = jnp.stack(
        [
            jnp.concatenate([s[:, :width_state].astype(full_type), g[:, None], f[:, None]], axis=1)
            for s, g, f in zip(grad_small, grad_gain, split_own(filter_part, 0))
        ]
    ).reshape(Y_SIZE, rows_dp, count_head, rows_all, width_state + 2)
    shared_own = reduce_head(jnp.moveaxis(shared_part, 2, 0))
    step_part = jnp.stack(
        [s[:, width_state : width_state + heads_own].astype(full_type) for s in grad_small]
    )
    step_part = step_part.reshape(Y_SIZE, rows_dp, rows_all, -1)
    table_part = jnp.concatenate([grad_channel.reshape(-1), grad_head.reshape(-1)])
    table_width = -(-table_part.shape[0] // rows_all)
    table_part = jnp.pad(table_part, (0, table_width * rows_all - table_part.shape[0]))
    table_part = jnp.broadcast_to(
        table_part.reshape(rows_all, table_width), (Y_SIZE, rows_dp, rows_all, table_width)
    )
    small_part = jnp.concatenate([shared_own, step_part, table_part], axis=3)
    small_part = small_part.reshape(Y_SIZE, rows_dp * rows_all, -1)
    small_begun = begin_reduce(small_part[0], small_part[1].astype(low))
    output_reduced = output_reduced.astype(full_type).T
    small_own = add_parts(swap_high(fold_low(swap_low(fold_pairs(small_begun)))))
    state_reduced = small_own[:, :width_state]
    gain_reduced = small_own[:, width_state]
    filter_reduced = small_own[:filter_size, width_state + 1].reshape(state_rows, KC + 1)
    at = width_state + 2
    step_reduced = small_own[:, at : at + step_part.shape[3]].reshape(-1, heads_own)
    table_own = small_own[:, at + step_part.shape[3] :].reshape(-1)
    channel_size = grad_channel.size
    channel_reduced = table_own[:channel_size].reshape(grad_channel.shape)
    head_reduced = table_own[channel_size : channel_size + grad_head.size].reshape(grad_head.shape)
    total_tokens = inputs.shape[0] * lax.axis_size("dp")
    matrix_rate = RATE_MATRIX / math.sqrt(total_tokens)
    vector_rate = RATE_VECTOR / math.sqrt(total_tokens)
    new_inner = advance_inner(
        weight_inner, momentum_inner, average_inner, gate_sent, [inner_reduced], matrix_rate
    )
    new_step = advance(weight_step, step_reduced, momentum_step, average_step, matrix_rate)
    new_output = advance(
        weight_output, output_reduced, momentum_output, average_output, matrix_rate
    )
    new_state = advance(weight_state, state_reduced, momentum_state, average_state, matrix_rate)
    new_gain = advance(norm_gain, gain_reduced, momentum_gain, average_gain, vector_rate)
    new_channel = advance(
        channel_table, channel_reduced, momentum_channel, average_channel, vector_rate
    )
    new_head = advance(head_table, head_reduced, momentum_head, average_head, vector_rate)
    new_filter = advance(state_filter, filter_reduced, momentum_filter, average_filter, vector_rate)
    return (
        layer_output,
        grad_input,
        new_inner[0],
        new_inner[1],
        new_inner[2],
        new_step[0],
        new_step[1],
        new_step[2],
        new_output[0],
        new_output[1],
        new_output[2],
        new_state[0],
        new_state[1],
        new_state[2],
        new_gain[0],
        new_gain[1],
        new_gain[2],
        new_channel[0],
        new_channel[1],
        new_channel[2],
        new_head[0],
        new_head[1],
        new_head[2],
        new_filter[0],
        new_filter[1],
        new_filter[2],
    )


def solution(mesh):
    in_specs = (
        P("dp", "head"),
        P("dp", "head"),
        P("dp"),
        P("dp"),
        P("dp"),
        P("dp", None, "head"),
        P("dp", "head"),
        P("head", "dp"),
        P(("dp", "head"), None),
        P(("dp", "head")),
        P(None, "head"),
        P(None, "head"),
        P(("dp", "head"), None),
        P("dp", None, "head"),
        P("dp", "head"),
        P("head", "dp"),
        P(("dp", "head"), None),
        P(("dp", "head")),
        P(None, "head"),
        P(None, "head"),
        P(("dp", "head"), None),
        P("dp", None, "head"),
        P("dp", "head"),
        P("head", "dp"),
        P(("dp", "head"), None),
        P(("dp", "head")),
        P(None, "head"),
        P(None, "head"),
        P(("dp", "head"), None),
    )
    out_specs = (
        P("dp", "head"),
        P("dp", "head"),
        P("dp", None, "head"),
        P("dp", None, "head"),
        P("dp", None, "head"),
        P("dp", "head"),
        P("dp", "head"),
        P("dp", "head"),
        P("head", "dp"),
        P("head", "dp"),
        P("head", "dp"),
        P(("dp", "head"), None),
        P(("dp", "head"), None),
        P(("dp", "head"), None),
        P(("dp", "head")),
        P(("dp", "head")),
        P(("dp", "head")),
        P(None, "head"),
        P(None, "head"),
        P(None, "head"),
        P(None, "head"),
        P(None, "head"),
        P(None, "head"),
        P(("dp", "head"), None),
        P(("dp", "head"), None),
        P(("dp", "head"), None),
    )
    return jax.shard_map(body, mesh=mesh, in_specs=in_specs, out_specs=out_specs, check_vma=False)
```

```python
import functools
import math

import jax
import jax.numpy as jnp
from jax import lax
from jax.experimental import pallas as pl
from jax.experimental.pallas import tpu as pltpu
from jax.sharding import PartitionSpec as P

D = 2048
H = 64
P_SIZE = 64
NS = 128
KC = 4
BLK = 256


EPS = 1e-05
MOMENTUM = 0.9
DECAY = 0.0001
AVERAGE = 0.75
RATE_MATRIX = 0.02
RATE_VECTOR = 0.1
HIGHEST = lax.Precision.HIGHEST


def rounded(value):
    return lax.optimization_barrier(value.astype(jnp.bfloat16)).astype(jnp.float32)


def advance(weight, gradient, moment, average, rate):
    adjusted = gradient + DECAY * weight
    moment_next = MOMENTUM * moment + adjusted
    weight_next = weight - rate * (adjusted + MOMENTUM * moment_next)
    average_next = AVERAGE * average + (1.0 - AVERAGE) * weight_next
    return (weight_next, moment_next, average_next)


LANES = 128
Y_SIZE = 2
FAR = -1e30
NT = (((1,), (1,)), ((), ()))
TN = (((0,), (0,)), ((), ()))


def dot32(first, second, dims=(((1,), (0,)), ((), ()))):
    return lax.dot_general(first, second, dims, preferred_element_type=jnp.float32)


def lasting(micros):
    work = int(micros * 1.0 * 1_000_000)
    return pl.CostEstimate(flops=work * 1000, transcendentals=1, bytes_accessed=work * 3)


def softplus(value):
    return jnp.maximum(value, 0.0) + jnp.log1p(jnp.exp(-jnp.abs(value)))


def triangle(upper):
    first = lax.broadcasted_iota(jnp.int32, (BLK, BLK), 0)
    second = lax.broadcasted_iota(jnp.int32, (BLK, BLK), 1)
    return first <= second if upper else first >= second


def filtered(window, taps, lanes):
    total = taps[KC : KC + 1, lanes] + taps[0:1, lanes] * window[5 : 5 + BLK, lanes]
    for offset in range(1, KC):
        total = total + taps[offset : offset + 1, lanes] * window[5 + offset : 5 + offset + BLK, lanes]
    return total


def step_parts(raw, table, heads):
    lane = lax.broadcasted_iota(jnp.int32, (BLK, LANES), 1)
    shifted = raw + table[0:1, :]
    rates = jnp.where(lane < heads, softplus(shifted), 0.0)
    decay = -jnp.exp(table[1:2, :])
    cumulated = jnp.dot(
        triangle(False).astype(jnp.float32),
        rates * decay,
        precision=HIGHEST,
        preferred_element_type=jnp.float32,
    )
    return shifted, rates, decay, cumulated


def spread_columns(value, out, heads):
    for head in range(heads):
        out[head] = jnp.broadcast_to(value[:, head : head + 1], (BLK, LANES))


def mixer_kernel(
    heads, opens, widths, v_ref, s_ref, tx, ts, table, mixed, entered,
    window, window_s, state, xs, cum_wide, rate_wide, cum_rows, rate_rows,
):
    block = pl.program_id(0)
    low = jnp.bfloat16

    @pl.when(opens[block] == 1)
    def _():
        window[0:8, :] = jnp.zeros_like(window[0:8, :])
        window_s[0:8, :] = jnp.zeros_like(window_s[0:8, :])
        state[...] = jnp.zeros_like(state)

    @pl.when(opens[block] != 1)
    def _():
        window[0:8, :] = window[BLK : BLK + 8, :]
        window_s[0:8, :] = window_s[BLK : BLK + 8, :]

    window[8 : 8 + BLK, :] = v_ref[...]
    window_s[8 : 8 + BLK, :] = s_ref[:, : 2 * NS]
    shared = filtered(window_s, ts, slice(None))
    shared = (shared * jax.nn.sigmoid(shared)).astype(low)
    maps_in, maps_out = shared[:, :NS], shared[:, NS:]
    maps_in_t = jnp.transpose(maps_in.astype(jnp.float32)).astype(low)
    _, rates, _, cumulated = step_parts(s_ref[:, 2 * NS :], table, heads)
    cum_rows[...] = jnp.transpose(cumulated)[: cum_rows.shape[0]]
    rate_rows[...] = jnp.transpose(rates)[: rate_rows.shape[0]]
    spread_columns(cumulated, cum_wide, heads)
    spread_columns(rates, rate_wide, heads)
    crossing = dot32(maps_out, maps_in, NT)
    width = widths[block]

    def pair(index, _):
        lanes = pl.ds(pl.multiple_of(index * LANES, LANES), LANES)
        pre = filtered(window, tx, lanes)
        values = (pre * jax.nn.sigmoid(pre)).astype(low)
        side = lax.broadcasted_iota(jnp.int32, (BLK, LANES), 1) < P_SIZE
        lower = triangle(False)
        cum_pair = jnp.where(side, cum_wide[2 * index], cum_wide[2 * index + 1])
        rate_pair = jnp.where(side, rate_wide[2 * index], rate_wide[2 * index + 1])
        now = state[:, lanes]
        entered[0, :, lanes] = now
        total = jnp.exp(cum_pair) * dot32(maps_out, now.astype(low))
        for half in range(2):
            head = 2 * index + half
            column = cum_wide[head]
            spread = jnp.concatenate([column, column], axis=1) - cum_rows[pl.ds(head, 1), :]
            decays = jnp.exp(jnp.where(lower, spread, FAR))
            mixing = (crossing * decays * rate_rows[pl.ds(head, 1), :]).astype(low)
            own = side if half == 0 else jnp.logical_not(side)
            total = total + dot32(mixing, jnp.where(own, values, jnp.zeros_like(values)))
        wide = values.astype(jnp.float32)
        total = total + tx[6:7, lanes] * wide
        row = lax.broadcasted_iota(jnp.int32, (1, LANES), 1)
        head_row = 2 * index + (row >= P_SIZE).astype(jnp.int32)
        used = (head_row * H < width * heads).astype(jnp.float32)
        mixed[:, lanes] = total * used
        last = cum_pair[BLK - 1 : BLK, :]
        ending = jnp.exp(last - cum_pair) * rate_pair
        state[:, lanes] = jnp.exp(last) * now + dot32(maps_in_t, (wide * ending).astype(low))
        return 0

    lax.fori_loop(0, heads // 2, pair, 0)


def mixer_back_kernel(
    heads, count, opens, v_ref, v_tail, s_ref, s_tail, tx, ts, table, ybar, entered,
    inner_low, small_low, tx_grad, ts_grad, table_grad,
    window, window_s, ahead, ahead_s, state_grad, cum_wide, rate_wide,
    cum_rows, z_rows, cross_grad, maps_grad, column_sum, outer_sum, rate_sum, last_sum,
):
    low = jnp.bfloat16
    step = pl.program_id(0)
    block = count - 1 - step
    opened = opens[block] == 1

    @pl.when(step == 0)
    def _():
        ahead[BLK : BLK + 8, :] = jnp.zeros_like(ahead[BLK : BLK + 8, :])
        ahead_s[BLK : BLK + 8, :] = jnp.zeros_like(ahead_s[BLK : BLK + 8, :])
        state_grad[...] = jnp.zeros_like(state_grad)
        tx_grad[...] = jnp.zeros_like(tx_grad)
        ts_grad[...] = jnp.zeros_like(ts_grad)
        table_grad[...] = jnp.zeros_like(table_grad)
        z_rows[...] = jnp.zeros_like(z_rows)

    @pl.when(opened)
    def _():
        window[0:8, :] = jnp.zeros_like(window[0:8, :])
        window_s[0:8, :] = jnp.zeros_like(window_s[0:8, :])

    @pl.when(jnp.logical_not(opened))
    def _():
        window[0:8, :] = v_tail[...]
        window_s[0:8, :] = s_tail[:, : 2 * NS]

    window[8 : 8 + BLK, :] = v_ref[...]
    window_s[8 : 8 + BLK, :] = s_ref[:, : 2 * NS]
    pre_s = filtered(window_s, ts, slice(None))
    share_s = jax.nn.sigmoid(pre_s)
    shared = (pre_s * share_s).astype(low)
    slope_s = share_s * (1.0 + pre_s * (1.0 - share_s))
    maps_in, maps_out = shared[:, :NS], shared[:, NS:]
    maps_out_t = jnp.transpose(maps_out.astype(jnp.float32)).astype(low)
    shifted, rates, decay, cumulated = step_parts(s_ref[:, 2 * NS :], table, heads)
    cum_rows[...] = jnp.transpose(cumulated)[: cum_rows.shape[0]]
    spread_columns(cumulated, cum_wide, heads)
    spread_columns(rates, rate_wide, heads)
    crossing = dot32(maps_in, maps_out, NT)
    for held in (cross_grad, maps_grad, column_sum, outer_sum, rate_sum, last_sum):
        held[...] = jnp.zeros_like(held)

    def pair(index, _):
        lanes = pl.ds(pl.multiple_of(index * LANES, LANES), LANES)
        pre = filtered(window, tx, lanes)
        share = jax.nn.sigmoid(pre)
        values = (pre * share).astype(low)
        slope = share * (1.0 + pre * (1.0 - share))
        lane = lax.broadcasted_iota(jnp.int32, (BLK, LANES), 1)
        side = lane < P_SIZE
        upper = triangle(True)
        cum_pair = jnp.where(side, cum_wide[2 * index], cum_wide[2 * index + 1])
        rate_pair = jnp.where(side, rate_wide[2 * index], rate_wide[2 * index + 1])
        back = ybar[:, lanes]
        back_low = back.astype(low)
        wide = values.astype(jnp.float32)
        now = entered[0, :, lanes]
        now_low = now.astype(low)
        after = state_grad[:, lanes]
        after_low = after.astype(low)
        grown = jnp.exp(cum_pair)
        last = cum_pair[BLK - 1 : BLK, :]
        total_decay = jnp.exp(last)
        ending = jnp.exp(last - cum_pair) * rate_pair
        outer = dot32(maps_out, now_low)
        inward = dot32(maps_in, after_low)
        back_grown = back * grown
        back_grown_low = back_grown.astype(low)
        maps_grad[:, NS:] += dot32(back_grown_low, now_low, NT)
        maps_grad[:, :NS] += dot32((wide * ending).astype(low), after_low, NT)
        state_grad[:, lanes] = total_decay * after + dot32(maps_out_t, back_grown_low)
        grad = ending * inward + tx[6:7, lanes] * back
        pick = (
            lax.broadcasted_iota(jnp.int32, (LANES, LANES), 1)
            == 2 * index + (lax.broadcasted_iota(jnp.int32, (LANES, LANES), 0) >= P_SIZE).astype(jnp.int32)
        ).astype(low)

        def to_heads(value):
            high = value.astype(low)
            rest = (value - high.astype(jnp.float32)).astype(low)
            return dot32(high, pick) + dot32(rest, pick)

        outer_sum[...] += to_heads(back_grown * outer)
        rate_sum[...] += to_heads(wide * inward)
        kept = jnp.sum(total_decay * after * now, axis=0, keepdims=True)
        last_sum[...] += to_heads(jnp.broadcast_to(kept, (8, LANES)))
        tx_grad[6:7, lanes] += jnp.sum(back * wide, axis=0, keepdims=True)
        zero = jnp.zeros_like(values)
        for half in range(2):
            head = 2 * index + half
            own = side if half == 0 else jnp.logical_not(side)
            column = cum_wide[head]
            rate = rate_wide[head]
            spread = cum_rows[pl.ds(head, 1), :] - jnp.concatenate([column, column], axis=1)
            decays = jnp.exp(jnp.where(upper, spread, FAR))
            weighted = decays * jnp.concatenate([rate, rate], axis=1)
            products = dot32(jnp.where(own, values, zero), back_low, NT)
            summed = jnp.sum(products * (crossing * decays), axis=1, keepdims=True)
            column_sum[...] += jnp.where(lane == head, summed, 0.0)
            mixing = crossing * weighted
            z_rows[pl.ds(head, 1), :] = jnp.sum(products * mixing, axis=0, keepdims=True)
            cross_grad[...] += products * weighted
            grad = grad + dot32(mixing.astype(low), jnp.where(own, back_low, zero))
        back_pre = grad * slope
        ahead[0:BLK, lanes] = back_pre
        spent = tx[KC - 1 : KC, lanes] * back_pre
        for offset in range(1, KC):
            spent = spent + tx[KC - 1 - offset : KC - offset, lanes] * ahead[offset : offset + BLK, lanes]
        inner_low[:, lanes] = spent.astype(low)
        for position in range(KC):
            tx_grad[position : position + 1, lanes] += jnp.sum(
                back_pre * window[5 + position : 5 + position + BLK, lanes], axis=0, keepdims=True
            )
        tx_grad[KC : KC + 1, lanes] += jnp.sum(back_pre, axis=0, keepdims=True)
        return 0

    lax.fori_loop(0, heads // 2, pair, 0)
    cross = cross_grad[...]
    cross_low = cross.astype(low)
    maps_grad[:, :NS] += dot32(cross_low, maps_out)
    maps_grad[:, NS:] += dot32(jnp.transpose(cross).astype(low), maps_in)
    back_pre_s = maps_grad[...] * slope_s
    ahead_s[0:BLK, :] = back_pre_s
    spent_s = ts[KC - 1 : KC, :] * back_pre_s
    for offset in range(1, KC):
        spent_s = spent_s + ts[KC - 1 - offset : KC - offset, :] * ahead_s[offset : offset + BLK, :]
    small_low[:, : 2 * NS] = spent_s.astype(low)
    for position in range(KC):
        ts_grad[position : position + 1, :] += jnp.sum(
            back_pre_s * window_s[5 + position : 5 + position + BLK, :], axis=0, keepdims=True
        )
    ts_grad[KC : KC + 1, :] += jnp.sum(back_pre_s, axis=0, keepdims=True)
    lane = lax.broadcasted_iota(jnp.int32, (BLK, LANES), 1)
    falling = jnp.exp(cumulated[BLK - 1 : BLK, :] - cumulated)
    ended = rate_sum[...] * falling
    ended_rate = ended * rates
    own_sum = column_sum[...]
    cum_grad = jnp.transpose(z_rows[...]) + outer_sum[...] - rates * own_sum - ended_rate
    final = last_sum[0:1, :] + jnp.sum(ended_rate, axis=0, keepdims=True)
    place = lax.broadcasted_iota(jnp.int32, (BLK, LANES), 0)
    cum_grad = cum_grad + jnp.where(place == BLK - 1, final, 0.0)
    log_grad = jnp.dot(
        triangle(True).astype(jnp.float32),
        cum_grad,
        precision=HIGHEST,
        preferred_element_type=jnp.float32,
    )
    rate_grad = own_sum + ended + decay * log_grad
    raw_grad = jnp.where(lane < heads, rate_grad * jax.nn.sigmoid(shifted), 0.0)
    small_low[:, 2 * NS :] = raw_grad.astype(low)
    table_grad[0:1, :] += jnp.sum(raw_grad, axis=0, keepdims=True)
    table_grad[1:2, :] += decay * jnp.sum(rates * log_grad, axis=0, keepdims=True)

    @pl.when(opened)
    def _():
        ahead[BLK : BLK + 8, :] = jnp.zeros_like(ahead[BLK : BLK + 8, :])
        ahead_s[BLK : BLK + 8, :] = jnp.zeros_like(ahead_s[BLK : BLK + 8, :])
        state_grad[...] = jnp.zeros_like(state_grad)

    @pl.when(jnp.logical_not(opened))
    def _():
        ahead[BLK : BLK + 8, :] = ahead[0:8, :]
        ahead_s[BLK : BLK + 8, :] = ahead_s[0:8, :]


VMEM_LIMIT = 56 * 1024 * 1024


def mixer(opens, widths, inner, small, tx, ts, table, interpret=False):
    tokens, channels = inner.shape
    heads, count = channels // P_SIZE, tokens // BLK
    whole = lambda rows, columns: pl.BlockSpec((rows, columns), lambda i, *_: (0, 0))
    rows = lambda columns: pl.BlockSpec((BLK, columns), lambda i, *_: (i, 0))
    wide = pltpu.VMEM((heads, BLK, LANES), jnp.float32)
    row_pad = -(-heads // 8) * 8
    return pl.pallas_call(
        functools.partial(mixer_kernel, heads),
        out_shape=(
            jax.ShapeDtypeStruct((tokens, channels), jnp.float32),
            jax.ShapeDtypeStruct((count, NS, channels), jnp.float32),
        ),
        grid_spec=pltpu.PrefetchScalarGridSpec(
            num_scalar_prefetch=2,
            grid=(count,),
            in_specs=[rows(channels), rows(3 * LANES), whole(8, channels), whole(8, 2 * NS), whole(8, LANES)],
            out_specs=[rows(channels), pl.BlockSpec((1, NS, channels), lambda i, *_: (i, 0, 0))],
            scratch_shapes=[
                pltpu.VMEM((BLK + 8, channels), jnp.float32),
                pltpu.VMEM((BLK + 8, 2 * NS), jnp.float32),
                pltpu.VMEM((NS, channels), jnp.float32),
                pltpu.VMEM((8, LANES), jnp.bfloat16),
                wide,
                wide,
                pltpu.VMEM((row_pad, BLK), jnp.float32),
                pltpu.VMEM((row_pad, BLK), jnp.float32),
            ],
        ),
        compiler_params=pltpu.CompilerParams(vmem_limit_bytes=VMEM_LIMIT),
        cost_estimate=lasting(25),
        name="mixer",
        interpret=interpret,
    )(opens, widths, inner, small, tx, ts, table)


def mixer_back(opens, inner, small, tx, ts, table, ybar, entered, interpret=False):
    tokens, channels = inner.shape
    heads, count = channels // P_SIZE, tokens // BLK
    per = BLK // 8
    turn = lambda i: count - 1 - i
    whole = lambda rows, columns: pl.BlockSpec((rows, columns), lambda i, *_: (0, 0))
    rows = lambda columns: pl.BlockSpec((BLK, columns), lambda i, *_: (turn(i), 0))
    tail = lambda columns: pl.BlockSpec(
        (8, columns), lambda i, *_: (jnp.maximum(turn(i) * per - 1, 0), 0)
    )
    wide = pltpu.VMEM((heads, BLK, LANES), jnp.float32)
    row_pad = -(-heads // 8) * 8
    column = pltpu.VMEM((BLK, LANES), jnp.float32)
    return pl.pallas_call(
        functools.partial(mixer_back_kernel, heads, count),
        out_shape=(
            jax.ShapeDtypeStruct((tokens, channels), jnp.bfloat16),
            jax.ShapeDtypeStruct((tokens, 3 * LANES), jnp.bfloat16),
            jax.ShapeDtypeStruct((8, channels), jnp.float32),
            jax.ShapeDtypeStruct((8, 2 * NS), jnp.float32),
            jax.ShapeDtypeStruct((8, LANES), jnp.float32),
        ),
        grid_spec=pltpu.PrefetchScalarGridSpec(
            num_scalar_prefetch=1,
            grid=(count,),
            in_specs=[
                rows(channels),
                tail(channels),
                rows(3 * LANES),
                tail(3 * LANES),
                whole(8, channels),
                whole(8, 2 * NS),
                whole(8, LANES),
                rows(channels),
                pl.BlockSpec((1, NS, channels), lambda i, *_: (turn(i), 0, 0)),
            ],
            out_specs=[rows(channels), rows(3 * LANES), whole(8, channels), whole(8, 2 * NS), whole(8, LANES)],
            scratch_shapes=[
                pltpu.VMEM((BLK + 8, channels), jnp.float32),
                pltpu.VMEM((BLK + 8, 2 * NS), jnp.float32),
                pltpu.VMEM((BLK + 8, channels), jnp.float32),
                pltpu.VMEM((BLK + 8, 2 * NS), jnp.float32),
                pltpu.VMEM((NS, channels), jnp.float32),
                wide,
                wide,
                pltpu.VMEM((row_pad, BLK), jnp.float32),
                pltpu.VMEM((LANES, BLK), jnp.float32),
                pltpu.VMEM((BLK, BLK), jnp.float32),
                pltpu.VMEM((BLK, 2 * NS), jnp.float32),
                column,
                column,
                column,
                pltpu.VMEM((8, LANES), jnp.float32),
            ],
        ),
        compiler_params=pltpu.CompilerParams(vmem_limit_bytes=VMEM_LIMIT),
        cost_estimate=lasting(43),
        name="mixer_back",
        interpret=interpret,
    )(opens, inner, inner, small, small, tx, ts, table, ybar, entered)


def advance_inner_kernel(rate, count, weight, moment, average, *refs):
    parts, outs = refs[:-3], refs[-3:]

    def total(some):
        return sum(x[...].astype(jnp.float32) for x in some)

    for k, gradient in enumerate((total(parts[:count]), total(parts[count:]))):
        news = advance(weight[:, k, :], gradient, moment[:, k, :], average[:, k, :], rate)
        for out, new in zip(outs, news):
            out[:, k, :] = new


def advance_inner(weight, moment, average, gate, inner, rate):
    rows, two, columns = weight.shape
    count = len(gate)
    tile = min(rows, 64)
    pair = pl.BlockSpec((tile, two, columns), lambda i: (i, 0, 0))
    flat = lambda n: pl.BlockSpec((tile, n), lambda i: (i, 0))
    return pl.pallas_call(
        functools.partial(advance_inner_kernel, rate, count),
        out_shape=(jax.ShapeDtypeStruct(weight.shape, weight.dtype),) * 3,
        grid=(rows // tile,),
        in_specs=[pair] * 3 + [flat(columns)] * (count + len(inner)),
        out_specs=[pair] * 3,
        compiler_params=pltpu.CompilerParams(vmem_limit_bytes=VMEM_LIMIT),
        cost_estimate=lasting(8),
        name="advance_inner",
    )(weight, moment, average, *gate, *inner)


def swap_pairs(size):
    return [(i, i ^ 1) for i in range(size)]


def after(value, *earlier):
    return lax.optimization_barrier((value, *earlier))[0]


def place_kernel(count, slots, *refs):
    pieces, out = refs[:count], refs[count]
    step = pl.program_id(0)
    for i in range(count):

        @pl.when(step == i)
        def _(i=i):
            out[...] = pieces[i][...]


def place(pieces, slots, shape=None):
    count = len(pieces)
    pieces = [x if isinstance(x, tuple) else (x, 0) for x in pieces]
    shape = shape or pieces[0][0].shape
    return pl.pallas_call(
        functools.partial(place_kernel, count),
        out_shape=jax.ShapeDtypeStruct((shape[0] * count, *shape[1:]), pieces[0][0].dtype),
        grid_spec=pltpu.PrefetchScalarGridSpec(
            num_scalar_prefetch=1,
            grid=(count,),
            in_specs=[pl.BlockSpec(shape, lambda i, slots, at=at: (at, 0)) for _, at in pieces],
            out_specs=pl.BlockSpec(shape, lambda i, slots: (slots[i], 0)),
        ),
        compiler_params=pltpu.CompilerParams(vmem_limit_bytes=VMEM_LIMIT),
        cost_estimate=lasting(4),
        name="place",
    )(jnp.stack(slots).astype(jnp.int32), *[x for x, _ in pieces])


def my_column():
    return lax.axis_index("dp") % Y_SIZE


def split_own(value, axis):
    count = lax.axis_size("dp")
    shape = value.shape
    wide = value.reshape(
        *shape[:axis], count // Y_SIZE, Y_SIZE, shape[axis] // count, *shape[axis + 1 :]
    )
    halves = [
        lax.index_in_dim(wide, i, axis + 1, keepdims=False).reshape(
            *shape[:axis], shape[axis] // Y_SIZE, *shape[axis + 1 :]
        )
        for i in range(Y_SIZE)
    ]
    first = my_column() == 0
    return jnp.where(first, halves[0], halves[1]), jnp.where(first, halves[1], halves[0])


def join_own(own, other, axis, width):
    first = my_column() == 0
    shape = own.shape
    halves = [
        x.reshape(*shape[:axis], shape[axis] // width, 1, width, *shape[axis + 1 :])
        for x in (jnp.where(first, own, other), jnp.where(first, other, own))
    ]
    return jnp.concatenate(halves, axis=axis + 1).reshape(
        *shape[:axis], shape[axis] * Y_SIZE, *shape[axis + 1 :]
    )


def halves_kernel(piece, column, x, own, other):
    value = x[...]
    first = column[0] == 0
    for row in range(value.shape[1] // piece // Y_SIZE):
        at = row * Y_SIZE * piece
        low, high = value[:, at : at + piece], value[:, at + piece : at + 2 * piece]
        own[:, row * piece : (row + 1) * piece] = jnp.where(first, low, high)
        other[:, row * piece : (row + 1) * piece] = jnp.where(first, high, low)


def split_columns(value):
    tokens, width = value.shape
    piece = width // lax.axis_size("dp")
    if piece % LANES:
        return split_own(value, 1)
    half = jax.ShapeDtypeStruct((tokens, width // Y_SIZE), value.dtype)
    rows = lambda columns: pl.BlockSpec((BLK, columns), lambda i, *_: (i, 0))
    return pl.pallas_call(
        functools.partial(halves_kernel, piece),
        out_shape=(half, half),
        grid_spec=pltpu.PrefetchScalarGridSpec(
            num_scalar_prefetch=1,
            grid=(tokens // BLK,),
            in_specs=[rows(width)],
            out_specs=[rows(width // Y_SIZE)] * 2,
        ),
        cost_estimate=lasting(5),
        name="halves",
    )(my_column().astype(jnp.int32)[None], value)


def columns_kernel(slots, *refs):
    pieces, own, other = refs[:-2], refs[-2], refs[-1]
    first = slots[len(pieces)] == 0
    half = own.shape[1]
    for i, piece in enumerate(pieces):

        @pl.when(pl.program_id(0) == i)
        def _(piece=piece):
            low, high = piece[:, :half], piece[:, half:]
            own[...] = jnp.where(first, low, high)
            other[...] = jnp.where(first, high, low)


def gather_columns(piece):
    tokens, width = piece.shape
    count = lax.axis_size("head")
    if not aligned(width * count // Y_SIZE):
        return split_columns(lax.all_gather(piece, "head", axis=1, tiled=True))
    index = lax.axis_index("head")
    far = lax.ppermute(piece, "head", [(i, i ^ 2) for i in range(count)])
    near = lax.ppermute(piece, "head", swap_pairs(count))
    last = lax.ppermute(far, "head", swap_pairs(count))
    slots = jnp.stack([index, index ^ 1, index ^ 2, index ^ 3, my_column()]).astype(jnp.int32)
    half = jax.ShapeDtypeStruct((tokens, width * count // Y_SIZE), piece.dtype)
    return pl.pallas_call(
        columns_kernel,
        out_shape=(half, half),
        grid_spec=pltpu.PrefetchScalarGridSpec(
            num_scalar_prefetch=1,
            grid=(count,),
            in_specs=[pl.BlockSpec(piece.shape, lambda i, slots: (0, 0))] * count,
            out_specs=[pl.BlockSpec((tokens, width // Y_SIZE), lambda i, slots: (0, slots[i]))] * 2,
        ),
        compiler_params=pltpu.CompilerParams(vmem_limit_bytes=VMEM_LIMIT),
        cost_estimate=lasting(5),
        name="columns",
    )(slots, piece, near, far, last)


def rows_phase(shard):
    count = lax.axis_size("dp")
    held = [shard]
    for shift in range(1, count // Y_SIZE):
        perm = [(i, (i + shift * Y_SIZE) % count) for i in range(count)]
        held.append(lax.ppermute(shard, "dp", perm))
    return held


def begin_gather(shard):
    if lax.axis_size("dp") != 8:
        return [shard]
    return rows_phase(shard)


def end_gather(held, *later):
    if lax.axis_size("dp") != 8:
        return split_own(lax.all_gather(held[0], "dp", axis=0, tiled=True), 0)
    if later:
        held = list(lax.optimization_barrier((*held, *later))[: len(held)])
    row = lax.axis_index("dp") // Y_SIZE
    own = place(held, [(row - i) % len(held) for i in range(len(held))])
    return own, lax.ppermute(own, "dp", swap_pairs(8))


def begin_reduce(kept, away):
    count = lax.axis_size("dp")
    if count != 8:
        return kept, away
    return kept, lax.ppermute(away, "dp", swap_pairs(count))


def fold_pairs(begun, axis=0):
    kept, came = begun
    count = lax.axis_size("dp")
    if count != 8:
        width = kept.shape[axis] // (count // Y_SIZE)
        return None, join_own(kept.astype(came.dtype), came, axis, width)
    shape = kept.shape
    wide = (*shape[:axis], 2, 2, shape[axis] // 4, *shape[axis + 1 :])
    bit = (lax.axis_index("dp") // Y_SIZE) % 2

    def pick(which):
        first, second = (
            lax.dynamic_index_in_dim(x.reshape(wide), which, axis + 1, keepdims=False)
            for x in (kept, came)
        )
        return first + second.astype(jnp.float32)

    return pick(bit), pick(1 - bit).astype(came.dtype)


def swap_low(fold):
    kept, away = fold
    if kept is None:
        return fold
    return kept, lax.ppermute(away, "dp", [(i, i ^ Y_SIZE) for i in range(8)])


def fold_low(swapped, axis=0):
    kept, came = swapped
    if kept is None:
        return None, lax.psum_scatter(came, "dp", scatter_dimension=axis, tiled=True)
    bit = lax.axis_index("dp") // Y_SIZE // 2

    def pick(which):
        first, second = (
            lax.dynamic_index_in_dim(x, which, axis, keepdims=False) for x in (kept, came)
        )
        return first + second.astype(jnp.float32)

    return pick(bit), pick(1 - bit).astype(came.dtype)


def swap_high(fold):
    kept, away = fold
    if kept is None:
        return [away]
    return [kept, lax.ppermute(away, "dp", [(i, i ^ (2 * Y_SIZE)) for i in range(8)])]


def add_parts(parts):
    return sum(x.astype(jnp.float32) for x in parts)


def reduce_head(value):
    count = lax.axis_size("head")
    low = jnp.bfloat16
    if count != 4:
        return lax.psum_scatter(value, "head", scatter_dimension=0, tiled=False)
    index = lax.axis_index("head")
    side, core = index // 2, index % 2
    both = value.reshape(2, 2, *value.shape[1:])
    away = lax.dynamic_index_in_dim(both, 1 - core, 1, keepdims=False)
    kept = lax.dynamic_index_in_dim(both, core, 1, keepdims=False)
    came = lax.ppermute(away.astype(low), "head", swap_pairs(count))
    pair = kept + came.astype(jnp.float32)
    away = lax.dynamic_index_in_dim(pair, 1 - side, 0, keepdims=False)
    kept = lax.dynamic_index_in_dim(pair, side, 0, keepdims=False)
    came = lax.ppermute(away.astype(low), "head", [(i, (i + 2) % 4) for i in range(count)])
    return kept + came.astype(jnp.float32)


def gather_head(piece):
    count = lax.axis_size("head")
    if count != 4:
        return lax.all_gather(piece, "head", axis=0, tiled=True)
    index = lax.axis_index("head")
    far = lax.ppermute(piece, "head", [(i, (i + 2) % 4) for i in range(count)])
    near = lax.ppermute(piece, "head", swap_pairs(count))
    last = lax.ppermute(far, "head", swap_pairs(count))
    across = (index + 2) % 4
    return place([piece, near, far, last], [index, index ^ 1, across, across ^ 1])


LASTING = {
    "norm": 6,
    "project": 8,
    "gate": 10,
    "scale": 6,
    "weight": 8,
    "whole_weight": 11,
    "output_back": 11,
    "norm_back": 10,
    "output": 9,
    "input_back": 20,
}


def call(kernel, name, grid, scalars, args, in_specs, outs, out_specs):
    return pl.pallas_call(
        kernel,
        out_shape=outs,
        grid_spec=pltpu.PrefetchScalarGridSpec(
            num_scalar_prefetch=len(scalars), grid=grid, in_specs=in_specs, out_specs=out_specs
        ),
        compiler_params=pltpu.CompilerParams(vmem_limit_bytes=VMEM_LIMIT),
        cost_estimate=lasting(LASTING[name]),
        name=name,
    )(*scalars, *args)


def rows_of(columns):
    return pl.BlockSpec((BLK, columns), lambda i, *_: (i, 0))


def line_of():
    return pl.BlockSpec((1, BLK), lambda i, *_: (0, i))


def fixed(array):
    return pl.BlockSpec(array.shape, lambda i, *_: (0, 0))


def held_once(array):
    return pl.BlockSpec(array.shape, lambda i, *_: (0, 0), pipeline_mode=pl.Buffered(1))


def typed(kind, *shape):
    return jax.ShapeDtypeStruct(shape, kind)


def to_column(line, columns):
    column = jnp.transpose(jnp.broadcast_to(line, (LANES, BLK)))
    return jnp.concatenate([column] * (columns // LANES), axis=1)


def to_line(value):
    part = value[:, :LANES]
    for at in range(LANES, value.shape[1], LANES):
        part = part + value[:, at : at + LANES]
    return jnp.sum(jnp.transpose(part), axis=0, keepdims=True)


def halves_of(value, piece, first):
    starts = range(0, value.shape[1], Y_SIZE * piece)
    low = jnp.concatenate([value[:, s : s + piece] for s in starts], axis=1)
    high = jnp.concatenate([value[:, s + piece : s + 2 * piece] for s in starts], axis=1)
    return jnp.where(first, low, high), jnp.where(first, high, low)


def norm_kernel(own_in, other_in, gains, own, other, inverse):
    xs = [x[...].astype(jnp.float32) for x in (own_in, other_in)]
    width = xs[0].shape[1]
    sums = to_line(xs[0] * xs[0] + xs[1] * xs[1])
    scale = lax.rsqrt(sums / (2 * width) + EPS)
    inverse[...] = scale
    column = to_column(scale, width)
    for i, (x, out) in enumerate(zip(xs, (own, other))):
        out[...] = (x * column * gains[i : i + 1, :]).astype(jnp.bfloat16)


def norm(xs, gains):
    tokens, width = xs[0].shape
    half = typed(jnp.bfloat16, tokens, width)
    own, other, inverse = call(
        norm_kernel,
        "norm",
        (tokens // BLK,),
        (),
        (*xs, gains),
        [rows_of(width)] * 2 + [fixed(gains)],
        (half, half, typed(jnp.float32, 1, tokens)),
        [rows_of(width)] * 2 + [line_of()],
    )
    return [own, other], inverse


def project_kernel(own, other, w_own, w_other, out):
    out[...] = dot32(own[...], w_own[...]) + dot32(other[...], w_other[...])


def project(halves, weights):
    tokens, width = halves[0].shape
    columns = weights[0].shape[1]
    return call(
        project_kernel,
        "project",
        (tokens // BLK,),
        (),
        (*halves, *weights),
        [rows_of(width)] * 2 + [held_once(w) for w in weights],
        typed(jnp.float32, tokens, columns),
        rows_of(columns),
    )


def gate_kernel(own, other, w_own, w_other, mixed, gate, squares):
    value = dot32(own[...], w_own[...]) + dot32(other[...], w_other[...])
    gate[...] = value
    gated = mixed[...] * (value * jax.nn.sigmoid(value))
    squares[...] = to_line(gated * gated)


def gate_project(halves, weights, mixed):
    tokens, width = halves[0].shape
    columns = mixed.shape[1]
    return call(
        gate_kernel,
        "gate",
        (tokens // BLK,),
        (),
        (*halves, *weights, mixed),
        [rows_of(width)] * 2 + [held_once(w) for w in weights] + [rows_of(columns)],
        (typed(jnp.float32, tokens, columns), typed(jnp.float32, 1, tokens)),
        [rows_of(columns), line_of()],
    )


def scale_kernel(mixed, gate, scale, gain, out):
    value = gate[...]
    gated = mixed[...] * (value * jax.nn.sigmoid(value))
    column = to_column(scale[...], value.shape[1])
    out[...] = (gated * column * gain[...]).astype(jnp.bfloat16)


def scale_gated(mixed, gate, scale, gain):
    tokens, columns = mixed.shape
    return call(
        scale_kernel,
        "scale",
        (tokens // BLK,),
        (),
        (mixed, gate, scale, gain),
        [rows_of(columns)] * 2 + [line_of(), fixed(gain)],
        typed(jnp.bfloat16, tokens, columns),
        rows_of(columns),
    )


def weight_kernel(own, other, back, kept, away):
    kept[...] = dot32(own[...], back[...], TN)
    away[...] = dot32(other[...], back[...], TN).astype(jnp.bfloat16)


def weight_grad(halves, back):
    tokens, width = halves[0].shape
    columns = back.shape[1]
    strip = pl.BlockSpec((tokens, BLK), lambda i, *_: (0, i))
    return call(
        weight_kernel,
        "weight",
        (width // BLK,),
        (),
        (*halves, back),
        [strip] * 2 + [held_once(back)],
        (typed(jnp.float32, width, columns), typed(jnp.bfloat16, width, columns)),
        [rows_of(columns)] * 2,
    )


def whole_weight_kernel(column, own, other, back, out):
    mine = pl.program_id(1) == 0

    @pl.when(mine)
    def _():
        out[...] = dot32(own[...], back[...], TN).astype(jnp.bfloat16)

    @pl.when(jnp.logical_not(mine))
    def _():
        out[...] = dot32(other[...], back[...], TN).astype(jnp.bfloat16)


def whole_weight_grad(halves, back):
    tokens, width = halves[0].shape
    columns = back.shape[1]
    piece = Y_SIZE * width // lax.axis_size("dp")
    if piece % LANES:
        kept, away = weight_grad(halves, back)
        return join_own(kept.astype(away.dtype), away, 0, piece)
    strip = pl.BlockSpec((tokens, piece), lambda i, j, *_: (0, i))
    spot = lambda i, j, column: (Y_SIZE * i + (column[0] + j) % Y_SIZE, 0)
    return call(
        whole_weight_kernel,
        "whole_weight",
        (width // piece, Y_SIZE),
        (my_column().astype(jnp.int32)[None],),
        (*halves, back),
        [strip] * 2
        + [pl.BlockSpec(back.shape, lambda i, j, *_: (0, 0), pipeline_mode=pl.Buffered(1))],
        typed(jnp.bfloat16, Y_SIZE * width, columns),
        pl.BlockSpec((piece, columns), spot),
    )


def store_heads(out, column, own, other):
    first = column[0] == 0
    low = jnp.where(first, own, other).astype(out.dtype)
    high = jnp.where(first, other, own).astype(out.dtype)
    half = out.shape[2] // Y_SIZE
    for head in range(out.shape[0]):
        part = slice(head * half, (head + 1) * half)
        out[head, :, :half] = low[:, part]
        out[head, :, half:] = high[:, part]


def heads_out(tokens, width):
    count = lax.axis_size("head")
    columns = Y_SIZE * width // count
    shape = typed(jnp.bfloat16, count, tokens, columns)
    return shape, pl.BlockSpec((count, BLK, columns), lambda i, *_: (0, i, 0))


def aligned(width):
    count = lax.axis_size("dp")
    return count == Y_SIZE * lax.axis_size("head") and Y_SIZE * width // count % LANES == 0


def begin_heads(value):
    if isinstance(value, tuple):
        step = Y_SIZE * value[0].shape[1] // lax.axis_size("dp")
        return None, join_own(*value, 1, step)
    core = lax.axis_index("head") % 2
    both = value.reshape(2, 2, *value.shape[1:])
    away = lax.dynamic_index_in_dim(both, 1 - core, 1, keepdims=False)
    kept = lax.dynamic_index_in_dim(both, core, 1, keepdims=False)
    return kept, lax.ppermute(away, "head", swap_pairs(4))


def fold_heads(begun):
    kept, near = begun
    if kept is None:
        return [lax.psum_scatter(near, "head", scatter_dimension=1, tiled=True)]
    side = lax.axis_index("head") // 2
    parts = [
        lax.dynamic_index_in_dim(kept, which, 0, keepdims=False).astype(jnp.float32)
        + lax.dynamic_index_in_dim(near, which, 0, keepdims=False)
        for which in (side, 1 - side)
    ]
    away = parts[1].astype(near.dtype)
    return [away, parts[0], lax.ppermute(away, "head", [(i, i ^ 2) for i in range(4)])]


def end_heads(folded):
    return sum(x.astype(jnp.float32) for x in folded[-2:])


def output_back_kernel(own, other, w_own, w_other, mixed, gate, gain, grad, dots):
    value = dot32(own[...], w_own[...]) + dot32(other[...], w_other[...])
    grad[...] = value
    raw = gate[...]
    gated = mixed[...] * (raw * jax.nn.sigmoid(raw))
    dots[...] = to_line(value * gain[...] * gated)


def output_back(halves, weights, mixed, gate, gain):
    tokens, width = halves[0].shape
    columns = mixed.shape[1]
    return call(
        output_back_kernel,
        "output_back",
        (tokens // BLK,),
        (),
        (*halves, *weights, mixed, gate, gain),
        [rows_of(width)] * 2
        + [held_once(w) for w in weights]
        + [rows_of(columns)] * 2
        + [fixed(gain)],
        (typed(jnp.float32, tokens, columns), typed(jnp.float32, 1, tokens)),
        [rows_of(columns), line_of()],
    )


def norm_back_kernel(heads, widths, grad, mixed, gate, gain, scale, scale_back, ybar, gate_low, gain_grad):
    block = pl.program_id(0)
    columns = grad.shape[1]
    raw = gate[...]
    share = jax.nn.sigmoid(raw)
    silu = raw * share
    value, state = grad[...], mixed[...]
    gated = state * silu
    column = to_column(scale[...], columns)
    back = value * gain[...] * column - gated * to_column(scale_back[...], columns)
    lane = lax.broadcasted_iota(jnp.int32, (1, columns), 1)
    used = ((lane // P_SIZE) * H < widths[block] * heads).astype(jnp.float32)
    ybar[...] = back * silu * used
    gate_low[...] = (back * state * (share * (1.0 + raw * (1.0 - share)))).astype(jnp.bfloat16)

    @pl.when(block == 0)
    def _():
        gain_grad[...] = jnp.zeros_like(gain_grad)

    gain_grad[...] += jnp.sum(value * gated * column, axis=0, keepdims=True)


def norm_back(widths, grad, mixed, gate, gain, scale, scale_back):
    tokens, columns = grad.shape
    return call(
        functools.partial(norm_back_kernel, columns // P_SIZE),
        "norm_back",
        (tokens // BLK,),
        (widths,),
        (grad, mixed, gate, gain, scale, scale_back),
        [rows_of(columns)] * 3 + [fixed(gain), line_of(), line_of()],
        (
            typed(jnp.float32, tokens, columns),
            typed(jnp.bfloat16, tokens, columns),
            typed(jnp.float32, 1, columns),
        ),
        [rows_of(columns)] * 2 + [pl.BlockSpec((1, columns), lambda i, *_: (0, 0))],
    )


def output_kernel(column, value, w_own, w_other, *outs):
    own, other = (dot32(value[...], w[...], NT) for w in (w_own, w_other))
    if len(outs) == 1:
        store_heads(outs[0], column, own, other)
    else:
        outs[0][...], outs[1][...] = own.astype(jnp.bfloat16), other.astype(jnp.bfloat16)


def output_project(value, weights):
    tokens, columns = value.shape
    width = weights[0].shape[0]
    half = typed(jnp.bfloat16, tokens, width)
    outs, out_specs = (half, half), [rows_of(width)] * 2
    if aligned(width):
        outs, out_specs = heads_out(tokens, width)
    return call(
        output_kernel,
        "output",
        (tokens // BLK,),
        (my_column().astype(jnp.int32)[None],),
        (value, *weights),
        [rows_of(columns)] + [held_once(w) for w in weights],
        outs,
        out_specs,
    )


def input_back_kernel(column, gate, inner, small, xo, xt, gains, inverse, *refs):
    weights, outs, line, sums = refs[:6], refs[6:-2], refs[-2], refs[-1]
    block = pl.program_id(0)
    scale = to_column(inverse[...], xo.shape[1])

    @pl.when(block == 0)
    def _():
        sums[...] = jnp.zeros_like(sums)

    total, values = None, []
    for i, x in enumerate((xo, xt)):
        value = (
            dot32(gate[...], weights[i][...], NT)
            + dot32(inner[...], weights[2 + i][...], NT)
            + dot32(small[...], weights[4 + i][...], NT)
        )
        values.append(value)
        product = value * x[...].astype(jnp.float32)
        sums[i : i + 1, :] += jnp.sum(product * scale, axis=0, keepdims=True)
        row = product * gains[i : i + 1, :]
        total = row if total is None else total + row
    line[...] = to_line(total)
    if len(outs) == 1:
        store_heads(outs[0], column, *values)
    else:
        outs[0][...], outs[1][...] = (v.astype(jnp.bfloat16) for v in values)


def input_back(backs, xs, gains, inverse, weights):
    tokens, width = xs[0].shape
    half = typed(jnp.bfloat16, tokens, width)
    outs, out_specs = [half, half], [rows_of(width)] * 2
    if aligned(width):
        outs, out_specs = [[x] for x in heads_out(tokens, width)]
    *grads, line, sums = call(
        input_back_kernel,
        "input_back",
        (tokens // BLK,),
        (my_column().astype(jnp.int32)[None],),
        (*backs, *xs, gains, inverse, *weights),
        [rows_of(b.shape[1]) for b in backs]
        + [rows_of(width)] * 2
        + [fixed(gains), line_of()]
        + [held_once(w) for w in weights],
        (*outs, typed(jnp.float32, 1, tokens), typed(jnp.float32, 2, width)),
        [*out_specs, line_of(), pl.BlockSpec((2, width), lambda i, *_: (0, 0))],
    )
    return grads[0] if len(grads) == 1 else tuple(grads), line, sums


def body(
    inputs,
    cotangent,
    token_valid,
    block_opens,
    block_widths,
    weight_inner,
    weight_step,
    weight_output,
    weight_state,
    norm_gain,
    channel_table,
    head_table,
    state_filter,
    momentum_inner,
    momentum_step,
    momentum_output,
    momentum_state,
    momentum_gain,
    momentum_channel,
    momentum_head,
    momentum_filter,
    average_inner,
    average_step,
    average_output,
    average_state,
    average_gain,
    average_channel,
    average_head,
    average_filter,
):
    low = jnp.bfloat16
    full_type = jnp.float32
    count_dp = lax.axis_size("dp")
    count_head = lax.axis_size("head")
    rows_dp, piece = count_dp // Y_SIZE, weight_inner.shape[0]
    tokens, channels = inputs.shape[0], weight_inner.shape[2]
    heads_own = weight_step.shape[1]
    rows_all, state_rows = weight_state.shape[0], state_filter.shape[0]
    width_state = weight_state.shape[1]
    filter_block = jnp.pad(state_filter.astype(low), ((0, rows_all - state_rows), (0, 0)))
    small_piece = jnp.concatenate(
        [
            weight_state.astype(low),
            weight_step.astype(low).reshape(rows_all, -1),
            norm_gain.astype(low)[:, None],
            filter_block,
        ],
        axis=1,
    )
    small_piece = jnp.pad(small_piece, ((0, 0), (0, -small_piece.shape[1] % LANES)))
    small_all = lax.all_gather(
        small_piece, ("dp", "head"), axis=0, tiled=False
    ).reshape(count_dp, count_head, rows_all, -1)
    step_size = rows_all * count_head * heads_own // rows_all
    step_full = lax.dynamic_index_in_dim(small_all, lax.axis_index("head"), 1, keepdims=False)
    step_full = step_full[:, :, width_state : width_state + step_size].reshape(D, heads_own)
    extra = small_all[:, :, :, width_state + step_size :].reshape(D, -1)[:, : 2 + KC]
    state_full = small_all[:, :, :, :width_state].reshape(D, width_state)
    filter_full = extra[:, 1:].reshape(-1, rows_all, KC + 1)[:, :state_rows].reshape(-1, KC + 1)
    gains = jnp.stack(split_own(extra[:, 0].astype(full_type), 0))
    step_wide = jnp.pad(step_full, ((0, 0), (0, LANES - heads_own)))
    small_w = split_own(jnp.concatenate([state_full, step_wide], axis=1), 0)
    shards = [
        weight_inner[:, 1].astype(low),
        weight_inner[:, 0].astype(low),
        weight_output.astype(low).T,
    ]
    inner_held = begin_gather(shards[0])
    inner_w = end_gather(inner_held)
    gate_held = begin_gather(after(shards[1], inner_w[0]))
    channel_used = rounded(channel_table)
    head_values = rounded(head_table)
    masked = cotangent * token_valid.astype(low)[:, None]
    masked = after(masked, small_all)
    cots = split_columns(lax.all_gather(masked, "head", axis=1, tiled=True))
    xs = gather_columns(inputs)
    normed, inverse_line = norm(xs, gains)
    small_x = project(normed, small_w)
    gate_w = end_gather(gate_held, small_x)
    output_held = begin_gather(after(shards[2], small_x, *gate_held[1:]))
    inner_x = project(normed, inner_w)
    widths = jnp.repeat(block_widths, BLK)
    norm_counts = (widths.astype(full_type) * P_SIZE)[None, :]
    valid_rows = token_valid.astype(full_type)
    gate_gain = channel_used[KC + 1]
    skip_wide = jnp.repeat(head_values[2], P_SIZE)
    taps_x = jnp.concatenate(
        [channel_used, skip_wide[None, :], jnp.zeros((1, channels), full_type)], axis=0
    )
    taps_s = jnp.pad(filter_full.astype(full_type).T, ((0, 8 - KC - 1), (0, 0)))
    table = jnp.pad(head_values, ((0, 5), (0, LANES - heads_own)))
    inner_x = after(inner_x, gate_w[0])
    mixed, entered = mixer(block_opens, block_widths, inner_x, small_x, taps_x, taps_s, table)
    output_w = end_gather(output_held, mixed)
    gate_w = lax.optimization_barrier((*gate_w, mixed, output_w[0]))[:2]
    gate_values, squares = gate_project(normed, gate_w, mixed)
    gain_line = gate_gain[None, :]
    norm_scale = lax.rsqrt(lax.psum(squares, "head") / norm_counts + EPS)
    projected = scale_gated(mixed, gate_values, norm_scale, gain_line)
    output_grad = whole_weight_grad(cots, projected)
    output_reduced = lax.psum_scatter(output_grad, "dp", scatter_dimension=0, tiled=True)
    output_w = lax.optimization_barrier((*output_w, output_grad))[:2]
    grad_normal, dot_line = output_back(cots, output_w, mixed, gate_values, gain_line)
    total_dot = lax.psum(dot_line, "head")
    scale_back = norm_scale * norm_scale * norm_scale / norm_counts * total_dot
    ybar, gate_low, grad_gate_gain = norm_back(
        block_widths, grad_normal, mixed, gate_values, gain_line, norm_scale, scale_back
    )
    gate_kept, gate_away = weight_grad(normed, gate_low)
    gate_begun = begin_reduce(gate_kept, gate_away)
    ybar = after(ybar, gate_away, gate_kept)
    inner_low, small_low, taps_grad, state_taps, table_grad = mixer_back(
        block_opens, inner_x, small_x, taps_x, taps_s, table, ybar, entered
    )
    inner_kept, inner_away = weight_grad(normed, inner_low)
    inner_begun = begin_reduce(inner_kept, inner_away)
    partial_out = output_project(after(projected, inner_away), output_w)
    out_begun = begin_heads(partial_out)
    gate_fold = fold_pairs(
        (gate_begun[0], after(gate_begun[1], *jax.tree.leaves(partial_out)))
    )
    gate_low_swap = swap_low(gate_fold)
    out_folded = fold_heads((out_begun[0], after(out_begun[1], gate_fold[1])))
    inner_low, output_reduced = lax.optimization_barrier(
        (inner_low, output_reduced, out_folded[0])
    )[:2]
    backs = [gate_low, inner_low, small_low]
    grad_normed, row_line, gain_sums = input_back(
        backs, xs, gains, inverse_line, (*gate_w, *inner_w, *small_w)
    )
    grad_begun = begin_heads(grad_normed)
    grad_small = weight_grad(normed, after(small_low, row_line))
    fold = fold_pairs((inner_begun[0], after(inner_begun[1], grad_small[1])))
    inner_swap = swap_low(fold)
    gate_high = fold_low((gate_low_swap[0], after(gate_low_swap[1], fold[1])))
    gate_sent = swap_high(gate_high)
    grad_folded = fold_heads((grad_begun[0], after(grad_begun[1], gate_high[1])))
    inner_sent = swap_high(fold_low(inner_swap))
    grad_small, gain_sums = lax.optimization_barrier((grad_small, gain_sums, grad_folded[0]))[:2]
    branch = end_heads(out_folded)
    own_grad = end_heads(grad_folded)
    own_inputs = inputs.astype(full_type)
    layer_output = (own_inputs + valid_rows[:, None] * branch).astype(low)
    grad_gain = [gain_sums[0], gain_sums[1]]
    inverse = inverse_line[0]
    row_total = lax.psum(row_line, "head")[0]
    own_width = inputs.shape[1]
    own_gain = lax.dynamic_slice_in_dim(
        join_own(gains[0], gains[1], 0, piece), lax.axis_index("head") * own_width, own_width
    )
    scaled = own_grad * own_gain[None, :]
    inverse_cube = inverse * inverse * inverse
    grad_input = (
        cotangent.astype(full_type)
        + inverse[:, None] * scaled
        - own_inputs * (inverse_cube * row_total / D)[:, None]
    )
    grad_channel = jnp.concatenate([taps_grad[: KC + 1], grad_gate_gain], axis=0)
    grad_skip = jnp.sum(taps_grad[KC + 2].reshape(heads_own, P_SIZE), axis=1)
    grad_head = jnp.concatenate([table_grad[:2, :heads_own], grad_skip[None, :]], axis=0)
    grad_filter = state_taps[: KC + 1].T
    filter_size = state_rows * (KC + 1)
    filter_part = jnp.pad(
        grad_filter.reshape(count_dp, count_head, filter_size),
        ((0, 0), (0, 0), (0, rows_all - filter_size)),
    ).reshape(D)
    shared_part = jnp.stack(
        [
            jnp.concatenate([s[:, :width_state].astype(full_type), g[:, None], f[:, None]], axis=1)
            for s, g, f in zip(grad_small, grad_gain, split_own(filter_part, 0))
        ]
    ).reshape(Y_SIZE, rows_dp, count_head, rows_all, width_state + 2)
    shared_own = reduce_head(jnp.moveaxis(shared_part, 2, 0))
    step_part = jnp.stack(
        [s[:, width_state : width_state + heads_own].astype(full_type) for s in grad_small]
    )
    step_part = step_part.reshape(Y_SIZE, rows_dp, rows_all, -1)
    table_part = jnp.concatenate([grad_channel.reshape(-1), grad_head.reshape(-1)])
    table_width = -(-table_part.shape[0] // rows_all)
    table_part = jnp.pad(table_part, (0, table_width * rows_all - table_part.shape[0]))
    table_part = jnp.broadcast_to(
        table_part.reshape(rows_all, table_width), (Y_SIZE, rows_dp, rows_all, table_width)
    )
    small_part = jnp.concatenate([shared_own, step_part, table_part], axis=3)
    small_part = small_part.reshape(Y_SIZE, rows_dp * rows_all, -1)
    small_begun = begin_reduce(small_part[0], small_part[1].astype(low))
    output_reduced = output_reduced.astype(full_type).T
    small_own = add_parts(swap_high(fold_low(swap_low(fold_pairs(small_begun)))))
    state_reduced = small_own[:, :width_state]
    gain_reduced = small_own[:, width_state]
    filter_reduced = small_own[:filter_size, width_state + 1].reshape(state_rows, KC + 1)
    at = width_state + 2
    step_reduced = small_own[:, at : at + step_part.shape[3]].reshape(-1, heads_own)
    table_own = small_own[:, at + step_part.shape[3] :].reshape(-1)
    channel_size = grad_channel.size
    channel_reduced = table_own[:channel_size].reshape(grad_channel.shape)
    head_reduced = table_own[channel_size : channel_size + grad_head.size].reshape(grad_head.shape)
    total_tokens = inputs.shape[0] * lax.axis_size("dp")
    matrix_rate = RATE_MATRIX / math.sqrt(total_tokens)
    vector_rate = RATE_VECTOR / math.sqrt(total_tokens)
    new_output = advance(
        weight_output, output_reduced, momentum_output, average_output, matrix_rate
    )
    new_inner = advance_inner(
        weight_inner, momentum_inner, average_inner, gate_sent, inner_sent, matrix_rate
    )
    new_step = advance(weight_step, step_reduced, momentum_step, average_step, matrix_rate)
    new_state = advance(weight_state, state_reduced, momentum_state, average_state, matrix_rate)
    new_gain = advance(norm_gain, gain_reduced, momentum_gain, average_gain, vector_rate)
    new_channel = advance(
        channel_table, channel_reduced, momentum_channel, average_channel, vector_rate
    )
    new_head = advance(head_table, head_reduced, momentum_head, average_head, vector_rate)
    new_filter = advance(state_filter, filter_reduced, momentum_filter, average_filter, vector_rate)
    return (
        layer_output,
        grad_input,
        new_inner[0],
        new_inner[1],
        new_inner[2],
        new_step[0],
        new_step[1],
        new_step[2],
        new_output[0],
        new_output[1],
        new_output[2],
        new_state[0],
        new_state[1],
        new_state[2],
        new_gain[0],
        new_gain[1],
        new_gain[2],
        new_channel[0],
        new_channel[1],
        new_channel[2],
        new_head[0],
        new_head[1],
        new_head[2],
        new_filter[0],
        new_filter[1],
        new_filter[2],
    )


def solution(mesh):
    in_specs = (
        P("dp", "head"),
        P("dp", "head"),
        P("dp"),
        P("dp"),
        P("dp"),
        P("dp", None, "head"),
        P("dp", "head"),
        P("head", "dp"),
        P(("dp", "head"), None),
        P(("dp", "head")),
        P(None, "head"),
        P(None, "head"),
        P(("dp", "head"), None),
        P("dp", None, "head"),
        P("dp", "head"),
        P("head", "dp"),
        P(("dp", "head"), None),
        P(("dp", "head")),
        P(None, "head"),
        P(None, "head"),
        P(("dp", "head"), None),
        P("dp", None, "head"),
        P("dp", "head"),
        P("head", "dp"),
        P(("dp", "head"), None),
        P(("dp", "head")),
        P(None, "head"),
        P(None, "head"),
        P(("dp", "head"), None),
    )
    out_specs = (
        P("dp", "head"),
        P("dp", "head"),
        P("dp", None, "head"),
        P("dp", None, "head"),
        P("dp", None, "head"),
        P("dp", "head"),
        P("dp", "head"),
        P("dp", "head"),
        P("head", "dp"),
        P("head", "dp"),
        P("head", "dp"),
        P(("dp", "head"), None),
        P(("dp", "head"), None),
        P(("dp", "head"), None),
        P(("dp", "head")),
        P(("dp", "head")),
        P(("dp", "head")),
        P(None, "head"),
        P(None, "head"),
        P(None, "head"),
        P(None, "head"),
        P(None, "head"),
        P(None, "head"),
        P(("dp", "head"), None),
        P(("dp", "head"), None),
        P(("dp", "head"), None),
    )
    return jax.shard_map(body, mesh=mesh, in_specs=in_specs, out_specs=out_specs, check_vma=False)
```

```python
import functools
import math

import jax
import jax.numpy as jnp
from jax import lax
from jax.experimental import pallas as pl
from jax.experimental.pallas import tpu as pltpu
from jax.sharding import PartitionSpec as P

D = 2048
H = 64
P_SIZE = 64
NS = 128
KC = 4
BLK = 256


EPS = 1e-05
MOMENTUM = 0.9
DECAY = 0.0001
AVERAGE = 0.75
RATE_MATRIX = 0.02
RATE_VECTOR = 0.1
HIGHEST = lax.Precision.HIGHEST


def rounded(value):
    return lax.optimization_barrier(value.astype(jnp.bfloat16)).astype(jnp.float32)


def advance(weight, gradient, moment, average, rate):
    adjusted = gradient + DECAY * weight
    moment_next = MOMENTUM * moment + adjusted
    weight_next = weight - rate * (adjusted + MOMENTUM * moment_next)
    average_next = AVERAGE * average + (1.0 - AVERAGE) * weight_next
    return (weight_next, moment_next, average_next)


LANES = 128
Y_SIZE = 2
FAR = -1e30
GROUP = 4
STEP = 256
WIDE = GROUP * P_SIZE
NT = (((1,), (1,)), ((), ()))
TN = (((0,), (0,)), ((), ()))


def dot32(first, second, dims=(((1,), (0,)), ((), ()))):
    return lax.dot_general(first, second, dims, preferred_element_type=jnp.float32)


def lasting(micros):
    work = int(micros * 1.0 * 1_000_000)
    return pl.CostEstimate(flops=work * 1000, transcendentals=1, bytes_accessed=work * 3)


def softplus(value):
    return jnp.maximum(value, 0.0) + jnp.log1p(jnp.exp(-jnp.abs(value)))


def triangle(upper):
    first = lax.broadcasted_iota(jnp.int32, (BLK, BLK), 0)
    second = lax.broadcasted_iota(jnp.int32, (BLK, BLK), 1)
    return first <= second if upper else first >= second


def filtered(window, taps, lanes):
    total = taps[KC : KC + 1, lanes] + taps[0:1, lanes] * window[5 : 5 + BLK, lanes]
    for offset in range(1, KC):
        total = total + taps[offset : offset + 1, lanes] * window[5 + offset : 5 + offset + BLK, lanes]
    return total


def step_parts(raw, table, heads):
    lane = lax.broadcasted_iota(jnp.int32, (BLK, LANES), 1)
    shifted = raw + table[0:1, :]
    rates = jnp.where(lane < heads, softplus(shifted), 0.0)
    decay = -jnp.exp(table[1:2, :])
    cumulated = jnp.dot(
        triangle(False).astype(jnp.float32),
        rates * decay,
        precision=HIGHEST,
        preferred_element_type=jnp.float32,
    )
    return shifted, rates, decay, cumulated


def spread_columns(value, out, heads):
    for head in range(heads):
        out[head] = jnp.broadcast_to(value[:, head : head + 1], (BLK, LANES))


def group_columns(columns, index):
    side = lax.broadcasted_iota(jnp.int32, (BLK, LANES), 1) < P_SIZE
    first = GROUP * index
    return jnp.concatenate(
        [
            jnp.where(side, columns[first + at], columns[first + at + 1])
            for at in range(0, GROUP, 2)
        ],
        axis=1,
    )


def mixer_kernel(
    heads, opens, widths, v_ref, s_ref, tx, ts, table, mixed, entered,
    window, window_s, state, xs, cum_wide, rate_wide, cum_rows, rate_rows,
):
    block = pl.program_id(0)
    low = jnp.bfloat16

    @pl.when(opens[block] == 1)
    def _():
        window[0:8, :] = jnp.zeros_like(window[0:8, :])
        window_s[0:8, :] = jnp.zeros_like(window_s[0:8, :])
        state[...] = jnp.zeros_like(state)

    @pl.when(opens[block] != 1)
    def _():
        window[0:8, :] = window[BLK : BLK + 8, :]
        window_s[0:8, :] = window_s[BLK : BLK + 8, :]

    window[8 : 8 + BLK, :] = v_ref[...]
    window_s[8 : 8 + BLK, :] = s_ref[:, : 2 * NS]
    shared = filtered(window_s, ts, slice(None))
    shared = (shared * jax.nn.sigmoid(shared)).astype(low)
    maps_in, maps_out = shared[:, :NS], shared[:, NS:]
    maps_in_t = jnp.transpose(maps_in.astype(jnp.float32)).astype(low)
    _, rates, _, cumulated = step_parts(s_ref[:, 2 * NS :], table, heads)
    cum_rows[...] = jnp.transpose(cumulated)[: cum_rows.shape[0]]
    rate_rows[...] = jnp.transpose(rates)[: rate_rows.shape[0]]
    spread_columns(cumulated, cum_wide, heads)
    spread_columns(rates, rate_wide, heads)
    crossing = dot32(maps_out, maps_in, NT)
    width = widths[block]

    def pair(index, _):
        lanes = pl.ds(pl.multiple_of(index * WIDE, WIDE), WIDE)
        pre = filtered(window, tx, lanes)
        values = (pre * jax.nn.sigmoid(pre)).astype(low)
        place_in = lax.broadcasted_iota(jnp.int32, (BLK, WIDE), 1) // P_SIZE
        lower = triangle(False)
        cum_pair = group_columns(cum_wide, index)
        rate_pair = group_columns(rate_wide, index)
        now = state[:, lanes]
        entered[0, :, lanes] = now
        total = jnp.exp(cum_pair) * dot32(maps_out, now.astype(low))
        for half in range(GROUP):
            head = GROUP * index + half
            column = cum_wide[head]
            spread = jnp.concatenate([column, column], axis=1) - cum_rows[pl.ds(head, 1), :]
            decays = jnp.exp(jnp.where(lower, spread, FAR))
            mixing = (crossing * decays * rate_rows[pl.ds(head, 1), :]).astype(low)
            own = place_in == half
            total = total + dot32(mixing, jnp.where(own, values, jnp.zeros_like(values)))
        wide = values.astype(jnp.float32)
        total = total + tx[6:7, lanes] * wide
        head_row = GROUP * index + lax.broadcasted_iota(jnp.int32, (1, WIDE), 1) // P_SIZE
        used = (head_row * H < width * heads).astype(jnp.float32)
        mixed[:, lanes] = total * used
        last = cum_pair[BLK - 1 : BLK, :]
        ending = jnp.exp(last - cum_pair) * rate_pair
        state[:, lanes] = jnp.exp(last) * now + dot32(maps_in_t, (wide * ending).astype(low))
        return 0

    lax.fori_loop(0, heads // GROUP, pair, 0)


def mixer_back_kernel(
    heads, count, opens, v_ref, v_tail, s_ref, s_tail, tx, ts, table, ybar, entered,
    inner_low, small_low, tx_grad, ts_grad, table_grad,
    window, window_s, ahead, ahead_s, state_grad, cum_wide, rate_wide,
    cum_rows, z_rows, cross_grad, maps_grad, column_sum, outer_sum, rate_sum, last_sum,
):
    low = jnp.bfloat16
    step = pl.program_id(0)
    block = count - 1 - step
    opened = opens[block] == 1

    @pl.when(step == 0)
    def _():
        ahead[BLK : BLK + 8, :] = jnp.zeros_like(ahead[BLK : BLK + 8, :])
        ahead_s[BLK : BLK + 8, :] = jnp.zeros_like(ahead_s[BLK : BLK + 8, :])
        state_grad[...] = jnp.zeros_like(state_grad)
        tx_grad[...] = jnp.zeros_like(tx_grad)
        ts_grad[...] = jnp.zeros_like(ts_grad)
        table_grad[...] = jnp.zeros_like(table_grad)
        z_rows[...] = jnp.zeros_like(z_rows)

    @pl.when(opened)
    def _():
        window[0:8, :] = jnp.zeros_like(window[0:8, :])
        window_s[0:8, :] = jnp.zeros_like(window_s[0:8, :])

    @pl.when(jnp.logical_not(opened))
    def _():
        window[0:8, :] = v_tail[...]
        window_s[0:8, :] = s_tail[:, : 2 * NS]

    window[8 : 8 + BLK, :] = v_ref[...]
    window_s[8 : 8 + BLK, :] = s_ref[:, : 2 * NS]
    pre_s = filtered(window_s, ts, slice(None))
    share_s = jax.nn.sigmoid(pre_s)
    shared = (pre_s * share_s).astype(low)
    slope_s = share_s * (1.0 + pre_s * (1.0 - share_s))
    maps_in, maps_out = shared[:, :NS], shared[:, NS:]
    maps_out_t = jnp.transpose(maps_out.astype(jnp.float32)).astype(low)
    shifted, rates, decay, cumulated = step_parts(s_ref[:, 2 * NS :], table, heads)
    cum_rows[...] = jnp.transpose(cumulated)[: cum_rows.shape[0]]
    spread_columns(cumulated, cum_wide, heads)
    spread_columns(rates, rate_wide, heads)
    crossing = dot32(maps_in, maps_out, NT)
    for held in (cross_grad, maps_grad, column_sum, outer_sum, rate_sum, last_sum):
        held[...] = jnp.zeros_like(held)

    def pair(index, _):
        lanes = pl.ds(pl.multiple_of(index * WIDE, WIDE), WIDE)
        pre = filtered(window, tx, lanes)
        share = jax.nn.sigmoid(pre)
        values = (pre * share).astype(low)
        slope = share * (1.0 + pre * (1.0 - share))
        lane = lax.broadcasted_iota(jnp.int32, (BLK, LANES), 1)
        place_in = lax.broadcasted_iota(jnp.int32, (BLK, WIDE), 1) // P_SIZE
        upper = triangle(True)
        cum_pair = group_columns(cum_wide, index)
        rate_pair = group_columns(rate_wide, index)
        back = ybar[:, lanes]
        back_low = back.astype(low)
        wide = values.astype(jnp.float32)
        now = entered[0, :, lanes]
        now_low = now.astype(low)
        after = state_grad[:, lanes]
        after_low = after.astype(low)
        grown = jnp.exp(cum_pair)
        last = cum_pair[BLK - 1 : BLK, :]
        total_decay = jnp.exp(last)
        ending = jnp.exp(last - cum_pair) * rate_pair
        outer = dot32(maps_out, now_low)
        inward = dot32(maps_in, after_low)
        back_grown = back * grown
        back_grown_low = back_grown.astype(low)
        maps_grad[:, NS:] += dot32(back_grown_low, now_low, NT)
        maps_grad[:, :NS] += dot32((wide * ending).astype(low), after_low, NT)
        state_grad[:, lanes] = total_decay * after + dot32(maps_out_t, back_grown_low)
        grad = ending * inward + tx[6:7, lanes] * back
        pick = (
            lax.broadcasted_iota(jnp.int32, (WIDE, LANES), 1)
            == GROUP * index + lax.broadcasted_iota(jnp.int32, (WIDE, LANES), 0) // P_SIZE
        ).astype(low)

        def to_heads(value):
            high = value.astype(low)
            rest = (value - high.astype(jnp.float32)).astype(low)
            return dot32(high, pick) + dot32(rest, pick)

        outer_sum[...] += to_heads(back_grown * outer)
        rate_sum[...] += to_heads(wide * inward)
        kept = jnp.sum(total_decay * after * now, axis=0, keepdims=True)
        last_sum[...] += to_heads(jnp.broadcast_to(kept, (8, WIDE)))
        tx_grad[6:7, lanes] += jnp.sum(back * wide, axis=0, keepdims=True)
        zero = jnp.zeros_like(values)
        for half in range(GROUP):
            head = GROUP * index + half
            own = place_in == half
            column = cum_wide[head]
            rate = rate_wide[head]
            spread = cum_rows[pl.ds(head, 1), :] - jnp.concatenate([column, column], axis=1)
            decays = jnp.exp(jnp.where(upper, spread, FAR))
            weighted = decays * jnp.concatenate([rate, rate], axis=1)
            products = dot32(jnp.where(own, values, zero), back_low, NT)
            summed = jnp.sum(products * (crossing * decays), axis=1, keepdims=True)
            column_sum[...] += jnp.where(lane == head, summed, 0.0)
            mixing = crossing * weighted
            z_rows[pl.ds(head, 1), :] = jnp.sum(products * mixing, axis=0, keepdims=True)
            cross_grad[...] += products * weighted
            grad = grad + dot32(mixing.astype(low), jnp.where(own, back_low, zero))
        back_pre = grad * slope
        ahead[0:BLK, lanes] = back_pre
        spent = tx[KC - 1 : KC, lanes] * back_pre
        for offset in range(1, KC):
            spent = spent + tx[KC - 1 - offset : KC - offset, lanes] * ahead[offset : offset + BLK, lanes]
        inner_low[:, lanes] = spent.astype(low)
        for position in range(KC):
            tx_grad[position : position + 1, lanes] += jnp.sum(
                back_pre * window[5 + position : 5 + position + BLK, lanes], axis=0, keepdims=True
            )
        tx_grad[KC : KC + 1, lanes] += jnp.sum(back_pre, axis=0, keepdims=True)
        return 0

    lax.fori_loop(0, heads // GROUP, pair, 0)
    cross = cross_grad[...]
    cross_low = cross.astype(low)
    maps_grad[:, :NS] += dot32(cross_low, maps_out)
    maps_grad[:, NS:] += dot32(jnp.transpose(cross).astype(low), maps_in)
    back_pre_s = maps_grad[...] * slope_s
    ahead_s[0:BLK, :] = back_pre_s
    spent_s = ts[KC - 1 : KC, :] * back_pre_s
    for offset in range(1, KC):
        spent_s = spent_s + ts[KC - 1 - offset : KC - offset, :] * ahead_s[offset : offset + BLK, :]
    small_low[:, : 2 * NS] = spent_s.astype(low)
    for position in range(KC):
        ts_grad[position : position + 1, :] += jnp.sum(
            back_pre_s * window_s[5 + position : 5 + position + BLK, :], axis=0, keepdims=True
        )
    ts_grad[KC : KC + 1, :] += jnp.sum(back_pre_s, axis=0, keepdims=True)
    lane = lax.broadcasted_iota(jnp.int32, (BLK, LANES), 1)
    falling = jnp.exp(cumulated[BLK - 1 : BLK, :] - cumulated)
    ended = rate_sum[...] * falling
    ended_rate = ended * rates
    own_sum = column_sum[...]
    cum_grad = jnp.transpose(z_rows[...]) + outer_sum[...] - rates * own_sum - ended_rate
    final = last_sum[0:1, :] + jnp.sum(ended_rate, axis=0, keepdims=True)
    place = lax.broadcasted_iota(jnp.int32, (BLK, LANES), 0)
    cum_grad = cum_grad + jnp.where(place == BLK - 1, final, 0.0)
    log_grad = jnp.dot(
        triangle(True).astype(jnp.float32),
        cum_grad,
        precision=HIGHEST,
        preferred_element_type=jnp.float32,
    )
    rate_grad = own_sum + ended + decay * log_grad
    raw_grad = jnp.where(lane < heads, rate_grad * jax.nn.sigmoid(shifted), 0.0)
    small_low[:, 2 * NS :] = raw_grad.astype(low)
    table_grad[0:1, :] += jnp.sum(raw_grad, axis=0, keepdims=True)
    table_grad[1:2, :] += decay * jnp.sum(rates * log_grad, axis=0, keepdims=True)

    @pl.when(opened)
    def _():
        ahead[BLK : BLK + 8, :] = jnp.zeros_like(ahead[BLK : BLK + 8, :])
        ahead_s[BLK : BLK + 8, :] = jnp.zeros_like(ahead_s[BLK : BLK + 8, :])
        state_grad[...] = jnp.zeros_like(state_grad)

    @pl.when(jnp.logical_not(opened))
    def _():
        ahead[BLK : BLK + 8, :] = ahead[0:8, :]
        ahead_s[BLK : BLK + 8, :] = ahead_s[0:8, :]


VMEM_LIMIT = 56 * 1024 * 1024


def mixer(opens, widths, inner, small, tx, ts, table, interpret=False):
    tokens, channels = inner.shape
    heads, count = channels // P_SIZE, tokens // BLK
    whole = lambda rows, columns: pl.BlockSpec((rows, columns), lambda i, *_: (0, 0))
    rows = lambda columns: pl.BlockSpec((BLK, columns), lambda i, *_: (i, 0))
    wide = pltpu.VMEM((heads, BLK, LANES), jnp.float32)
    row_pad = -(-heads // 8) * 8
    return pl.pallas_call(
        functools.partial(mixer_kernel, heads),
        out_shape=(
            jax.ShapeDtypeStruct((tokens, channels), jnp.float32),
            jax.ShapeDtypeStruct((count, NS, channels), jnp.float32),
        ),
        grid_spec=pltpu.PrefetchScalarGridSpec(
            num_scalar_prefetch=2,
            grid=(count,),
            in_specs=[rows(channels), rows(3 * LANES), whole(8, channels), whole(8, 2 * NS), whole(8, LANES)],
            out_specs=[rows(channels), pl.BlockSpec((1, NS, channels), lambda i, *_: (i, 0, 0))],
            scratch_shapes=[
                pltpu.VMEM((BLK + 8, channels), jnp.float32),
                pltpu.VMEM((BLK + 8, 2 * NS), jnp.float32),
                pltpu.VMEM((NS, channels), jnp.float32),
                pltpu.VMEM((8, LANES), jnp.bfloat16),
                wide,
                wide,
                pltpu.VMEM((row_pad, BLK), jnp.float32),
                pltpu.VMEM((row_pad, BLK), jnp.float32),
            ],
        ),
        compiler_params=pltpu.CompilerParams(vmem_limit_bytes=VMEM_LIMIT),
        cost_estimate=lasting(25),
        name="mixer",
        interpret=interpret,
    )(opens, widths, inner, small, tx, ts, table)


def mixer_back(opens, inner, small, tx, ts, table, ybar, entered, interpret=False):
    tokens, channels = inner.shape
    heads, count = channels // P_SIZE, tokens // BLK
    per = BLK // 8
    turn = lambda i: count - 1 - i
    whole = lambda rows, columns: pl.BlockSpec((rows, columns), lambda i, *_: (0, 0))
    rows = lambda columns: pl.BlockSpec((BLK, columns), lambda i, *_: (turn(i), 0))
    tail = lambda columns: pl.BlockSpec(
        (8, columns), lambda i, *_: (jnp.maximum(turn(i) * per - 1, 0), 0)
    )
    wide = pltpu.VMEM((heads, BLK, LANES), jnp.float32)
    row_pad = -(-heads // 8) * 8
    column = pltpu.VMEM((BLK, LANES), jnp.float32)
    return pl.pallas_call(
        functools.partial(mixer_back_kernel, heads, count),
        out_shape=(
            jax.ShapeDtypeStruct((tokens, channels), jnp.bfloat16),
            jax.ShapeDtypeStruct((tokens, 3 * LANES), jnp.bfloat16),
            jax.ShapeDtypeStruct((8, channels), jnp.float32),
            jax.ShapeDtypeStruct((8, 2 * NS), jnp.float32),
            jax.ShapeDtypeStruct((8, LANES), jnp.float32),
        ),
        grid_spec=pltpu.PrefetchScalarGridSpec(
            num_scalar_prefetch=1,
            grid=(count,),
            in_specs=[
                rows(channels),
                tail(channels),
                rows(3 * LANES),
                tail(3 * LANES),
                whole(8, channels),
                whole(8, 2 * NS),
                whole(8, LANES),
                rows(channels),
                pl.BlockSpec((1, NS, channels), lambda i, *_: (turn(i), 0, 0)),
            ],
            out_specs=[rows(channels), rows(3 * LANES), whole(8, channels), whole(8, 2 * NS), whole(8, LANES)],
            scratch_shapes=[
                pltpu.VMEM((BLK + 8, channels), jnp.float32),
                pltpu.VMEM((BLK + 8, 2 * NS), jnp.float32),
                pltpu.VMEM((BLK + 8, channels), jnp.float32),
                pltpu.VMEM((BLK + 8, 2 * NS), jnp.float32),
                pltpu.VMEM((NS, channels), jnp.float32),
                wide,
                wide,
                pltpu.VMEM((row_pad, BLK), jnp.float32),
                pltpu.VMEM((LANES, BLK), jnp.float32),
                pltpu.VMEM((BLK, BLK), jnp.float32),
                pltpu.VMEM((BLK, 2 * NS), jnp.float32),
                column,
                column,
                column,
                pltpu.VMEM((8, LANES), jnp.float32),
            ],
        ),
        compiler_params=pltpu.CompilerParams(vmem_limit_bytes=VMEM_LIMIT),
        cost_estimate=lasting(43),
        name="mixer_back",
        interpret=interpret,
    )(opens, inner, inner, small, small, tx, ts, table, ybar, entered)


def advance_inner_kernel(rate, count, weight, moment, average, *refs):
    parts, outs = refs[:-3], refs[-3:]

    def total(some):
        return sum(x[...].astype(jnp.float32) for x in some)

    for k, gradient in enumerate((total(parts[:count]), total(parts[count:]))):
        news = advance(weight[:, k, :], gradient, moment[:, k, :], average[:, k, :], rate)
        for out, new in zip(outs, news):
            out[:, k, :] = new


def advance_inner(weight, moment, average, gate, inner, rate):
    rows, two, columns = weight.shape
    count = len(gate)
    tile = min(rows, 64)
    pair = pl.BlockSpec((tile, two, columns), lambda i: (i, 0, 0))
    flat = lambda n: pl.BlockSpec((tile, n), lambda i: (i, 0))
    return pl.pallas_call(
        functools.partial(advance_inner_kernel, rate, count),
        out_shape=(jax.ShapeDtypeStruct(weight.shape, weight.dtype),) * 3,
        grid=(rows // tile,),
        in_specs=[pair] * 3 + [flat(columns)] * (count + len(inner)),
        out_specs=[pair] * 3,
        compiler_params=pltpu.CompilerParams(vmem_limit_bytes=VMEM_LIMIT),
        cost_estimate=lasting(8),
        name="advance_inner",
    )(weight, moment, average, *gate, *inner)


def swap_pairs(size):
    return [(i, i ^ 1) for i in range(size)]


def after(value, *earlier):
    return lax.optimization_barrier((value, *earlier))[0]


def place_kernel(count, slots, *refs):
    pieces, out = refs[:count], refs[count]
    step = pl.program_id(0)
    for i in range(count):

        @pl.when(step == i)
        def _(i=i):
            out[...] = pieces[i][...]


def place(pieces, slots, shape=None):
    count = len(pieces)
    pieces = [x if isinstance(x, tuple) else (x, 0) for x in pieces]
    shape = shape or pieces[0][0].shape
    return pl.pallas_call(
        functools.partial(place_kernel, count),
        out_shape=jax.ShapeDtypeStruct((shape[0] * count, *shape[1:]), pieces[0][0].dtype),
        grid_spec=pltpu.PrefetchScalarGridSpec(
            num_scalar_prefetch=1,
            grid=(count,),
            in_specs=[pl.BlockSpec(shape, lambda i, slots, at=at: (at, 0)) for _, at in pieces],
            out_specs=pl.BlockSpec(shape, lambda i, slots: (slots[i], 0)),
        ),
        compiler_params=pltpu.CompilerParams(vmem_limit_bytes=VMEM_LIMIT),
        cost_estimate=lasting(4),
        name="place",
    )(jnp.stack(slots).astype(jnp.int32), *[x for x, _ in pieces])


def my_column():
    return lax.axis_index("dp") % Y_SIZE


def split_own(value, axis):
    count = lax.axis_size("dp")
    shape = value.shape
    wide = value.reshape(
        *shape[:axis], count // Y_SIZE, Y_SIZE, shape[axis] // count, *shape[axis + 1 :]
    )
    halves = [
        lax.index_in_dim(wide, i, axis + 1, keepdims=False).reshape(
            *shape[:axis], shape[axis] // Y_SIZE, *shape[axis + 1 :]
        )
        for i in range(Y_SIZE)
    ]
    first = my_column() == 0
    return jnp.where(first, halves[0], halves[1]), jnp.where(first, halves[1], halves[0])


def join_own(own, other, axis, width):
    first = my_column() == 0
    shape = own.shape
    halves = [
        x.reshape(*shape[:axis], shape[axis] // width, 1, width, *shape[axis + 1 :])
        for x in (jnp.where(first, own, other), jnp.where(first, other, own))
    ]
    return jnp.concatenate(halves, axis=axis + 1).reshape(
        *shape[:axis], shape[axis] * Y_SIZE, *shape[axis + 1 :]
    )


def halves_kernel(piece, column, x, own, other):
    value = x[...]
    first = column[0] == 0
    for row in range(value.shape[1] // piece // Y_SIZE):
        at = row * Y_SIZE * piece
        low, high = value[:, at : at + piece], value[:, at + piece : at + 2 * piece]
        own[:, row * piece : (row + 1) * piece] = jnp.where(first, low, high)
        other[:, row * piece : (row + 1) * piece] = jnp.where(first, high, low)


def split_columns(value):
    tokens, width = value.shape
    piece = width // lax.axis_size("dp")
    if piece % LANES:
        return split_own(value, 1)
    half = jax.ShapeDtypeStruct((tokens, width // Y_SIZE), value.dtype)
    rows = lambda columns: pl.BlockSpec((BLK, columns), lambda i, *_: (i, 0))
    return pl.pallas_call(
        functools.partial(halves_kernel, piece),
        out_shape=(half, half),
        grid_spec=pltpu.PrefetchScalarGridSpec(
            num_scalar_prefetch=1,
            grid=(tokens // BLK,),
            in_specs=[rows(width)],
            out_specs=[rows(width // Y_SIZE)] * 2,
        ),
        cost_estimate=lasting(5),
        name="halves",
    )(my_column().astype(jnp.int32)[None], value)


def columns_kernel(slots, *refs):
    pieces, own, other = refs[:-2], refs[-2], refs[-1]
    first = slots[len(pieces)] == 0
    half = own.shape[1]
    for i, piece in enumerate(pieces):

        @pl.when(pl.program_id(0) == i)
        def _(piece=piece):
            low, high = piece[:, :half], piece[:, half:]
            own[...] = jnp.where(first, low, high)
            other[...] = jnp.where(first, high, low)


def gather_columns(piece):
    tokens, width = piece.shape
    count = lax.axis_size("head")
    if not aligned(width * count // Y_SIZE):
        return split_columns(lax.all_gather(piece, "head", axis=1, tiled=True))
    index = lax.axis_index("head")
    far = lax.ppermute(piece, "head", [(i, i ^ 2) for i in range(count)])
    near = lax.ppermute(piece, "head", swap_pairs(count))
    last = lax.ppermute(far, "head", swap_pairs(count))
    slots = jnp.stack([index, index ^ 1, index ^ 2, index ^ 3, my_column()]).astype(jnp.int32)
    half = jax.ShapeDtypeStruct((tokens, width * count // Y_SIZE), piece.dtype)
    return pl.pallas_call(
        columns_kernel,
        out_shape=(half, half),
        grid_spec=pltpu.PrefetchScalarGridSpec(
            num_scalar_prefetch=1,
            grid=(count,),
            in_specs=[pl.BlockSpec(piece.shape, lambda i, slots: (0, 0))] * count,
            out_specs=[pl.BlockSpec((tokens, width // Y_SIZE), lambda i, slots: (0, slots[i]))] * 2,
        ),
        compiler_params=pltpu.CompilerParams(vmem_limit_bytes=VMEM_LIMIT),
        cost_estimate=lasting(5),
        name="columns",
    )(slots, piece, near, far, last)


def rows_phase(shard):
    count = lax.axis_size("dp")
    held = [shard]
    for shift in range(1, count // Y_SIZE):
        perm = [(i, (i + shift * Y_SIZE) % count) for i in range(count)]
        held.append(lax.ppermute(shard, "dp", perm))
    return held


def begin_gather(shard):
    if lax.axis_size("dp") != 8:
        return [shard]
    return rows_phase(shard)


def end_gather(held, *later):
    if lax.axis_size("dp") != 8:
        return split_own(lax.all_gather(held[0], "dp", axis=0, tiled=True), 0)
    if later:
        held = list(lax.optimization_barrier((*held, *later))[: len(held)])
    row = lax.axis_index("dp") // Y_SIZE
    own = place(held, [(row - i) % len(held) for i in range(len(held))])
    return own, lax.ppermute(own, "dp", swap_pairs(8))


def begin_reduce(kept, away):
    count = lax.axis_size("dp")
    if count != 8:
        return kept, away
    return kept, lax.ppermute(away, "dp", swap_pairs(count))


def fold_pairs(begun, axis=0):
    kept, came = begun
    count = lax.axis_size("dp")
    if count != 8:
        width = kept.shape[axis] // (count // Y_SIZE)
        return None, join_own(kept.astype(came.dtype), came, axis, width)
    shape = kept.shape
    wide = (*shape[:axis], 2, 2, shape[axis] // 4, *shape[axis + 1 :])
    bit = (lax.axis_index("dp") // Y_SIZE) % 2

    def pick(which):
        first, second = (
            lax.dynamic_index_in_dim(x.reshape(wide), which, axis + 1, keepdims=False)
            for x in (kept, came)
        )
        return first + second.astype(jnp.float32)

    return pick(bit), pick(1 - bit).astype(came.dtype)


def swap_low(fold):
    kept, away = fold
    if kept is None:
        return fold
    return kept, lax.ppermute(away, "dp", [(i, i ^ Y_SIZE) for i in range(8)])


def fold_low(swapped, axis=0):
    kept, came = swapped
    if kept is None:
        return None, lax.psum_scatter(came, "dp", scatter_dimension=axis, tiled=True)
    bit = lax.axis_index("dp") // Y_SIZE // 2

    def pick(which):
        first, second = (
            lax.dynamic_index_in_dim(x, which, axis, keepdims=False) for x in (kept, came)
        )
        return first + second.astype(jnp.float32)

    return pick(bit), pick(1 - bit).astype(came.dtype)


def swap_high(fold):
    kept, away = fold
    if kept is None:
        return [away]
    return [kept, lax.ppermute(away, "dp", [(i, i ^ (2 * Y_SIZE)) for i in range(8)])]


def add_parts(parts):
    return sum(x.astype(jnp.float32) for x in parts)


def reduce_head(value):
    count = lax.axis_size("head")
    low = jnp.bfloat16
    if count != 4:
        return lax.psum_scatter(value, "head", scatter_dimension=0, tiled=False)
    index = lax.axis_index("head")
    side, core = index // 2, index % 2
    both = value.reshape(2, 2, *value.shape[1:])
    away = lax.dynamic_index_in_dim(both, 1 - core, 1, keepdims=False)
    kept = lax.dynamic_index_in_dim(both, core, 1, keepdims=False)
    came = lax.ppermute(away.astype(low), "head", swap_pairs(count))
    pair = kept + came.astype(jnp.float32)
    away = lax.dynamic_index_in_dim(pair, 1 - side, 0, keepdims=False)
    kept = lax.dynamic_index_in_dim(pair, side, 0, keepdims=False)
    came = lax.ppermute(away.astype(low), "head", [(i, (i + 2) % 4) for i in range(count)])
    return kept + came.astype(jnp.float32)


def gather_head(piece):
    count = lax.axis_size("head")
    if count != 4:
        return lax.all_gather(piece, "head", axis=0, tiled=True)
    index = lax.axis_index("head")
    far = lax.ppermute(piece, "head", [(i, (i + 2) % 4) for i in range(count)])
    near = lax.ppermute(piece, "head", swap_pairs(count))
    last = lax.ppermute(far, "head", swap_pairs(count))
    across = (index + 2) % 4
    return place([piece, near, far, last], [index, index ^ 1, across, across ^ 1])


LASTING = {
    "norm": 6,
    "project": 8,
    "gate": 10,
    "scale": 6,
    "weight": 8,
    "whole_weight": 11,
    "output_back": 11,
    "norm_back": 10,
    "output": 9,
    "input_back": 20,
}


def call(kernel, name, grid, scalars, args, in_specs, outs, out_specs):
    return pl.pallas_call(
        kernel,
        out_shape=outs,
        grid_spec=pltpu.PrefetchScalarGridSpec(
            num_scalar_prefetch=len(scalars), grid=grid, in_specs=in_specs, out_specs=out_specs
        ),
        compiler_params=pltpu.CompilerParams(vmem_limit_bytes=VMEM_LIMIT),
        cost_estimate=lasting(LASTING[name]),
        name=name,
    )(*scalars, *args)


def rows_of(columns):
    return pl.BlockSpec((STEP, columns), lambda i, *_: (i, 0))


def line_of():
    return pl.BlockSpec((1, STEP), lambda i, *_: (0, i))


def fixed(array):
    return pl.BlockSpec(array.shape, lambda i, *_: (0, 0))


def held_once(array):
    return pl.BlockSpec(array.shape, lambda i, *_: (0, 0), pipeline_mode=pl.Buffered(1))


def typed(kind, *shape):
    return jax.ShapeDtypeStruct(shape, kind)


def to_column(line, columns):
    column = jnp.transpose(jnp.broadcast_to(line, (LANES, line.shape[1])))
    return jnp.concatenate([column] * (columns // LANES), axis=1)


def to_line(value):
    part = value[:, :LANES]
    for at in range(LANES, value.shape[1], LANES):
        part = part + value[:, at : at + LANES]
    return jnp.sum(jnp.transpose(part), axis=0, keepdims=True)


def halves_of(value, piece, first):
    starts = range(0, value.shape[1], Y_SIZE * piece)
    low = jnp.concatenate([value[:, s : s + piece] for s in starts], axis=1)
    high = jnp.concatenate([value[:, s + piece : s + 2 * piece] for s in starts], axis=1)
    return jnp.where(first, low, high), jnp.where(first, high, low)


def norm_kernel(own_in, other_in, gains, own, other, inverse):
    xs = [x[...].astype(jnp.float32) for x in (own_in, other_in)]
    width = xs[0].shape[1]
    sums = to_line(xs[0] * xs[0] + xs[1] * xs[1])
    scale = lax.rsqrt(sums / (2 * width) + EPS)
    inverse[...] = scale
    column = to_column(scale, width)
    for i, (x, out) in enumerate(zip(xs, (own, other))):
        out[...] = (x * column * gains[i : i + 1, :]).astype(jnp.bfloat16)


def norm(xs, gains):
    tokens, width = xs[0].shape
    half = typed(jnp.bfloat16, tokens, width)
    own, other, inverse = call(
        norm_kernel,
        "norm",
        (tokens // STEP,),
        (),
        (*xs, gains),
        [rows_of(width)] * 2 + [fixed(gains)],
        (half, half, typed(jnp.float32, 1, tokens)),
        [rows_of(width)] * 2 + [line_of()],
    )
    return [own, other], inverse


def project_kernel(own, other, w_own, w_other, out):
    out[...] = dot32(own[...], w_own[...]) + dot32(other[...], w_other[...])


def project(halves, weights):
    tokens, width = halves[0].shape
    columns = weights[0].shape[1]
    return call(
        project_kernel,
        "project",
        (tokens // STEP,),
        (),
        (*halves, *weights),
        [rows_of(width)] * 2 + [held_once(w) for w in weights],
        typed(jnp.float32, tokens, columns),
        rows_of(columns),
    )


def gate_kernel(own, other, w_own, w_other, mixed, gate, squares):
    value = dot32(own[...], w_own[...]) + dot32(other[...], w_other[...])
    gate[...] = value
    gated = mixed[...] * (value * jax.nn.sigmoid(value))
    squares[...] = to_line(gated * gated)


def gate_project(halves, weights, mixed):
    tokens, width = halves[0].shape
    columns = mixed.shape[1]
    return call(
        gate_kernel,
        "gate",
        (tokens // STEP,),
        (),
        (*halves, *weights, mixed),
        [rows_of(width)] * 2 + [held_once(w) for w in weights] + [rows_of(columns)],
        (typed(jnp.float32, tokens, columns), typed(jnp.float32, 1, tokens)),
        [rows_of(columns), line_of()],
    )


def scale_kernel(mixed, gate, scale, gain, out):
    value = gate[...]
    gated = mixed[...] * (value * jax.nn.sigmoid(value))
    column = to_column(scale[...], value.shape[1])
    out[...] = (gated * column * gain[...]).astype(jnp.bfloat16)


def scale_gated(mixed, gate, scale, gain):
    tokens, columns = mixed.shape
    return call(
        scale_kernel,
        "scale",
        (tokens // STEP,),
        (),
        (mixed, gate, scale, gain),
        [rows_of(columns)] * 2 + [line_of(), fixed(gain)],
        typed(jnp.bfloat16, tokens, columns),
        rows_of(columns),
    )


def weight_kernel(own, other, back, kept, away):
    kept[...] = dot32(own[...], back[...], TN)
    away[...] = dot32(other[...], back[...], TN).astype(jnp.bfloat16)


def weight_grad(halves, back):
    tokens, width = halves[0].shape
    columns = back.shape[1]
    strip = pl.BlockSpec((tokens, BLK), lambda i, *_: (0, i))
    return call(
        weight_kernel,
        "weight",
        (width // BLK,),
        (),
        (*halves, back),
        [strip] * 2 + [held_once(back)],
        (typed(jnp.float32, width, columns), typed(jnp.bfloat16, width, columns)),
        [pl.BlockSpec((BLK, columns), lambda i, *_: (i, 0))] * 2,
    )


def whole_weight_kernel(column, own, other, back, out):
    mine = pl.program_id(1) == 0

    @pl.when(mine)
    def _():
        out[...] = dot32(own[...], back[...], TN).astype(jnp.bfloat16)

    @pl.when(jnp.logical_not(mine))
    def _():
        out[...] = dot32(other[...], back[...], TN).astype(jnp.bfloat16)


def whole_weight_grad(halves, back):
    tokens, width = halves[0].shape
    columns = back.shape[1]
    piece = Y_SIZE * width // lax.axis_size("dp")
    if piece % LANES:
        kept, away = weight_grad(halves, back)
        return join_own(kept.astype(away.dtype), away, 0, piece)
    strip = pl.BlockSpec((tokens, piece), lambda i, j, *_: (0, i))
    spot = lambda i, j, column: (Y_SIZE * i + (column[0] + j) % Y_SIZE, 0)
    return call(
        whole_weight_kernel,
        "whole_weight",
        (width // piece, Y_SIZE),
        (my_column().astype(jnp.int32)[None],),
        (*halves, back),
        [strip] * 2
        + [pl.BlockSpec(back.shape, lambda i, j, *_: (0, 0), pipeline_mode=pl.Buffered(1))],
        typed(jnp.bfloat16, Y_SIZE * width, columns),
        pl.BlockSpec((piece, columns), spot),
    )


def store_heads(kept, away, spot, own, other):
    first, even = spot[0] == 0, spot[1] == 0
    low = jnp.where(first, own, other).astype(kept.dtype)
    high = jnp.where(first, other, own).astype(kept.dtype)
    half = kept.shape[2] // Y_SIZE
    for side in range(kept.shape[0]):
        for at, value in ((0, low), (half, high)):
            start = 2 * side * half
            one, two = value[:, start : start + half], value[:, start + half : start + 2 * half]
            kept[side, :, at : at + half] = jnp.where(even, one, two)
            away[side, :, at : at + half] = jnp.where(even, two, one)


def my_spot():
    return jnp.stack([my_column(), lax.axis_index("head") % 2]).astype(jnp.int32)


def heads_out(tokens, width):
    count = lax.axis_size("head")
    columns = Y_SIZE * width // count
    shape = typed(jnp.bfloat16, count // 2, tokens, columns)
    return [shape] * 2, [pl.BlockSpec((count // 2, STEP, columns), lambda i, *_: (0, i, 0))] * 2


def aligned(width):
    count = lax.axis_size("dp")
    return count == Y_SIZE * lax.axis_size("head") and Y_SIZE * width // count % LANES == 0


def begin_heads(pair, width):
    if not aligned(width):
        return None, join_own(*pair, 1, Y_SIZE * width // lax.axis_size("dp"))
    kept, away = pair
    return kept, lax.ppermute(away, "head", swap_pairs(4))


def fold_heads(begun):
    kept, near = begun
    if kept is None:
        return [lax.psum_scatter(near, "head", scatter_dimension=1, tiled=True)]
    side = lax.axis_index("head") // 2
    parts = [
        lax.dynamic_index_in_dim(kept, which, 0, keepdims=False).astype(jnp.float32)
        + lax.dynamic_index_in_dim(near, which, 0, keepdims=False)
        for which in (side, 1 - side)
    ]
    away = parts[1].astype(near.dtype)
    return [away, parts[0], lax.ppermute(away, "head", [(i, i ^ 2) for i in range(4)])]


def end_heads(folded):
    return sum(x.astype(jnp.float32) for x in folded[-2:])


def output_back_kernel(own, other, w_own, w_other, mixed, gate, gain, grad, dots):
    value = dot32(own[...], w_own[...]) + dot32(other[...], w_other[...])
    grad[...] = value
    raw = gate[...]
    gated = mixed[...] * (raw * jax.nn.sigmoid(raw))
    dots[...] = to_line(value * gain[...] * gated)


def output_back(halves, weights, mixed, gate, gain):
    tokens, width = halves[0].shape
    columns = mixed.shape[1]
    return call(
        output_back_kernel,
        "output_back",
        (tokens // STEP,),
        (),
        (*halves, *weights, mixed, gate, gain),
        [rows_of(width)] * 2
        + [held_once(w) for w in weights]
        + [rows_of(columns)] * 2
        + [fixed(gain)],
        (typed(jnp.float32, tokens, columns), typed(jnp.float32, 1, tokens)),
        [rows_of(columns), line_of()],
    )


def norm_back_kernel(heads, widths, grad, mixed, gate, gain, scale, scale_back, ybar, gate_low, gain_grad):
    block = pl.program_id(0)
    columns = grad.shape[1]
    raw = gate[...]
    share = jax.nn.sigmoid(raw)
    silu = raw * share
    value, state = grad[...], mixed[...]
    gated = state * silu
    column = to_column(scale[...], columns)
    back = value * gain[...] * column - gated * to_column(scale_back[...], columns)
    lane = lax.broadcasted_iota(jnp.int32, (1, columns), 1)
    used = jnp.concatenate(
        [
            jnp.broadcast_to(
                ((lane // P_SIZE) * H < widths[block * (STEP // BLK) + at] * heads).astype(
                    jnp.float32
                ),
                (BLK, columns),
            )
            for at in range(STEP // BLK)
        ],
        axis=0,
    )
    ybar[...] = back * silu * used
    gate_low[...] = (back * state * (share * (1.0 + raw * (1.0 - share)))).astype(jnp.bfloat16)

    @pl.when(block == 0)
    def _():
        gain_grad[...] = jnp.zeros_like(gain_grad)

    gain_grad[...] += jnp.sum(value * gated * column, axis=0, keepdims=True)


def norm_back(widths, grad, mixed, gate, gain, scale, scale_back):
    tokens, columns = grad.shape
    return call(
        functools.partial(norm_back_kernel, columns // P_SIZE),
        "norm_back",
        (tokens // STEP,),
        (widths,),
        (grad, mixed, gate, gain, scale, scale_back),
        [rows_of(columns)] * 3 + [fixed(gain), line_of(), line_of()],
        (
            typed(jnp.float32, tokens, columns),
            typed(jnp.bfloat16, tokens, columns),
            typed(jnp.float32, 1, columns),
        ),
        [rows_of(columns)] * 2 + [pl.BlockSpec((1, columns), lambda i, *_: (0, 0))],
    )


def output_kernel(whole, spot, value, w_own, w_other, *outs):
    own, other = (dot32(value[...], w[...], NT) for w in (w_own, w_other))
    if whole:
        store_heads(*outs, spot, own, other)
    else:
        outs[0][...], outs[1][...] = own.astype(jnp.bfloat16), other.astype(jnp.bfloat16)


def output_project(value, weights):
    tokens, columns = value.shape
    width = weights[0].shape[0]
    outs, out_specs = [typed(jnp.bfloat16, tokens, width)] * 2, [rows_of(width)] * 2
    if aligned(width):
        outs, out_specs = heads_out(tokens, width)
    return call(
        functools.partial(output_kernel, aligned(width)),
        "output",
        (tokens // STEP,),
        (my_spot(),),
        (value, *weights),
        [rows_of(columns)] + [held_once(w) for w in weights],
        outs,
        out_specs,
    )


def input_back_kernel(whole, spot, gate, inner, small, xo, xt, gains, inverse, *refs):
    weights, outs, line, sums = refs[:6], refs[6:-2], refs[-2], refs[-1]
    block = pl.program_id(0)
    scale = to_column(inverse[...], xo.shape[1])

    @pl.when(block == 0)
    def _():
        sums[...] = jnp.zeros_like(sums)

    total, values = None, []
    for i, x in enumerate((xo, xt)):
        value = (
            dot32(gate[...], weights[i][...], NT)
            + dot32(inner[...], weights[2 + i][...], NT)
            + dot32(small[...], weights[4 + i][...], NT)
        )
        values.append(value)
        product = value * x[...].astype(jnp.float32)
        sums[i : i + 1, :] += jnp.sum(product * scale, axis=0, keepdims=True)
        row = product * gains[i : i + 1, :]
        total = row if total is None else total + row
    line[...] = to_line(total)
    if whole:
        store_heads(*outs, spot, *values)
    else:
        outs[0][...], outs[1][...] = (v.astype(jnp.bfloat16) for v in values)


def input_back(backs, xs, gains, inverse, weights):
    tokens, width = xs[0].shape
    outs, out_specs = [typed(jnp.bfloat16, tokens, width)] * 2, [rows_of(width)] * 2
    if aligned(width):
        outs, out_specs = heads_out(tokens, width)
    *grads, line, sums = call(
        functools.partial(input_back_kernel, aligned(width)),
        "input_back",
        (tokens // STEP,),
        (my_spot(),),
        (*backs, *xs, gains, inverse, *weights),
        [rows_of(b.shape[1]) for b in backs]
        + [rows_of(width)] * 2
        + [fixed(gains), line_of()]
        + [held_once(w) for w in weights],
        (*outs, typed(jnp.float32, 1, tokens), typed(jnp.float32, 2, width)),
        [*out_specs, line_of(), pl.BlockSpec((2, width), lambda i, *_: (0, 0))],
    )
    return tuple(grads), line, sums


def body(
    inputs,
    cotangent,
    token_valid,
    block_opens,
    block_widths,
    weight_inner,
    weight_step,
    weight_output,
    weight_state,
    norm_gain,
    channel_table,
    head_table,
    state_filter,
    momentum_inner,
    momentum_step,
    momentum_output,
    momentum_state,
    momentum_gain,
    momentum_channel,
    momentum_head,
    momentum_filter,
    average_inner,
    average_step,
    average_output,
    average_state,
    average_gain,
    average_channel,
    average_head,
    average_filter,
):
    low = jnp.bfloat16
    full_type = jnp.float32
    count_dp = lax.axis_size("dp")
    count_head = lax.axis_size("head")
    rows_dp, piece = count_dp // Y_SIZE, weight_inner.shape[0]
    tokens, channels = inputs.shape[0], weight_inner.shape[2]
    heads_own = weight_step.shape[1]
    rows_all, state_rows = weight_state.shape[0], state_filter.shape[0]
    width_state = weight_state.shape[1]
    filter_block = jnp.pad(state_filter.astype(low), ((0, rows_all - state_rows), (0, 0)))
    small_piece = jnp.concatenate(
        [
            weight_state.astype(low),
            weight_step.astype(low).reshape(rows_all, -1),
            norm_gain.astype(low)[:, None],
            filter_block,
        ],
        axis=1,
    )
    small_piece = jnp.pad(small_piece, ((0, 0), (0, -small_piece.shape[1] % LANES)))
    small_all = lax.all_gather(
        small_piece, ("dp", "head"), axis=0, tiled=False
    ).reshape(count_dp, count_head, rows_all, -1)
    step_size = rows_all * count_head * heads_own // rows_all
    step_full = lax.dynamic_index_in_dim(small_all, lax.axis_index("head"), 1, keepdims=False)
    step_full = step_full[:, :, width_state : width_state + step_size].reshape(D, heads_own)
    extra = small_all[:, :, :, width_state + step_size :].reshape(D, -1)[:, : 2 + KC]
    state_full = small_all[:, :, :, :width_state].reshape(D, width_state)
    filter_full = extra[:, 1:].reshape(-1, rows_all, KC + 1)[:, :state_rows].reshape(-1, KC + 1)
    gains = jnp.stack(split_own(extra[:, 0].astype(full_type), 0))
    step_wide = jnp.pad(step_full, ((0, 0), (0, LANES - heads_own)))
    small_w = split_own(jnp.concatenate([state_full, step_wide], axis=1), 0)
    shards = [
        weight_inner[:, 1].astype(low),
        weight_inner[:, 0].astype(low),
        weight_output.astype(low).T,
    ]
    inner_held = begin_gather(shards[0])
    inner_w = end_gather(inner_held)
    gate_held = begin_gather(after(shards[1], inner_w[0]))
    channel_used = rounded(channel_table)
    head_values = rounded(head_table)
    masked = cotangent * token_valid.astype(low)[:, None]
    masked = after(masked, small_all)
    cots = split_columns(lax.all_gather(masked, "head", axis=1, tiled=True))
    xs = gather_columns(inputs)
    normed, inverse_line = norm(xs, gains)
    small_x = project(normed, small_w)
    gate_w = end_gather(gate_held, small_x)
    output_held = begin_gather(after(shards[2], small_x, *gate_held[1:]))
    inner_x = project(normed, inner_w)
    widths = jnp.repeat(block_widths, BLK)
    norm_counts = (widths.astype(full_type) * P_SIZE)[None, :]
    valid_rows = token_valid.astype(full_type)
    gate_gain = channel_used[KC + 1]
    skip_wide = jnp.repeat(head_values[2], P_SIZE)
    taps_x = jnp.concatenate(
        [channel_used, skip_wide[None, :], jnp.zeros((1, channels), full_type)], axis=0
    )
    taps_s = jnp.pad(filter_full.astype(full_type).T, ((0, 8 - KC - 1), (0, 0)))
    table = jnp.pad(head_values, ((0, 5), (0, LANES - heads_own)))
    inner_x = after(inner_x, gate_w[0])
    mixed, entered = mixer(block_opens, block_widths, inner_x, small_x, taps_x, taps_s, table)
    output_w = end_gather(output_held, mixed)
    gate_w = lax.optimization_barrier((*gate_w, mixed, output_w[0]))[:2]
    gate_values, squares = gate_project(normed, gate_w, mixed)
    gain_line = gate_gain[None, :]
    norm_scale = lax.rsqrt(lax.psum(squares, "head") / norm_counts + EPS)
    projected = scale_gated(mixed, gate_values, norm_scale, gain_line)
    output_grad = whole_weight_grad(cots, projected)
    output_reduced = lax.psum_scatter(output_grad, "dp", scatter_dimension=0, tiled=True)
    output_w = lax.optimization_barrier((*output_w, output_grad))[:2]
    grad_normal, dot_line = output_back(cots, output_w, mixed, gate_values, gain_line)
    total_dot = lax.psum(dot_line, "head")
    scale_back = norm_scale * norm_scale * norm_scale / norm_counts * total_dot
    ybar, gate_low, grad_gate_gain = norm_back(
        block_widths, grad_normal, mixed, gate_values, gain_line, norm_scale, scale_back
    )
    gate_kept, gate_away = weight_grad(normed, gate_low)
    gate_begun = begin_reduce(gate_kept, gate_away)
    ybar = after(ybar, gate_away, gate_kept)
    inner_low, small_low, taps_grad, state_taps, table_grad = mixer_back(
        block_opens, inner_x, small_x, taps_x, taps_s, table, ybar, entered
    )
    inner_kept, inner_away = weight_grad(normed, inner_low)
    inner_begun = begin_reduce(inner_kept, inner_away)
    partial_out = output_project(after(projected, inner_away), output_w)
    out_begun = begin_heads(partial_out, output_w[0].shape[0])
    gate_fold = fold_pairs(
        (gate_begun[0], after(gate_begun[1], *jax.tree.leaves(partial_out)))
    )
    gate_low_swap = swap_low(gate_fold)
    out_folded = fold_heads((out_begun[0], after(out_begun[1], gate_fold[1])))
    inner_low, output_reduced = lax.optimization_barrier(
        (inner_low, output_reduced, out_folded[0])
    )[:2]
    backs = [gate_low, inner_low, small_low]
    grad_normed, row_line, gain_sums = input_back(
        backs, xs, gains, inverse_line, (*gate_w, *inner_w, *small_w)
    )
    grad_begun = begin_heads(grad_normed, inner_w[0].shape[0])
    grad_small = weight_grad(normed, after(small_low, row_line))
    fold = fold_pairs((inner_begun[0], after(inner_begun[1], grad_small[1])))
    inner_swap = swap_low(fold)
    gate_high = fold_low((gate_low_swap[0], after(gate_low_swap[1], fold[1])))
    gate_sent = swap_high(gate_high)
    grad_folded = fold_heads((grad_begun[0], after(grad_begun[1], gate_high[1])))
    inner_sent = swap_high(fold_low(inner_swap))
    grad_small, gain_sums = lax.optimization_barrier((grad_small, gain_sums, grad_folded[0]))[:2]
    branch = end_heads(out_folded)
    own_grad = end_heads(grad_folded)
    own_inputs = inputs.astype(full_type)
    layer_output = (own_inputs + valid_rows[:, None] * branch).astype(low)
    grad_gain = [gain_sums[0], gain_sums[1]]
    inverse = inverse_line[0]
    row_total = lax.psum(row_line, "head")[0]
    own_width = inputs.shape[1]
    own_gain = lax.dynamic_slice_in_dim(
        join_own(gains[0], gains[1], 0, piece), lax.axis_index("head") * own_width, own_width
    )
    scaled = own_grad * own_gain[None, :]
    inverse_cube = inverse * inverse * inverse
    grad_input = (
        cotangent.astype(full_type)
        + inverse[:, None] * scaled
        - own_inputs * (inverse_cube * row_total / D)[:, None]
    )
    grad_channel = jnp.concatenate([taps_grad[: KC + 1], grad_gate_gain], axis=0)
    grad_skip = jnp.sum(taps_grad[KC + 2].reshape(heads_own, P_SIZE), axis=1)
    grad_head = jnp.concatenate([table_grad[:2, :heads_own], grad_skip[None, :]], axis=0)
    grad_filter = state_taps[: KC + 1].T
    filter_size = state_rows * (KC + 1)
    filter_part = jnp.pad(
        grad_filter.reshape(count_dp, count_head, filter_size),
        ((0, 0), (0, 0), (0, rows_all - filter_size)),
    ).reshape(D)
    shared_part = jnp.stack(
        [
            jnp.concatenate([s[:, :width_state].astype(full_type), g[:, None], f[:, None]], axis=1)
            for s, g, f in zip(grad_small, grad_gain, split_own(filter_part, 0))
        ]
    ).reshape(Y_SIZE, rows_dp, count_head, rows_all, width_state + 2)
    shared_own = reduce_head(jnp.moveaxis(shared_part, 2, 0))
    step_part = jnp.stack(
        [s[:, width_state : width_state + heads_own].astype(full_type) for s in grad_small]
    )
    step_part = step_part.reshape(Y_SIZE, rows_dp, rows_all, -1)
    table_part = jnp.concatenate([grad_channel.reshape(-1), grad_head.reshape(-1)])
    table_width = -(-table_part.shape[0] // rows_all)
    table_part = jnp.pad(table_part, (0, table_width * rows_all - table_part.shape[0]))
    table_part = jnp.broadcast_to(
        table_part.reshape(rows_all, table_width), (Y_SIZE, rows_dp, rows_all, table_width)
    )
    small_part = jnp.concatenate([shared_own, step_part, table_part], axis=3)
    small_part = small_part.reshape(Y_SIZE, rows_dp * rows_all, -1)
    small_begun = begin_reduce(small_part[0], small_part[1].astype(low))
    output_reduced = output_reduced.astype(full_type).T
    small_own = add_parts(swap_high(fold_low(swap_low(fold_pairs(small_begun)))))
    state_reduced = small_own[:, :width_state]
    gain_reduced = small_own[:, width_state]
    filter_reduced = small_own[:filter_size, width_state + 1].reshape(state_rows, KC + 1)
    at = width_state + 2
    step_reduced = small_own[:, at : at + step_part.shape[3]].reshape(-1, heads_own)
    table_own = small_own[:, at + step_part.shape[3] :].reshape(-1)
    channel_size = grad_channel.size
    channel_reduced = table_own[:channel_size].reshape(grad_channel.shape)
    head_reduced = table_own[channel_size : channel_size + grad_head.size].reshape(grad_head.shape)
    total_tokens = inputs.shape[0] * lax.axis_size("dp")
    matrix_rate = RATE_MATRIX / math.sqrt(total_tokens)
    vector_rate = RATE_VECTOR / math.sqrt(total_tokens)
    new_output = advance(
        weight_output, output_reduced, momentum_output, average_output, matrix_rate
    )
    new_inner = advance_inner(
        weight_inner, momentum_inner, average_inner, gate_sent, inner_sent, matrix_rate
    )
    new_step = advance(weight_step, step_reduced, momentum_step, average_step, matrix_rate)
    new_state = advance(weight_state, state_reduced, momentum_state, average_state, matrix_rate)
    new_gain = advance(norm_gain, gain_reduced, momentum_gain, average_gain, vector_rate)
    new_channel = advance(
        channel_table, channel_reduced, momentum_channel, average_channel, vector_rate
    )
    new_head = advance(head_table, head_reduced, momentum_head, average_head, vector_rate)
    new_filter = advance(state_filter, filter_reduced, momentum_filter, average_filter, vector_rate)
    return (
        layer_output,
        grad_input,
        new_inner[0],
        new_inner[1],
        new_inner[2],
        new_step[0],
        new_step[1],
        new_step[2],
        new_output[0],
        new_output[1],
        new_output[2],
        new_state[0],
        new_state[1],
        new_state[2],
        new_gain[0],
        new_gain[1],
        new_gain[2],
        new_channel[0],
        new_channel[1],
        new_channel[2],
        new_head[0],
        new_head[1],
        new_head[2],
        new_filter[0],
        new_filter[1],
        new_filter[2],
    )


def solution(mesh):
    in_specs = (
        P("dp", "head"),
        P("dp", "head"),
        P("dp"),
        P("dp"),
        P("dp"),
        P("dp", None, "head"),
        P("dp", "head"),
        P("head", "dp"),
        P(("dp", "head"), None),
        P(("dp", "head")),
        P(None, "head"),
        P(None, "head"),
        P(("dp", "head"), None),
        P("dp", None, "head"),
        P("dp", "head"),
        P("head", "dp"),
        P(("dp", "head"), None),
        P(("dp", "head")),
        P(None, "head"),
        P(None, "head"),
        P(("dp", "head"), None),
        P("dp", None, "head"),
        P("dp", "head"),
        P("head", "dp"),
        P(("dp", "head"), None),
        P(("dp", "head")),
        P(None, "head"),
        P(None, "head"),
        P(("dp", "head"), None),
    )
    out_specs = (
        P("dp", "head"),
        P("dp", "head"),
        P("dp", None, "head"),
        P("dp", None, "head"),
        P("dp", None, "head"),
        P("dp", "head"),
        P("dp", "head"),
        P("dp", "head"),
        P("head", "dp"),
        P("head", "dp"),
        P("head", "dp"),
        P(("dp", "head"), None),
        P(("dp", "head"), None),
        P(("dp", "head"), None),
        P(("dp", "head")),
        P(("dp", "head")),
        P(("dp", "head")),
        P(None, "head"),
        P(None, "head"),
        P(None, "head"),
        P(None, "head"),
        P(None, "head"),
        P(None, "head"),
        P(("dp", "head"), None),
        P(("dp", "head"), None),
        P(("dp", "head"), None),
    )
    return jax.shard_map(body, mesh=mesh, in_specs=in_specs, out_specs=out_specs, check_vma=False)
```

```python
import functools
import math

import jax
import jax.numpy as jnp
from jax import lax
from jax.experimental import pallas as pl
from jax.experimental.pallas import tpu as pltpu
from jax.sharding import PartitionSpec as P

D = 2048
H = 64
P_SIZE = 64
NS = 128
KC = 4
BLK = 256


EPS = 1e-05
MOMENTUM = 0.9
DECAY = 0.0001
AVERAGE = 0.75
RATE_MATRIX = 0.02
RATE_VECTOR = 0.1
HIGHEST = lax.Precision.HIGHEST


def rounded(value):
    return lax.optimization_barrier(value.astype(jnp.bfloat16)).astype(jnp.float32)


def advance(weight, gradient, moment, average, rate):
    adjusted = gradient + DECAY * weight
    moment_next = MOMENTUM * moment + adjusted
    weight_next = weight - rate * (adjusted + MOMENTUM * moment_next)
    average_next = AVERAGE * average + (1.0 - AVERAGE) * weight_next
    return (weight_next, moment_next, average_next)


LANES = 128
Y_SIZE = 2
FAR = -1e30
GROUP = 2
STEP = 256
WIDE = GROUP * P_SIZE
NT = (((1,), (1,)), ((), ()))
TN = (((0,), (0,)), ((), ()))


def dot32(first, second, dims=(((1,), (0,)), ((), ()))):
    return lax.dot_general(first, second, dims, preferred_element_type=jnp.float32)


def lasting(micros):
    work = int(micros * 1.0 * 1_000_000)
    return pl.CostEstimate(flops=work * 1000, transcendentals=1, bytes_accessed=work * 3)


def softplus(value):
    return jnp.maximum(value, 0.0) + jnp.log1p(jnp.exp(-jnp.abs(value)))


def triangle(upper):
    first = lax.broadcasted_iota(jnp.int32, (BLK, BLK), 0)
    second = lax.broadcasted_iota(jnp.int32, (BLK, BLK), 1)
    return first <= second if upper else first >= second


def filtered(window, taps, lanes):
    total = taps[KC : KC + 1, lanes] + taps[0:1, lanes] * window[5 : 5 + BLK, lanes]
    for offset in range(1, KC):
        total = total + taps[offset : offset + 1, lanes] * window[5 + offset : 5 + offset + BLK, lanes]
    return total


def step_parts(raw, table, heads):
    lane = lax.broadcasted_iota(jnp.int32, (BLK, LANES), 1)
    shifted = raw + table[0:1, :]
    rates = jnp.where(lane < heads, softplus(shifted), 0.0)
    decay = -jnp.exp(table[1:2, :])
    cumulated = jnp.dot(
        triangle(False).astype(jnp.float32),
        rates * decay,
        precision=HIGHEST,
        preferred_element_type=jnp.float32,
    )
    return shifted, rates, decay, cumulated


def spread_columns(value, out, heads):
    for head in range(heads):
        out[head] = jnp.broadcast_to(value[:, head : head + 1], (BLK, LANES))


def group_columns(columns, index):
    side = lax.broadcasted_iota(jnp.int32, (BLK, LANES), 1) < P_SIZE
    first = GROUP * index
    return jnp.concatenate(
        [
            jnp.where(side, columns[first + at], columns[first + at + 1])
            for at in range(0, GROUP, 2)
        ],
        axis=1,
    )


def mixer_kernel(
    heads, opens, widths, v_ref, s_ref, tx, ts, table, mixed, entered,
    window, window_s, state, xs, cum_wide, rate_wide, cum_rows, rate_rows,
):
    block = pl.program_id(0)
    low = jnp.bfloat16

    @pl.when(opens[block] == 1)
    def _():
        window[0:8, :] = jnp.zeros_like(window[0:8, :])
        window_s[0:8, :] = jnp.zeros_like(window_s[0:8, :])
        state[...] = jnp.zeros_like(state)

    @pl.when(opens[block] != 1)
    def _():
        window[0:8, :] = window[BLK : BLK + 8, :]
        window_s[0:8, :] = window_s[BLK : BLK + 8, :]

    window[8 : 8 + BLK, :] = v_ref[...]
    window_s[8 : 8 + BLK, :] = s_ref[:, : 2 * NS]
    shared = filtered(window_s, ts, slice(None))
    shared = (shared * jax.nn.sigmoid(shared)).astype(low)
    maps_in, maps_out = shared[:, :NS], shared[:, NS:]
    maps_in_t = jnp.transpose(maps_in.astype(jnp.float32)).astype(low)
    _, rates, _, cumulated = step_parts(s_ref[:, 2 * NS :], table, heads)
    cum_rows[...] = jnp.transpose(cumulated)[: cum_rows.shape[0]]
    rate_rows[...] = jnp.transpose(rates)[: rate_rows.shape[0]]
    spread_columns(cumulated, cum_wide, heads)
    spread_columns(rates, rate_wide, heads)
    crossing = dot32(maps_out, maps_in, NT)
    width = widths[block]

    def pair(index, _):
        lanes = pl.ds(pl.multiple_of(index * WIDE, WIDE), WIDE)
        pre = filtered(window, tx, lanes)
        values = (pre * jax.nn.sigmoid(pre)).astype(low)
        place_in = lax.broadcasted_iota(jnp.int32, (BLK, WIDE), 1) // P_SIZE
        lower = triangle(False)
        cum_pair = group_columns(cum_wide, index)
        rate_pair = group_columns(rate_wide, index)
        now = state[:, lanes]
        entered[0, :, lanes] = now
        total = jnp.exp(cum_pair) * dot32(maps_out, now.astype(low))
        for half in range(GROUP):
            head = GROUP * index + half
            column = cum_wide[head]
            spread = jnp.concatenate([column, column], axis=1) - cum_rows[pl.ds(head, 1), :]
            decays = jnp.exp(jnp.where(lower, spread, FAR))
            mixing = (crossing * decays * rate_rows[pl.ds(head, 1), :]).astype(low)
            own = place_in == half
            total = total + dot32(mixing, jnp.where(own, values, jnp.zeros_like(values)))
        wide = values.astype(jnp.float32)
        total = total + tx[6:7, lanes] * wide
        head_row = GROUP * index + lax.broadcasted_iota(jnp.int32, (1, WIDE), 1) // P_SIZE
        used = (head_row * H < width * heads).astype(jnp.float32)
        mixed[:, lanes] = total * used
        last = cum_pair[BLK - 1 : BLK, :]
        ending = jnp.exp(last - cum_pair) * rate_pair
        state[:, lanes] = jnp.exp(last) * now + dot32(maps_in_t, (wide * ending).astype(low))
        return 0

    lax.fori_loop(0, heads // GROUP, pair, 0)


def mixer_back_kernel(
    heads, count, opens, v_ref, v_tail, s_ref, s_tail, tx, ts, table, ybar, entered,
    inner_low, small_low, tx_grad, ts_grad, table_grad,
    window, window_s, ahead, ahead_s, state_grad, cum_wide, rate_wide,
    cum_rows, z_rows, cross_grad, maps_grad, column_sum, outer_sum, rate_sum, last_sum,
):
    low = jnp.bfloat16
    step = pl.program_id(0)
    block = count - 1 - step
    opened = opens[block] == 1

    @pl.when(step == 0)
    def _():
        ahead[BLK : BLK + 8, :] = jnp.zeros_like(ahead[BLK : BLK + 8, :])
        ahead_s[BLK : BLK + 8, :] = jnp.zeros_like(ahead_s[BLK : BLK + 8, :])
        state_grad[...] = jnp.zeros_like(state_grad)
        tx_grad[...] = jnp.zeros_like(tx_grad)
        ts_grad[...] = jnp.zeros_like(ts_grad)
        table_grad[...] = jnp.zeros_like(table_grad)
        z_rows[...] = jnp.zeros_like(z_rows)

    @pl.when(opened)
    def _():
        window[0:8, :] = jnp.zeros_like(window[0:8, :])
        window_s[0:8, :] = jnp.zeros_like(window_s[0:8, :])

    @pl.when(jnp.logical_not(opened))
    def _():
        window[0:8, :] = v_tail[...]
        window_s[0:8, :] = s_tail[:, : 2 * NS]

    window[8 : 8 + BLK, :] = v_ref[...]
    window_s[8 : 8 + BLK, :] = s_ref[:, : 2 * NS]
    pre_s = filtered(window_s, ts, slice(None))
    share_s = jax.nn.sigmoid(pre_s)
    shared = (pre_s * share_s).astype(low)
    slope_s = share_s * (1.0 + pre_s * (1.0 - share_s))
    maps_in, maps_out = shared[:, :NS], shared[:, NS:]
    maps_out_t = jnp.transpose(maps_out.astype(jnp.float32)).astype(low)
    shifted, rates, decay, cumulated = step_parts(s_ref[:, 2 * NS :], table, heads)
    cum_rows[...] = jnp.transpose(cumulated)[: cum_rows.shape[0]]
    spread_columns(cumulated, cum_wide, heads)
    spread_columns(rates, rate_wide, heads)
    crossing = dot32(maps_in, maps_out, NT)
    for held in (cross_grad, maps_grad, column_sum, outer_sum, rate_sum, last_sum):
        held[...] = jnp.zeros_like(held)

    def pair(index, _):
        lanes = pl.ds(pl.multiple_of(index * WIDE, WIDE), WIDE)
        pre = filtered(window, tx, lanes)
        share = jax.nn.sigmoid(pre)
        values = (pre * share).astype(low)
        slope = share * (1.0 + pre * (1.0 - share))
        lane = lax.broadcasted_iota(jnp.int32, (BLK, LANES), 1)
        place_in = lax.broadcasted_iota(jnp.int32, (BLK, WIDE), 1) // P_SIZE
        upper = triangle(True)
        cum_pair = group_columns(cum_wide, index)
        rate_pair = group_columns(rate_wide, index)
        back = ybar[:, lanes]
        back_low = back.astype(low)
        wide = values.astype(jnp.float32)
        now = entered[0, :, lanes]
        now_low = now.astype(low)
        after = state_grad[:, lanes]
        after_low = after.astype(low)
        grown = jnp.exp(cum_pair)
        last = cum_pair[BLK - 1 : BLK, :]
        total_decay = jnp.exp(last)
        ending = jnp.exp(last - cum_pair) * rate_pair
        outer = dot32(maps_out, now_low)
        inward = dot32(maps_in, after_low)
        back_grown = back * grown
        back_grown_low = back_grown.astype(low)
        maps_grad[:, NS:] += dot32(back_grown_low, now_low, NT)
        maps_grad[:, :NS] += dot32((wide * ending).astype(low), after_low, NT)
        state_grad[:, lanes] = total_decay * after + dot32(maps_out_t, back_grown_low)
        grad = ending * inward + tx[6:7, lanes] * back
        pick = (
            lax.broadcasted_iota(jnp.int32, (WIDE, LANES), 1)
            == GROUP * index + lax.broadcasted_iota(jnp.int32, (WIDE, LANES), 0) // P_SIZE
        ).astype(low)

        def to_heads(value):
            high = value.astype(low)
            rest = (value - high.astype(jnp.float32)).astype(low)
            return dot32(high, pick) + dot32(rest, pick)

        outer_sum[...] += to_heads(back_grown * outer)
        rate_sum[...] += to_heads(wide * inward)
        kept = jnp.sum(total_decay * after * now, axis=0, keepdims=True)
        last_sum[...] += to_heads(jnp.broadcast_to(kept, (8, WIDE)))
        tx_grad[6:7, lanes] += jnp.sum(back * wide, axis=0, keepdims=True)
        zero = jnp.zeros_like(values)
        for half in range(GROUP):
            head = GROUP * index + half
            own = place_in == half
            column = cum_wide[head]
            rate = rate_wide[head]
            spread = cum_rows[pl.ds(head, 1), :] - jnp.concatenate([column, column], axis=1)
            decays = jnp.exp(jnp.where(upper, spread, FAR))
            weighted = decays * jnp.concatenate([rate, rate], axis=1)
            products = dot32(jnp.where(own, values, zero), back_low, NT)
            summed = jnp.sum(products * (crossing * decays), axis=1, keepdims=True)
            column_sum[...] += jnp.where(lane == head, summed, 0.0)
            mixing = crossing * weighted
            z_rows[pl.ds(head, 1), :] = jnp.sum(products * mixing, axis=0, keepdims=True)
            cross_grad[...] += products * weighted
            grad = grad + dot32(mixing.astype(low), jnp.where(own, back_low, zero))
        back_pre = grad * slope
        ahead[0:BLK, lanes] = back_pre
        spent = tx[KC - 1 : KC, lanes] * back_pre
        for offset in range(1, KC):
            spent = spent + tx[KC - 1 - offset : KC - offset, lanes] * ahead[offset : offset + BLK, lanes]
        inner_low[:, lanes] = spent.astype(low)
        for position in range(KC):
            tx_grad[position : position + 1, lanes] += jnp.sum(
                back_pre * window[5 + position : 5 + position + BLK, lanes], axis=0, keepdims=True
            )
        tx_grad[KC : KC + 1, lanes] += jnp.sum(back_pre, axis=0, keepdims=True)
        return 0

    lax.fori_loop(0, heads // GROUP, pair, 0)
    cross = cross_grad[...]
    cross_low = cross.astype(low)
    maps_grad[:, :NS] += dot32(cross_low, maps_out)
    maps_grad[:, NS:] += dot32(jnp.transpose(cross).astype(low), maps_in)
    back_pre_s = maps_grad[...] * slope_s
    ahead_s[0:BLK, :] = back_pre_s
    spent_s = ts[KC - 1 : KC, :] * back_pre_s
    for offset in range(1, KC):
        spent_s = spent_s + ts[KC - 1 - offset : KC - offset, :] * ahead_s[offset : offset + BLK, :]
    small_low[:, : 2 * NS] = spent_s.astype(low)
    for position in range(KC):
        ts_grad[position : position + 1, :] += jnp.sum(
            back_pre_s * window_s[5 + position : 5 + position + BLK, :], axis=0, keepdims=True
        )
    ts_grad[KC : KC + 1, :] += jnp.sum(back_pre_s, axis=0, keepdims=True)
    lane = lax.broadcasted_iota(jnp.int32, (BLK, LANES), 1)
    falling = jnp.exp(cumulated[BLK - 1 : BLK, :] - cumulated)
    ended = rate_sum[...] * falling
    ended_rate = ended * rates
    own_sum = column_sum[...]
    cum_grad = jnp.transpose(z_rows[...]) + outer_sum[...] - rates * own_sum - ended_rate
    final = last_sum[0:1, :] + jnp.sum(ended_rate, axis=0, keepdims=True)
    place = lax.broadcasted_iota(jnp.int32, (BLK, LANES), 0)
    cum_grad = cum_grad + jnp.where(place == BLK - 1, final, 0.0)
    log_grad = jnp.dot(
        triangle(True).astype(jnp.float32),
        cum_grad,
        precision=HIGHEST,
        preferred_element_type=jnp.float32,
    )
    rate_grad = own_sum + ended + decay * log_grad
    raw_grad = jnp.where(lane < heads, rate_grad * jax.nn.sigmoid(shifted), 0.0)
    small_low[:, 2 * NS :] = raw_grad.astype(low)
    table_grad[0:1, :] += jnp.sum(raw_grad, axis=0, keepdims=True)
    table_grad[1:2, :] += decay * jnp.sum(rates * log_grad, axis=0, keepdims=True)

    @pl.when(opened)
    def _():
        ahead[BLK : BLK + 8, :] = jnp.zeros_like(ahead[BLK : BLK + 8, :])
        ahead_s[BLK : BLK + 8, :] = jnp.zeros_like(ahead_s[BLK : BLK + 8, :])
        state_grad[...] = jnp.zeros_like(state_grad)

    @pl.when(jnp.logical_not(opened))
    def _():
        ahead[BLK : BLK + 8, :] = ahead[0:8, :]
        ahead_s[BLK : BLK + 8, :] = ahead_s[0:8, :]


VMEM_LIMIT = 56 * 1024 * 1024


def mixer(opens, widths, inner, small, tx, ts, table, interpret=False):
    tokens, channels = inner.shape
    heads, count = channels // P_SIZE, tokens // BLK
    whole = lambda rows, columns: pl.BlockSpec((rows, columns), lambda i, *_: (0, 0))
    rows = lambda columns: pl.BlockSpec((BLK, columns), lambda i, *_: (i, 0))
    wide = pltpu.VMEM((heads, BLK, LANES), jnp.float32)
    row_pad = -(-heads // 8) * 8
    return pl.pallas_call(
        functools.partial(mixer_kernel, heads),
        out_shape=(
            jax.ShapeDtypeStruct((tokens, channels), jnp.float32),
            jax.ShapeDtypeStruct((count, NS, channels), jnp.float32),
        ),
        grid_spec=pltpu.PrefetchScalarGridSpec(
            num_scalar_prefetch=2,
            grid=(count,),
            in_specs=[rows(channels), rows(3 * LANES), whole(8, channels), whole(8, 2 * NS), whole(8, LANES)],
            out_specs=[rows(channels), pl.BlockSpec((1, NS, channels), lambda i, *_: (i, 0, 0))],
            scratch_shapes=[
                pltpu.VMEM((BLK + 8, channels), jnp.float32),
                pltpu.VMEM((BLK + 8, 2 * NS), jnp.float32),
                pltpu.VMEM((NS, channels), jnp.float32),
                pltpu.VMEM((8, LANES), jnp.bfloat16),
                wide,
                wide,
                pltpu.VMEM((row_pad, BLK), jnp.float32),
                pltpu.VMEM((row_pad, BLK), jnp.float32),
            ],
        ),
        compiler_params=pltpu.CompilerParams(vmem_limit_bytes=VMEM_LIMIT),
        cost_estimate=lasting(25),
        name="mixer",
        interpret=interpret,
    )(opens, widths, inner, small, tx, ts, table)


def mixer_back(opens, inner, small, tx, ts, table, ybar, entered, interpret=False):
    tokens, channels = inner.shape
    heads, count = channels // P_SIZE, tokens // BLK
    per = BLK // 8
    turn = lambda i: count - 1 - i
    whole = lambda rows, columns: pl.BlockSpec((rows, columns), lambda i, *_: (0, 0))
    rows = lambda columns: pl.BlockSpec((BLK, columns), lambda i, *_: (turn(i), 0))
    tail = lambda columns: pl.BlockSpec(
        (8, columns), lambda i, *_: (jnp.maximum(turn(i) * per - 1, 0), 0)
    )
    wide = pltpu.VMEM((heads, BLK, LANES), jnp.float32)
    row_pad = -(-heads // 8) * 8
    column = pltpu.VMEM((BLK, LANES), jnp.float32)
    return pl.pallas_call(
        functools.partial(mixer_back_kernel, heads, count),
        out_shape=(
            jax.ShapeDtypeStruct((tokens, channels), jnp.bfloat16),
            jax.ShapeDtypeStruct((tokens, 3 * LANES), jnp.bfloat16),
            jax.ShapeDtypeStruct((8, channels), jnp.float32),
            jax.ShapeDtypeStruct((8, 2 * NS), jnp.float32),
            jax.ShapeDtypeStruct((8, LANES), jnp.float32),
        ),
        grid_spec=pltpu.PrefetchScalarGridSpec(
            num_scalar_prefetch=1,
            grid=(count,),
            in_specs=[
                rows(channels),
                tail(channels),
                rows(3 * LANES),
                tail(3 * LANES),
                whole(8, channels),
                whole(8, 2 * NS),
                whole(8, LANES),
                rows(channels),
                pl.BlockSpec((1, NS, channels), lambda i, *_: (turn(i), 0, 0)),
            ],
            out_specs=[rows(channels), rows(3 * LANES), whole(8, channels), whole(8, 2 * NS), whole(8, LANES)],
            scratch_shapes=[
                pltpu.VMEM((BLK + 8, channels), jnp.float32),
                pltpu.VMEM((BLK + 8, 2 * NS), jnp.float32),
                pltpu.VMEM((BLK + 8, channels), jnp.float32),
                pltpu.VMEM((BLK + 8, 2 * NS), jnp.float32),
                pltpu.VMEM((NS, channels), jnp.float32),
                wide,
                wide,
                pltpu.VMEM((row_pad, BLK), jnp.float32),
                pltpu.VMEM((LANES, BLK), jnp.float32),
                pltpu.VMEM((BLK, BLK), jnp.float32),
                pltpu.VMEM((BLK, 2 * NS), jnp.float32),
                column,
                column,
                column,
                pltpu.VMEM((8, LANES), jnp.float32),
            ],
        ),
        compiler_params=pltpu.CompilerParams(vmem_limit_bytes=VMEM_LIMIT),
        cost_estimate=lasting(43),
        name="mixer_back",
        interpret=interpret,
    )(opens, inner, inner, small, small, tx, ts, table, ybar, entered)


def advance_inner_kernel(rate, count, weight, moment, average, *refs):
    parts, outs = refs[:-3], refs[-3:]

    def total(some):
        return sum(x[...].astype(jnp.float32) for x in some)

    for k, gradient in enumerate((total(parts[:count]), total(parts[count:]))):
        news = advance(weight[:, k, :], gradient, moment[:, k, :], average[:, k, :], rate)
        for out, new in zip(outs, news):
            out[:, k, :] = new


def advance_inner(weight, moment, average, gate, inner, rate):
    rows, two, columns = weight.shape
    count = len(gate)
    tile = min(rows, 64)
    pair = pl.BlockSpec((tile, two, columns), lambda i: (i, 0, 0))
    flat = lambda n: pl.BlockSpec((tile, n), lambda i: (i, 0))
    return pl.pallas_call(
        functools.partial(advance_inner_kernel, rate, count),
        out_shape=(jax.ShapeDtypeStruct(weight.shape, weight.dtype),) * 3,
        grid=(rows // tile,),
        in_specs=[pair] * 3 + [flat(columns)] * (count + len(inner)),
        out_specs=[pair] * 3,
        compiler_params=pltpu.CompilerParams(vmem_limit_bytes=VMEM_LIMIT),
        cost_estimate=lasting(8),
        name="advance_inner",
    )(weight, moment, average, *gate, *inner)


def swap_pairs(size):
    return [(i, i ^ 1) for i in range(size)]


def after(value, *earlier):
    return lax.optimization_barrier((value, *earlier))[0]


def place_kernel(count, slots, *refs):
    pieces, out = refs[:count], refs[count]
    step = pl.program_id(0)
    for i in range(count):

        @pl.when(step == i)
        def _(i=i):
            out[...] = pieces[i][...]


def place(pieces, slots, shape=None):
    count = len(pieces)
    pieces = [x if isinstance(x, tuple) else (x, 0) for x in pieces]
    shape = shape or pieces[0][0].shape
    return pl.pallas_call(
        functools.partial(place_kernel, count),
        out_shape=jax.ShapeDtypeStruct((shape[0] * count, *shape[1:]), pieces[0][0].dtype),
        grid_spec=pltpu.PrefetchScalarGridSpec(
            num_scalar_prefetch=1,
            grid=(count,),
            in_specs=[pl.BlockSpec(shape, lambda i, slots, at=at: (at, 0)) for _, at in pieces],
            out_specs=pl.BlockSpec(shape, lambda i, slots: (slots[i], 0)),
        ),
        compiler_params=pltpu.CompilerParams(vmem_limit_bytes=VMEM_LIMIT),
        cost_estimate=lasting(4),
        name="place",
    )(jnp.stack(slots).astype(jnp.int32), *[x for x, _ in pieces])


def my_column():
    return lax.axis_index("dp") % Y_SIZE


def split_own(value, axis):
    count = lax.axis_size("dp")
    shape = value.shape
    wide = value.reshape(
        *shape[:axis], count // Y_SIZE, Y_SIZE, shape[axis] // count, *shape[axis + 1 :]
    )
    halves = [
        lax.index_in_dim(wide, i, axis + 1, keepdims=False).reshape(
            *shape[:axis], shape[axis] // Y_SIZE, *shape[axis + 1 :]
        )
        for i in range(Y_SIZE)
    ]
    first = my_column() == 0
    return jnp.where(first, halves[0], halves[1]), jnp.where(first, halves[1], halves[0])


def join_own(own, other, axis, width):
    first = my_column() == 0
    shape = own.shape
    halves = [
        x.reshape(*shape[:axis], shape[axis] // width, 1, width, *shape[axis + 1 :])
        for x in (jnp.where(first, own, other), jnp.where(first, other, own))
    ]
    return jnp.concatenate(halves, axis=axis + 1).reshape(
        *shape[:axis], shape[axis] * Y_SIZE, *shape[axis + 1 :]
    )


def halves_kernel(piece, column, x, own, other):
    value = x[...]
    first = column[0] == 0
    for row in range(value.shape[1] // piece // Y_SIZE):
        at = row * Y_SIZE * piece
        low, high = value[:, at : at + piece], value[:, at + piece : at + 2 * piece]
        own[:, row * piece : (row + 1) * piece] = jnp.where(first, low, high)
        other[:, row * piece : (row + 1) * piece] = jnp.where(first, high, low)


def split_columns(value):
    tokens, width = value.shape
    piece = width // lax.axis_size("dp")
    if piece % LANES:
        return split_own(value, 1)
    half = jax.ShapeDtypeStruct((tokens, width // Y_SIZE), value.dtype)
    rows = lambda columns: pl.BlockSpec((BLK, columns), lambda i, *_: (i, 0))
    return pl.pallas_call(
        functools.partial(halves_kernel, piece),
        out_shape=(half, half),
        grid_spec=pltpu.PrefetchScalarGridSpec(
            num_scalar_prefetch=1,
            grid=(tokens // BLK,),
            in_specs=[rows(width)],
            out_specs=[rows(width // Y_SIZE)] * 2,
        ),
        cost_estimate=lasting(5),
        name="halves",
    )(my_column().astype(jnp.int32)[None], value)


def columns_kernel(slots, *refs):
    pieces, own, other = refs[:-2], refs[-2], refs[-1]
    first = slots[len(pieces)] == 0
    half = own.shape[1]
    for i, piece in enumerate(pieces):

        @pl.when(pl.program_id(0) == i)
        def _(piece=piece):
            low, high = piece[:, :half], piece[:, half:]
            own[...] = jnp.where(first, low, high)
            other[...] = jnp.where(first, high, low)


def gather_columns(piece):
    tokens, width = piece.shape
    count = lax.axis_size("head")
    if not aligned(width * count // Y_SIZE):
        return split_columns(lax.all_gather(piece, "head", axis=1, tiled=True))
    index = lax.axis_index("head")
    far = lax.ppermute(piece, "head", [(i, i ^ 2) for i in range(count)])
    near = lax.ppermute(piece, "head", swap_pairs(count))
    last = lax.ppermute(far, "head", swap_pairs(count))
    slots = jnp.stack([index, index ^ 1, index ^ 2, index ^ 3, my_column()]).astype(jnp.int32)
    half = jax.ShapeDtypeStruct((tokens, width * count // Y_SIZE), piece.dtype)
    return pl.pallas_call(
        columns_kernel,
        out_shape=(half, half),
        grid_spec=pltpu.PrefetchScalarGridSpec(
            num_scalar_prefetch=1,
            grid=(count,),
            in_specs=[pl.BlockSpec(piece.shape, lambda i, slots: (0, 0))] * count,
            out_specs=[pl.BlockSpec((tokens, width // Y_SIZE), lambda i, slots: (0, slots[i]))] * 2,
        ),
        compiler_params=pltpu.CompilerParams(vmem_limit_bytes=VMEM_LIMIT),
        cost_estimate=lasting(5),
        name="columns",
    )(slots, piece, near, far, last)


def rows_phase(shard):
    count = lax.axis_size("dp")
    held = [shard]
    for shift in range(1, count // Y_SIZE):
        perm = [(i, (i + shift * Y_SIZE) % count) for i in range(count)]
        held.append(lax.ppermute(shard, "dp", perm))
    return held


def begin_gather(shard):
    if lax.axis_size("dp") != 8:
        return [shard]
    return rows_phase(shard)


def end_gather(held, *later):
    if lax.axis_size("dp") != 8:
        return split_own(lax.all_gather(held[0], "dp", axis=0, tiled=True), 0)
    if later:
        held = list(lax.optimization_barrier((*held, *later))[: len(held)])
    row = lax.axis_index("dp") // Y_SIZE
    own = place(held, [(row - i) % len(held) for i in range(len(held))])
    return own, lax.ppermute(own, "dp", swap_pairs(8))


def begin_reduce(kept, away):
    count = lax.axis_size("dp")
    if count != 8:
        return kept, away
    return kept, lax.ppermute(away, "dp", swap_pairs(count))


def fold_pairs(begun, axis=0):
    kept, came = begun
    count = lax.axis_size("dp")
    if count != 8:
        width = kept.shape[axis] // (count // Y_SIZE)
        return None, join_own(kept.astype(came.dtype), came, axis, width)
    shape = kept.shape
    wide = (*shape[:axis], 2, 2, shape[axis] // 4, *shape[axis + 1 :])
    bit = (lax.axis_index("dp") // Y_SIZE) % 2

    def pick(which):
        first, second = (
            lax.dynamic_index_in_dim(x.reshape(wide), which, axis + 1, keepdims=False)
            for x in (kept, came)
        )
        return first + second.astype(jnp.float32)

    return pick(bit), pick(1 - bit).astype(came.dtype)


def swap_low(fold):
    kept, away = fold
    if kept is None:
        return fold
    return kept, lax.ppermute(away, "dp", [(i, i ^ Y_SIZE) for i in range(8)])


def fold_low(swapped, axis=0):
    kept, came = swapped
    if kept is None:
        return None, lax.psum_scatter(came, "dp", scatter_dimension=axis, tiled=True)
    bit = lax.axis_index("dp") // Y_SIZE // 2

    def pick(which):
        first, second = (
            lax.dynamic_index_in_dim(x, which, axis, keepdims=False) for x in (kept, came)
        )
        return first + second.astype(jnp.float32)

    return pick(bit), pick(1 - bit).astype(came.dtype)


def swap_high(fold):
    kept, away = fold
    if kept is None:
        return [away]
    return [kept, lax.ppermute(away, "dp", [(i, i ^ (2 * Y_SIZE)) for i in range(8)])]


def add_parts(parts):
    return sum(x.astype(jnp.float32) for x in parts)


def reduce_head(value):
    count = lax.axis_size("head")
    low = jnp.bfloat16
    if count != 4:
        return lax.psum_scatter(value, "head", scatter_dimension=0, tiled=False)
    index = lax.axis_index("head")
    side, core = index // 2, index % 2
    both = value.reshape(2, 2, *value.shape[1:])
    away = lax.dynamic_index_in_dim(both, 1 - core, 1, keepdims=False)
    kept = lax.dynamic_index_in_dim(both, core, 1, keepdims=False)
    came = lax.ppermute(away.astype(low), "head", swap_pairs(count))
    pair = kept + came.astype(jnp.float32)
    away = lax.dynamic_index_in_dim(pair, 1 - side, 0, keepdims=False)
    kept = lax.dynamic_index_in_dim(pair, side, 0, keepdims=False)
    came = lax.ppermute(away.astype(low), "head", [(i, (i + 2) % 4) for i in range(count)])
    return kept + came.astype(jnp.float32)


def gather_head(piece):
    count = lax.axis_size("head")
    if count != 4:
        return lax.all_gather(piece, "head", axis=0, tiled=True)
    index = lax.axis_index("head")
    far = lax.ppermute(piece, "head", [(i, (i + 2) % 4) for i in range(count)])
    near = lax.ppermute(piece, "head", swap_pairs(count))
    last = lax.ppermute(far, "head", swap_pairs(count))
    across = (index + 2) % 4
    return place([piece, near, far, last], [index, index ^ 1, across, across ^ 1])


LASTING = {
    "norm": 6,
    "project": 8,
    "gate": 10,
    "scale": 6,
    "weight": 8,
    "whole_weight": 11,
    "output_back": 11,
    "norm_back": 10,
    "output": 9,
    "input_back": 20,
}


def call(kernel, name, grid, scalars, args, in_specs, outs, out_specs):
    return pl.pallas_call(
        kernel,
        out_shape=outs,
        grid_spec=pltpu.PrefetchScalarGridSpec(
            num_scalar_prefetch=len(scalars), grid=grid, in_specs=in_specs, out_specs=out_specs
        ),
        compiler_params=pltpu.CompilerParams(vmem_limit_bytes=VMEM_LIMIT),
        cost_estimate=lasting(LASTING[name]),
        name=name,
    )(*scalars, *args)


def rows_of(columns):
    return pl.BlockSpec((STEP, columns), lambda i, *_: (i, 0))


def line_of():
    return pl.BlockSpec((1, STEP), lambda i, *_: (0, i))


def fixed(array):
    return pl.BlockSpec(array.shape, lambda i, *_: (0, 0))


def held_once(array):
    return pl.BlockSpec(array.shape, lambda i, *_: (0, 0), pipeline_mode=pl.Buffered(1))


def typed(kind, *shape):
    return jax.ShapeDtypeStruct(shape, kind)


def to_column(line, columns):
    column = jnp.transpose(jnp.broadcast_to(line, (LANES, line.shape[1])))
    return jnp.concatenate([column] * (columns // LANES), axis=1)


def to_line(value):
    part = value[:, :LANES]
    for at in range(LANES, value.shape[1], LANES):
        part = part + value[:, at : at + LANES]
    return jnp.sum(jnp.transpose(part), axis=0, keepdims=True)


def halves_of(value, piece, first):
    starts = range(0, value.shape[1], Y_SIZE * piece)
    low = jnp.concatenate([value[:, s : s + piece] for s in starts], axis=1)
    high = jnp.concatenate([value[:, s + piece : s + 2 * piece] for s in starts], axis=1)
    return jnp.where(first, low, high), jnp.where(first, high, low)


def norm_kernel(own_in, other_in, gains, own, other, inverse):
    xs = [x[...].astype(jnp.float32) for x in (own_in, other_in)]
    width = xs[0].shape[1]
    sums = to_line(xs[0] * xs[0] + xs[1] * xs[1])
    scale = lax.rsqrt(sums / (2 * width) + EPS)
    inverse[...] = scale
    column = to_column(scale, width)
    for i, (x, out) in enumerate(zip(xs, (own, other))):
        out[...] = (x * column * gains[i : i + 1, :]).astype(jnp.bfloat16)


def norm(xs, gains):
    tokens, width = xs[0].shape
    half = typed(jnp.bfloat16, tokens, width)
    own, other, inverse = call(
        norm_kernel,
        "norm",
        (tokens // STEP,),
        (),
        (*xs, gains),
        [rows_of(width)] * 2 + [fixed(gains)],
        (half, half, typed(jnp.float32, 1, tokens)),
        [rows_of(width)] * 2 + [line_of()],
    )
    return [own, other], inverse


def project_kernel(own, other, w_own, w_other, out):
    out[...] = dot32(own[...], w_own[...]) + dot32(other[...], w_other[...])


def project(halves, weights):
    tokens, width = halves[0].shape
    columns = weights[0].shape[1]
    return call(
        project_kernel,
        "project",
        (tokens // STEP,),
        (),
        (*halves, *weights),
        [rows_of(width)] * 2 + [held_once(w) for w in weights],
        typed(jnp.float32, tokens, columns),
        rows_of(columns),
    )


def gate_kernel(own, other, w_own, w_other, mixed, gate, squares):
    value = dot32(own[...], w_own[...]) + dot32(other[...], w_other[...])
    gate[...] = value
    gated = mixed[...] * (value * jax.nn.sigmoid(value))
    squares[...] = to_line(gated * gated)


def gate_project(halves, weights, mixed):
    tokens, width = halves[0].shape
    columns = mixed.shape[1]
    return call(
        gate_kernel,
        "gate",
        (tokens // STEP,),
        (),
        (*halves, *weights, mixed),
        [rows_of(width)] * 2 + [held_once(w) for w in weights] + [rows_of(columns)],
        (typed(jnp.float32, tokens, columns), typed(jnp.float32, 1, tokens)),
        [rows_of(columns), line_of()],
    )


def scale_kernel(mixed, gate, scale, gain, out):
    value = gate[...]
    gated = mixed[...] * (value * jax.nn.sigmoid(value))
    column = to_column(scale[...], value.shape[1])
    out[...] = (gated * column * gain[...]).astype(jnp.bfloat16)


def scale_gated(mixed, gate, scale, gain):
    tokens, columns = mixed.shape
    return call(
        scale_kernel,
        "scale",
        (tokens // STEP,),
        (),
        (mixed, gate, scale, gain),
        [rows_of(columns)] * 2 + [line_of(), fixed(gain)],
        typed(jnp.bfloat16, tokens, columns),
        rows_of(columns),
    )


def weight_kernel(own, other, back, kept, away):
    kept[...] = dot32(own[...], back[...], TN)
    away[...] = dot32(other[...], back[...], TN).astype(jnp.bfloat16)


def weight_grad(halves, back):
    tokens, width = halves[0].shape
    columns = back.shape[1]
    strip = pl.BlockSpec((tokens, BLK), lambda i, *_: (0, i))
    return call(
        weight_kernel,
        "weight",
        (width // BLK,),
        (),
        (*halves, back),
        [strip] * 2 + [held_once(back)],
        (typed(jnp.float32, width, columns), typed(jnp.bfloat16, width, columns)),
        [pl.BlockSpec((BLK, columns), lambda i, *_: (i, 0))] * 2,
    )


def whole_weight_kernel(column, own, other, back, out):
    mine = pl.program_id(1) == 0

    @pl.when(mine)
    def _():
        out[...] = dot32(own[...], back[...], TN).astype(jnp.bfloat16)

    @pl.when(jnp.logical_not(mine))
    def _():
        out[...] = dot32(other[...], back[...], TN).astype(jnp.bfloat16)


def whole_weight_grad(halves, back):
    tokens, width = halves[0].shape
    columns = back.shape[1]
    piece = Y_SIZE * width // lax.axis_size("dp")
    if piece % LANES:
        kept, away = weight_grad(halves, back)
        return join_own(kept.astype(away.dtype), away, 0, piece)
    strip = pl.BlockSpec((tokens, piece), lambda i, j, *_: (0, i))
    spot = lambda i, j, column: (Y_SIZE * i + (column[0] + j) % Y_SIZE, 0)
    return call(
        whole_weight_kernel,
        "whole_weight",
        (width // piece, Y_SIZE),
        (my_column().astype(jnp.int32)[None],),
        (*halves, back),
        [strip] * 2
        + [pl.BlockSpec(back.shape, lambda i, j, *_: (0, 0), pipeline_mode=pl.Buffered(1))],
        typed(jnp.bfloat16, Y_SIZE * width, columns),
        pl.BlockSpec((piece, columns), spot),
    )


def store_heads(kept, away, spot, own, other):
    first, even = spot[0] == 0, spot[1] == 0
    low = jnp.where(first, own, other).astype(kept.dtype)
    high = jnp.where(first, other, own).astype(kept.dtype)
    half = kept.shape[2] // Y_SIZE
    for side in range(kept.shape[0]):
        for at, value in ((0, low), (half, high)):
            start = 2 * side * half
            one, two = value[:, start : start + half], value[:, start + half : start + 2 * half]
            kept[side, :, at : at + half] = jnp.where(even, one, two)
            away[side, :, at : at + half] = jnp.where(even, two, one)


def my_spot():
    return jnp.stack([my_column(), lax.axis_index("head") % 2]).astype(jnp.int32)


def heads_out(tokens, width):
    count = lax.axis_size("head")
    columns = Y_SIZE * width // count
    shape = typed(jnp.bfloat16, count // 2, tokens, columns)
    return [shape] * 2, [pl.BlockSpec((count // 2, STEP, columns), lambda i, *_: (0, i, 0))] * 2


def aligned(width):
    count = lax.axis_size("dp")
    return count == Y_SIZE * lax.axis_size("head") and Y_SIZE * width // count % LANES == 0


def begin_heads(pair, width):
    if not aligned(width):
        return None, join_own(*pair, 1, Y_SIZE * width // lax.axis_size("dp"))
    kept, away = pair
    return kept, lax.ppermute(away, "head", swap_pairs(4))


def fold_heads(begun):
    kept, near = begun
    if kept is None:
        return [lax.psum_scatter(near, "head", scatter_dimension=1, tiled=True)]
    side = lax.axis_index("head") // 2
    parts = [
        lax.dynamic_index_in_dim(kept, which, 0, keepdims=False).astype(jnp.float32)
        + lax.dynamic_index_in_dim(near, which, 0, keepdims=False)
        for which in (side, 1 - side)
    ]
    away = parts[1].astype(near.dtype)
    return [away, parts[0], lax.ppermute(away, "head", [(i, i ^ 2) for i in range(4)])]


def end_heads(folded):
    return sum(x.astype(jnp.float32) for x in folded[-2:])


def output_back_kernel(own, other, w_own, w_other, mixed, gate, gain, grad, dots):
    value = dot32(own[...], w_own[...]) + dot32(other[...], w_other[...])
    grad[...] = value
    raw = gate[...]
    gated = mixed[...] * (raw * jax.nn.sigmoid(raw))
    dots[...] = to_line(value * gain[...] * gated)


def output_back(halves, weights, mixed, gate, gain):
    tokens, width = halves[0].shape
    columns = mixed.shape[1]
    return call(
        output_back_kernel,
        "output_back",
        (tokens // STEP,),
        (),
        (*halves, *weights, mixed, gate, gain),
        [rows_of(width)] * 2
        + [held_once(w) for w in weights]
        + [rows_of(columns)] * 2
        + [fixed(gain)],
        (typed(jnp.float32, tokens, columns), typed(jnp.float32, 1, tokens)),
        [rows_of(columns), line_of()],
    )


def norm_back_kernel(heads, widths, grad, mixed, gate, gain, scale, scale_back, ybar, gate_low, gain_grad):
    block = pl.program_id(0)
    columns = grad.shape[1]
    raw = gate[...]
    share = jax.nn.sigmoid(raw)
    silu = raw * share
    value, state = grad[...], mixed[...]
    gated = state * silu
    column = to_column(scale[...], columns)
    back = value * gain[...] * column - gated * to_column(scale_back[...], columns)
    lane = lax.broadcasted_iota(jnp.int32, (1, columns), 1)
    used = jnp.concatenate(
        [
            jnp.broadcast_to(
                ((lane // P_SIZE) * H < widths[block * (STEP // BLK) + at] * heads).astype(
                    jnp.float32
                ),
                (BLK, columns),
            )
            for at in range(STEP // BLK)
        ],
        axis=0,
    )
    ybar[...] = back * silu * used
    gate_low[...] = (back * state * (share * (1.0 + raw * (1.0 - share)))).astype(jnp.bfloat16)

    @pl.when(block == 0)
    def _():
        gain_grad[...] = jnp.zeros_like(gain_grad)

    gain_grad[...] += jnp.sum(value * gated * column, axis=0, keepdims=True)


def norm_back(widths, grad, mixed, gate, gain, scale, scale_back):
    tokens, columns = grad.shape
    return call(
        functools.partial(norm_back_kernel, columns // P_SIZE),
        "norm_back",
        (tokens // STEP,),
        (widths,),
        (grad, mixed, gate, gain, scale, scale_back),
        [rows_of(columns)] * 3 + [fixed(gain), line_of(), line_of()],
        (
            typed(jnp.float32, tokens, columns),
            typed(jnp.bfloat16, tokens, columns),
            typed(jnp.float32, 1, columns),
        ),
        [rows_of(columns)] * 2 + [pl.BlockSpec((1, columns), lambda i, *_: (0, 0))],
    )


def output_kernel(whole, spot, value, w_own, w_other, *outs):
    own, other = (dot32(value[...], w[...], NT) for w in (w_own, w_other))
    if whole:
        store_heads(*outs, spot, own, other)
    else:
        outs[0][...], outs[1][...] = own.astype(jnp.bfloat16), other.astype(jnp.bfloat16)


def output_project(value, weights):
    tokens, columns = value.shape
    width = weights[0].shape[0]
    outs, out_specs = [typed(jnp.bfloat16, tokens, width)] * 2, [rows_of(width)] * 2
    if aligned(width):
        outs, out_specs = heads_out(tokens, width)
    return call(
        functools.partial(output_kernel, aligned(width)),
        "output",
        (tokens // STEP,),
        (my_spot(),),
        (value, *weights),
        [rows_of(columns)] + [held_once(w) for w in weights],
        outs,
        out_specs,
    )


def input_back_kernel(whole, spot, gate, inner, small, xo, xt, gains, inverse, *refs):
    weights, outs, line, sums = refs[:6], refs[6:-2], refs[-2], refs[-1]
    block = pl.program_id(0)
    scale = to_column(inverse[...], xo.shape[1])

    @pl.when(block == 0)
    def _():
        sums[...] = jnp.zeros_like(sums)

    total, values = None, []
    for i, x in enumerate((xo, xt)):
        value = (
            dot32(gate[...], weights[i][...], NT)
            + dot32(inner[...], weights[2 + i][...], NT)
            + dot32(small[...], weights[4 + i][...], NT)
        )
        values.append(value)
        product = value * x[...].astype(jnp.float32)
        sums[i : i + 1, :] += jnp.sum(product * scale, axis=0, keepdims=True)
        row = product * gains[i : i + 1, :]
        total = row if total is None else total + row
    line[...] = to_line(total)
    if whole:
        store_heads(*outs, spot, *values)
    else:
        outs[0][...], outs[1][...] = (v.astype(jnp.bfloat16) for v in values)


def input_back(backs, xs, gains, inverse, weights):
    tokens, width = xs[0].shape
    outs, out_specs = [typed(jnp.bfloat16, tokens, width)] * 2, [rows_of(width)] * 2
    if aligned(width):
        outs, out_specs = heads_out(tokens, width)
    *grads, line, sums = call(
        functools.partial(input_back_kernel, aligned(width)),
        "input_back",
        (tokens // STEP,),
        (my_spot(),),
        (*backs, *xs, gains, inverse, *weights),
        [rows_of(b.shape[1]) for b in backs]
        + [rows_of(width)] * 2
        + [fixed(gains), line_of()]
        + [held_once(w) for w in weights],
        (*outs, typed(jnp.float32, 1, tokens), typed(jnp.float32, 2, width)),
        [*out_specs, line_of(), pl.BlockSpec((2, width), lambda i, *_: (0, 0))],
    )
    return tuple(grads), line, sums


def body(
    inputs,
    cotangent,
    token_valid,
    block_opens,
    block_widths,
    weight_inner,
    weight_step,
    weight_output,
    weight_state,
    norm_gain,
    channel_table,
    head_table,
    state_filter,
    momentum_inner,
    momentum_step,
    momentum_output,
    momentum_state,
    momentum_gain,
    momentum_channel,
    momentum_head,
    momentum_filter,
    average_inner,
    average_step,
    average_output,
    average_state,
    average_gain,
    average_channel,
    average_head,
    average_filter,
):
    low = jnp.bfloat16
    full_type = jnp.float32
    count_dp = lax.axis_size("dp")
    count_head = lax.axis_size("head")
    rows_dp, piece = count_dp // Y_SIZE, weight_inner.shape[0]
    tokens, channels = inputs.shape[0], weight_inner.shape[2]
    heads_own = weight_step.shape[1]
    rows_all, state_rows = weight_state.shape[0], state_filter.shape[0]
    width_state = weight_state.shape[1]
    filter_block = jnp.pad(state_filter.astype(low), ((0, rows_all - state_rows), (0, 0)))
    small_piece = jnp.concatenate(
        [
            weight_state.astype(low),
            weight_step.astype(low).reshape(rows_all, -1),
            norm_gain.astype(low)[:, None],
            filter_block,
        ],
        axis=1,
    )
    small_piece = jnp.pad(small_piece, ((0, 0), (0, -small_piece.shape[1] % LANES)))
    small_all = lax.all_gather(
        small_piece, ("dp", "head"), axis=0, tiled=False
    ).reshape(count_dp, count_head, rows_all, -1)
    step_size = rows_all * count_head * heads_own // rows_all
    step_full = lax.dynamic_index_in_dim(small_all, lax.axis_index("head"), 1, keepdims=False)
    step_full = step_full[:, :, width_state : width_state + step_size].reshape(D, heads_own)
    extra = small_all[:, :, :, width_state + step_size :].reshape(D, -1)[:, : 2 + KC]
    state_full = small_all[:, :, :, :width_state].reshape(D, width_state)
    filter_full = extra[:, 1:].reshape(-1, rows_all, KC + 1)[:, :state_rows].reshape(-1, KC + 1)
    gains = jnp.stack(split_own(extra[:, 0].astype(full_type), 0))
    step_wide = jnp.pad(step_full, ((0, 0), (0, LANES - heads_own)))
    small_w = split_own(jnp.concatenate([state_full, step_wide], axis=1), 0)
    shards = [
        weight_inner[:, 1].astype(low),
        weight_inner[:, 0].astype(low),
        weight_output.astype(low).T,
    ]
    inner_held = begin_gather(shards[0])
    inner_w = end_gather(inner_held)
    gate_held = begin_gather(after(shards[1], inner_w[0]))
    channel_used = rounded(channel_table)
    head_values = rounded(head_table)
    masked = cotangent * token_valid.astype(low)[:, None]
    masked = after(masked, small_all)
    cots = split_columns(lax.all_gather(masked, "head", axis=1, tiled=True))
    xs = gather_columns(inputs)
    normed, inverse_line = norm(xs, gains)
    small_x = project(normed, small_w)
    gate_w = end_gather(gate_held, small_x)
    output_held = begin_gather(after(shards[2], small_x, *gate_held[1:]))
    inner_x = project(normed, inner_w)
    widths = jnp.repeat(block_widths, BLK)
    norm_counts = (widths.astype(full_type) * P_SIZE)[None, :]
    valid_rows = token_valid.astype(full_type)
    gate_gain = channel_used[KC + 1]
    skip_wide = jnp.repeat(head_values[2], P_SIZE)
    taps_x = jnp.concatenate(
        [channel_used, skip_wide[None, :], jnp.zeros((1, channels), full_type)], axis=0
    )
    taps_s = jnp.pad(filter_full.astype(full_type).T, ((0, 8 - KC - 1), (0, 0)))
    table = jnp.pad(head_values, ((0, 5), (0, LANES - heads_own)))
    inner_x = after(inner_x, gate_w[0])
    mixed, entered = mixer(block_opens, block_widths, inner_x, small_x, taps_x, taps_s, table)
    output_w = end_gather(output_held, mixed)
    gate_w = lax.optimization_barrier((*gate_w, mixed, output_w[0]))[:2]
    gate_values, squares = gate_project(normed, gate_w, mixed)
    gain_line = gate_gain[None, :]
    norm_scale = lax.rsqrt(lax.psum(squares, "head") / norm_counts + EPS)
    projected = scale_gated(mixed, gate_values, norm_scale, gain_line)
    output_grad = whole_weight_grad(cots, projected)
    output_reduced = lax.psum_scatter(output_grad, "dp", scatter_dimension=0, tiled=True)
    output_w = lax.optimization_barrier((*output_w, output_grad))[:2]
    grad_normal, dot_line = output_back(cots, output_w, mixed, gate_values, gain_line)
    total_dot = lax.psum(dot_line, "head")
    scale_back = norm_scale * norm_scale * norm_scale / norm_counts * total_dot
    ybar, gate_low, grad_gate_gain = norm_back(
        block_widths, grad_normal, mixed, gate_values, gain_line, norm_scale, scale_back
    )
    gate_kept, gate_away = weight_grad(normed, gate_low)
    gate_begun = begin_reduce(gate_kept, gate_away)
    ybar = after(ybar, gate_away, gate_kept)
    inner_low, small_low, taps_grad, state_taps, table_grad = mixer_back(
        block_opens, inner_x, small_x, taps_x, taps_s, table, ybar, entered
    )
    inner_kept, inner_away = weight_grad(normed, inner_low)
    inner_begun = begin_reduce(inner_kept, inner_away)
    partial_out = output_project(after(projected, inner_away), output_w)
    out_begun = begin_heads(partial_out, output_w[0].shape[0])
    gate_fold = fold_pairs(
        (gate_begun[0], after(gate_begun[1], *jax.tree.leaves(partial_out)))
    )
    gate_low_swap = swap_low(gate_fold)
    out_folded = fold_heads((out_begun[0], after(out_begun[1], gate_fold[1])))
    inner_low, output_reduced = lax.optimization_barrier(
        (inner_low, output_reduced, out_folded[0])
    )[:2]
    backs = [gate_low, inner_low, small_low]
    grad_normed, row_line, gain_sums = input_back(
        backs, xs, gains, inverse_line, (*gate_w, *inner_w, *small_w)
    )
    grad_begun = begin_heads(grad_normed, inner_w[0].shape[0])
    grad_small = weight_grad(normed, after(small_low, row_line))
    fold = fold_pairs((inner_begun[0], after(inner_begun[1], grad_small[1])))
    inner_swap = swap_low(fold)
    gate_high = fold_low((gate_low_swap[0], after(gate_low_swap[1], fold[1])))
    gate_sent = swap_high(gate_high)
    grad_folded = fold_heads((grad_begun[0], after(grad_begun[1], gate_high[1])))
    inner_sent = swap_high(fold_low(inner_swap))
    grad_small, gain_sums = lax.optimization_barrier((grad_small, gain_sums, grad_folded[0]))[:2]
    branch = end_heads(out_folded)
    own_grad = end_heads(grad_folded)
    own_inputs = inputs.astype(full_type)
    layer_output = (own_inputs + valid_rows[:, None] * branch).astype(low)
    grad_gain = [gain_sums[0], gain_sums[1]]
    inverse = inverse_line[0]
    row_total = lax.psum(row_line, "head")[0]
    own_width = inputs.shape[1]
    own_gain = lax.dynamic_slice_in_dim(
        join_own(gains[0], gains[1], 0, piece), lax.axis_index("head") * own_width, own_width
    )
    scaled = own_grad * own_gain[None, :]
    inverse_cube = inverse * inverse * inverse
    grad_input = (
        cotangent.astype(full_type)
        + inverse[:, None] * scaled
        - own_inputs * (inverse_cube * row_total / D)[:, None]
    )
    grad_channel = jnp.concatenate([taps_grad[: KC + 1], grad_gate_gain], axis=0)
    grad_skip = jnp.sum(taps_grad[KC + 2].reshape(heads_own, P_SIZE), axis=1)
    grad_head = jnp.concatenate([table_grad[:2, :heads_own], grad_skip[None, :]], axis=0)
    grad_filter = state_taps[: KC + 1].T
    filter_size = state_rows * (KC + 1)
    filter_part = jnp.pad(
        grad_filter.reshape(count_dp, count_head, filter_size),
        ((0, 0), (0, 0), (0, rows_all - filter_size)),
    ).reshape(D)
    shared_part = jnp.stack(
        [
            jnp.concatenate([s[:, :width_state].astype(full_type), g[:, None], f[:, None]], axis=1)
            for s, g, f in zip(grad_small, grad_gain, split_own(filter_part, 0))
        ]
    ).reshape(Y_SIZE, rows_dp, count_head, rows_all, width_state + 2)
    shared_own = reduce_head(jnp.moveaxis(shared_part, 2, 0))
    step_part = jnp.stack(
        [s[:, width_state : width_state + heads_own].astype(full_type) for s in grad_small]
    )
    step_part = step_part.reshape(Y_SIZE, rows_dp, rows_all, -1)
    table_part = jnp.concatenate([grad_channel.reshape(-1), grad_head.reshape(-1)])
    table_width = -(-table_part.shape[0] // rows_all)
    table_part = jnp.pad(table_part, (0, table_width * rows_all - table_part.shape[0]))
    table_part = jnp.broadcast_to(
        table_part.reshape(rows_all, table_width), (Y_SIZE, rows_dp, rows_all, table_width)
    )
    small_part = jnp.concatenate([shared_own, step_part, table_part], axis=3)
    small_part = small_part.reshape(Y_SIZE, rows_dp * rows_all, -1)
    small_begun = begin_reduce(small_part[0], small_part[1].astype(low))
    output_reduced = output_reduced.astype(full_type).T
    small_own = add_parts(swap_high(fold_low(swap_low(fold_pairs(small_begun)))))
    state_reduced = small_own[:, :width_state]
    gain_reduced = small_own[:, width_state]
    filter_reduced = small_own[:filter_size, width_state + 1].reshape(state_rows, KC + 1)
    at = width_state + 2
    step_reduced = small_own[:, at : at + step_part.shape[3]].reshape(-1, heads_own)
    table_own = small_own[:, at + step_part.shape[3] :].reshape(-1)
    channel_size = grad_channel.size
    channel_reduced = table_own[:channel_size].reshape(grad_channel.shape)
    head_reduced = table_own[channel_size : channel_size + grad_head.size].reshape(grad_head.shape)
    total_tokens = inputs.shape[0] * lax.axis_size("dp")
    matrix_rate = RATE_MATRIX / math.sqrt(total_tokens)
    vector_rate = RATE_VECTOR / math.sqrt(total_tokens)
    new_output = advance(
        weight_output, output_reduced, momentum_output, average_output, matrix_rate
    )
    new_inner = advance_inner(
        weight_inner, momentum_inner, average_inner, gate_sent, inner_sent, matrix_rate
    )
    new_step = advance(weight_step, step_reduced, momentum_step, average_step, matrix_rate)
    new_state = advance(weight_state, state_reduced, momentum_state, average_state, matrix_rate)
    new_gain = advance(norm_gain, gain_reduced, momentum_gain, average_gain, vector_rate)
    new_channel = advance(
        channel_table, channel_reduced, momentum_channel, average_channel, vector_rate
    )
    new_head = advance(head_table, head_reduced, momentum_head, average_head, vector_rate)
    new_filter = advance(state_filter, filter_reduced, momentum_filter, average_filter, vector_rate)
    return (
        layer_output,
        grad_input,
        new_inner[0],
        new_inner[1],
        new_inner[2],
        new_step[0],
        new_step[1],
        new_step[2],
        new_output[0],
        new_output[1],
        new_output[2],
        new_state[0],
        new_state[1],
        new_state[2],
        new_gain[0],
        new_gain[1],
        new_gain[2],
        new_channel[0],
        new_channel[1],
        new_channel[2],
        new_head[0],
        new_head[1],
        new_head[2],
        new_filter[0],
        new_filter[1],
        new_filter[2],
    )


def solution(mesh):
    in_specs = (
        P("dp", "head"),
        P("dp", "head"),
        P("dp"),
        P("dp"),
        P("dp"),
        P("dp", None, "head"),
        P("dp", "head"),
        P("head", "dp"),
        P(("dp", "head"), None),
        P(("dp", "head")),
        P(None, "head"),
        P(None, "head"),
        P(("dp", "head"), None),
        P("dp", None, "head"),
        P("dp", "head"),
        P("head", "dp"),
        P(("dp", "head"), None),
        P(("dp", "head")),
        P(None, "head"),
        P(None, "head"),
        P(("dp", "head"), None),
        P("dp", None, "head"),
        P("dp", "head"),
        P("head", "dp"),
        P(("dp", "head"), None),
        P(("dp", "head")),
        P(None, "head"),
        P(None, "head"),
        P(("dp", "head"), None),
    )
    out_specs = (
        P("dp", "head"),
        P("dp", "head"),
        P("dp", None, "head"),
        P("dp", None, "head"),
        P("dp", None, "head"),
        P("dp", "head"),
        P("dp", "head"),
        P("dp", "head"),
        P("head", "dp"),
        P("head", "dp"),
        P("head", "dp"),
        P(("dp", "head"), None),
        P(("dp", "head"), None),
        P(("dp", "head"), None),
        P(("dp", "head")),
        P(("dp", "head")),
        P(("dp", "head")),
        P(None, "head"),
        P(None, "head"),
        P(None, "head"),
        P(None, "head"),
        P(None, "head"),
        P(None, "head"),
        P(("dp", "head"), None),
        P(("dp", "head"), None),
        P(("dp", "head"), None),
    )
    return jax.shard_map(body, mesh=mesh, in_specs=in_specs, out_specs=out_specs, check_vma=False)
```
